32 devices in a mesh: batch: 8 (over z, y), seq: 4 (over x, core).
Axes of the slice: x: 2, y: 2, z: 4, core: 2. Of those that a mesh axis runs over, the one named last changes fastest.
Arguments:
- tokens: bfloat16 [24, 1024, 1024], P('batch', 'seq'), may hold values from -6 to 6
- lengths: int32 [16], replicated, may hold values from 150 to 1024, as said below
- assignment: int32 [24], P('batch'), may hold values from -1 to 15, as said below
- query_weight: bfloat16 [1024, 1024], P(None, 'seq'), may hold values from -0.1875 to 0.1875
- key_weight: bfloat16 [1024, 1024], P(None, 'seq'), may hold values from -0.1875 to 0.1875
- value_weight: bfloat16 [1024, 1024], P(None, 'seq'), may hold values from -0.1875 to 0.1875
- gate_weight: bfloat16 [1024, 1024], P(None, 'seq'), may hold values from -0.1875 to 0.1875
- out_weight: bfloat16 [1024, 1024], P('seq'), may hold values from -0.375 to 0.375
- up_weight: bfloat16 [1024, 2816], P(None, 'seq'), may hold values from -0.1875 to 0.1875
- pair_weight: bfloat16 [1024, 2816], P(None, 'seq'), may hold values from -0.1875 to 0.1875
- down_weight: bfloat16 [2816, 1024], P('seq'), may hold values from -0.109375 to 0.109375
- attention_norm_gain: float32 [1024], replicated, may hold values from 0.5 to 1.5
- mlp_gain: float32 [1024], replicated, may hold values from 0.5 to 1.5
- head_gain: float32 [1024], P('seq'), may hold values from 0.5 to 1.5
- cotangent: bfloat16 [24, 1024, 1024], P('batch', 'seq'), may hold values from -6 to 6
Outputs:
- result: bfloat16 [24, 1024, 1024], P('batch', 'seq')
- grad_tokens: float32 [24, 1024, 1024], P('batch', 'seq')
- grad_query_weight: float32 [1024, 1024], P(None, 'seq')
- grad_key_weight: float32 [1024, 1024], P(None, 'seq')
- grad_value_weight: float32 [1024, 1024], P(None, 'seq')
- grad_gate_weight: float32 [1024, 1024], P(None, 'seq')
- grad_out_weight: float32 [1024, 1024], P('seq')
- grad_up_weight: float32 [1024, 2816], P(None, 'seq')
- grad_pair_weight: float32 [1024, 2816], P(None, 'seq')
- grad_down_weight: float32 [2816, 1024], P('seq')
- grad_attention_gain: float32 [1024], replicated
- grad_mlp_gain: float32 [1024], replicated
- grad_head_gain: float32 [1024], P('seq')
The draws below stay inside these ranges and needn't reach their ends.
Inputs may be any that keep to these rules, and one draw needn't show every extreme that they name: `lengths`: the true tokens of each sequence; positions from the length on are padding and give no keys. `assignment`: each sequence stands in exactly one slot; the slots come in groups of 3 consecutive slots; each group holds 1 to 3 sequences in its first slots, the rest are -1.
All inputs are finite; a program needn't handle non-finite values.
Results may differ from the reference program's by a relative error of at most 0.025.
Values may be sent and summed in bfloat16 or wider, within the bound.
A program may use at most 256 MiB of HBM per device.

```python
import jax
import jax.numpy as jnp
from jax import lax

D = 1024
HEADS = 16
HD = 64
FF = 2816
SLOTS = 3
L = 1024
LEAST = 150
SEQS = 24
REAL = 16


def draw_lengths(key, part):
    base = jax.random.randint(jax.random.fold_in(key, 3), (REAL,), LEAST, L + 1)
    longest = jax.random.randint(jax.random.fold_in(key, 4), (), 0, REAL)
    return jnp.where(jnp.arange(REAL) == longest, L, base).astype(jnp.int32)


def draw_assignment(key, part):
    groups = REAL // 2
    pairs = groups // 2
    extra = jax.random.randint(jax.random.fold_in(key, 1), (pairs,), 0, 3)
    extra = extra.at[0].set(2)
    counts = jnp.stack([1 + extra, 3 - extra], axis=1).reshape(groups)
    offsets = jnp.cumsum(counts) - counts
    order = jax.random.permutation(jax.random.fold_in(key, 2), REAL)
    slot = jnp.arange(SLOTS)
    index = jnp.clip(offsets[:, None] + slot[None, :], 0, REAL - 1)
    filled = slot[None, :] < counts[:, None]
    picked = order[index]
    return jnp.where(filled, picked, -1).reshape(groups * SLOTS).astype(jnp.int32)


def block_levels(key, extent, cuts, least, high):
    def one(dim, blocks):
        steps = jax.random.uniform(jax.random.fold_in(jax.random.fold_in(key, 6), dim), (blocks,), jnp.float32, least / len(cuts), high / len(cuts))
        return jnp.repeat(jnp.exp(steps), extent[dim] // blocks).reshape((-1,) + (1,) * (len(extent) - dim - 1))

    level = one(*cuts[0])
    for cut in cuts[1:]:
        level = level * one(*cut)
    return level


def bell_draw(rng, dims, deviation, limit, pieces=(), kind=jnp.bfloat16):
    level = block_levels(rng, dims, pieces, -0.22, 0.18) if pieces else 1.0
    result = jax.random.normal(rng, dims, jnp.float32) * deviation * level
    return jnp.minimum(jnp.maximum(result, -limit), limit).astype(kind)


def setup_inputs(seed: int = 0) -> dict:
    key_list = jax.random.split(jax.random.key(seed), 16)
    tokens = bell_draw(key_list[0], (SEQS, L, D), 1.0, 6.0, ((0, 8), (1, 4)))
    lengths = draw_lengths(jax.random.fold_in(key_list[15], 71), 0)
    assignment = draw_assignment(jax.random.fold_in(key_list[15], 71), 0)
    query_weight = bell_draw(key_list[3], (D, D), D ** -0.5, 0.1875, ((1, 4),))
    key_weight = bell_draw(key_list[4], (D, D), D ** -0.5, 0.1875, ((1, 4),))
    value_weight = bell_draw(key_list[5], (D, D), D ** -0.5, 0.1875, ((1, 4),))
    gate_weight = bell_draw(key_list[6], (D, D), D ** -0.5, 0.1875, ((1, 4),))
    out_weight = bell_draw(key_list[7], (D, D), (D // 4) ** -0.5, 0.375, ((0, 4),))
    up_weight = bell_draw(key_list[8], (D, FF), D ** -0.5, 0.1875, ((1, 4),))
    pair_weight = bell_draw(key_list[9], (D, FF), D ** -0.5, 0.1875, ((1, 4),))
    down_weight = bell_draw(key_list[10], (FF, D), FF ** -0.5, 0.109375, ((0, 4),))
    attention_norm_gain = jnp.clip(1.0 + 0.1 * jax.random.normal(key_list[11], (D,), jnp.float32), 0.5, 1.5)
    mlp_gain = jnp.clip(1.0 + 0.1 * jax.random.normal(key_list[12], (D,), jnp.float32), 0.5, 1.5)
    head_gain = jnp.clip(1.0 + 0.1 * jax.random.normal(key_list[13], (D,), jnp.float32), 0.5, 1.5)
    cotangent = bell_draw(key_list[14], (SEQS, L, D), 1.0, 6.0, ((0, 8), (1, 4)))
    return dict(tokens=tokens, lengths=lengths, assignment=assignment, query_weight=query_weight, key_weight=key_weight, value_weight=value_weight, gate_weight=gate_weight, out_weight=out_weight, up_weight=up_weight, pair_weight=pair_weight, down_weight=down_weight, attention_norm_gain=attention_norm_gain, mlp_gain=mlp_gain, head_gain=head_gain, cotangent=cotangent)


EPS = 1e-05
HIGH_ACCURACY = lax.Precision.HIGHEST

@jax.custom_vjp
def low(v):
    return lax.optimization_barrier(v.astype(jnp.bfloat16)).astype(jnp.float32)

@jax.custom_vjp
def low_back(v):
    return v

def low_keep(v):
    return (low(v), None)

def low_pass(kept, grad):
    return (grad,)

def back_keep(v):
    return (v, None)

def back_low(kept, grad):
    return (low(grad),)
low.defvjp(low_keep, low_pass)
low_back.defvjp(back_keep, back_low)

def simple_norm(values, gain):
    scale = lax.rsqrt(lax.optimization_barrier(jnp.mean(values * values, axis=-1, keepdims=True)) + EPS)
    return values * scale * gain

def project(left_operand, right_operand):
    return jnp.einsum('mqw,wi->mqi', left_operand, right_operand, precision=HIGH_ACCURACY)

def forward(inputs, valid, query_weight, key_weight, value_weight, gate_weight, out_weight, up_weight, pair_weight, down_weight, attention_norm_gain, mlp_gain, head_gain):
    normed = low(simple_norm(inputs, attention_norm_gain))
    query = low_back(low(jax.nn.softplus(project(normed, query_weight))))
    keys = low_back(low(jax.nn.softplus(project(normed, key_weight)) * valid[..., None]))
    values = low_back(low(project(normed, value_weight)))
    gate_pre = low_back(project(normed, gate_weight))

    def attend(parts):
        one_query, one_keys, one_values = parts
        length = one_query.shape[0]
        query_heads = one_query.reshape(length, HEADS, HD).transpose(1, 0, 2)
        key_heads = one_keys.reshape(length, HEADS, HD).transpose(1, 0, 2)
        value_heads = one_values.reshape(length, HEADS, HD).transpose(1, 0, 2)
        causal = jnp.arange(length)[:, None] >= jnp.arange(length)[None, :]
        scores = jnp.einsum('hid,hjd->hij', query_heads, key_heads, precision=HIGH_ACCURACY)
        scores = low_back(low(jnp.where(causal[None], scores, 0.0)))
        mixed = low_back(jnp.einsum('hij,hjd->hid', scores, value_heads, precision=HIGH_ACCURACY))
        normed_heads = simple_norm(mixed, head_gain.reshape(HEADS, 1, HD))
        return normed_heads.transpose(1, 0, 2).reshape(length, D)
    attention_result = lax.map(jax.checkpoint(attend), (query, keys, values))
    gated = low_back(low(attention_result * jax.nn.silu(gate_pre)))
    middle = inputs + low_back(project(gated, out_weight))
    normed_two = low(simple_norm(middle, mlp_gain))
    up_part = low_back(project(normed_two, up_weight))
    pair_part = low_back(project(normed_two, pair_weight))
    product = low_back(low(up_part * pair_part))
    return middle + project(product, down_weight)

def reference(tokens, lengths, assignment, query_weight, key_weight, value_weight, gate_weight, out_weight, up_weight, pair_weight, down_weight, attention_norm_gain, mlp_gain, head_gain, cotangent):
    ids = jnp.arange(REAL, dtype=jnp.int32)
    slot_length = lax.optimization_barrier(jnp.sum(jnp.where(assignment[:, None] == ids[None, :], lengths[None, :], 0), axis=1)).astype(jnp.int32)
    positions = jnp.arange(L, dtype=jnp.int32)
    valid = (positions[None, :] < slot_length[:, None]).astype(jnp.float32)

    def wrapped(inputs, wq, wk, wv, wg, wo, wu, wp, wd, ga, gm, gh):
        return forward(inputs, valid, wq, wk, wv, wg, wo, wu, wp, wd, ga, gm, gh)
    primals = (tokens.astype(jnp.float32), query_weight.astype(jnp.float32), key_weight.astype(jnp.float32), value_weight.astype(jnp.float32), gate_weight.astype(jnp.float32), out_weight.astype(jnp.float32), up_weight.astype(jnp.float32), pair_weight.astype(jnp.float32), down_weight.astype(jnp.float32), attention_norm_gain.astype(jnp.float32), mlp_gain.astype(jnp.float32), head_gain.astype(jnp.float32))
    output, pullback = jax.vjp(wrapped, *primals)
    grads = pullback(cotangent.astype(jnp.float32))
    return (output.astype(jnp.bfloat16), grads[0], grads[1], grads[2], grads[3], grads[4], grads[5], grads[6], grads[7], grads[8], grads[9], grads[10], grads[11])
```

```python
import functools

import jax
import jax.numpy as jnp
from jax import lax
from jax.experimental import pallas as pl
from jax.experimental.pallas import tpu as pltpu
from jax.sharding import PartitionSpec as P

HD = 64
EPS = 1e-05
BF = jnp.bfloat16
F32 = jnp.float32
VMEM_LIMIT = 62 * 1024 * 1024
MESH = pl.DeviceIdType.MESH
BLOCKS = 4


def nn(a, b):
    return lax.dot_general(a, b, (((1,), (0,)), ((), ())), preferred_element_type=F32)


def nt(a, b):
    return lax.dot_general(a, b, (((1,), (1,)), ((), ())), preferred_element_type=F32)


def tn(a, b):
    return lax.dot_general(a, b, (((0,), (0,)), ((), ())), preferred_element_type=F32)


def same_head(width):
    rows = lax.broadcasted_iota(jnp.int32, (width, width), 0) // HD
    cols = lax.broadcasted_iota(jnp.int32, (width, width), 1) // HD
    return rows == cols


def by_head(array):
    rows, width = array.shape
    lane = lax.broadcasted_iota(jnp.int32, (rows, width), 1) // HD
    zero = jnp.zeros_like(array)
    return jnp.concatenate([jnp.where(lane == h, array, zero) for h in range(width // HD)], axis=0)


def causal(rows, heads, transposed):
    one = lax.broadcasted_iota(jnp.int32, (rows, rows), 0)
    two = lax.broadcasted_iota(jnp.int32, (rows, rows), 1)
    keep = (two >= one) if transposed else (one >= two)
    return jnp.concatenate([keep] * heads, axis=1)


def masked(scores, keep):
    return jnp.where(keep, scores, 0.0).astype(BF)


def head_mean(array, ones):
    return nn(array.astype(BF), ones) * (1.0 / HD)


def softplus(v):
    return jnp.maximum(v, 0.0) + jnp.log1p(jnp.exp(-jnp.abs(v)))


def sigmoid_of_softplus(q):
    series = q * (1.0 - q * (0.5 - q * (1.0 / 6.0)))
    return jnp.where(q < 0.03, series, 1.0 - jnp.exp(-q))


def sigmoid(v):
    return 1.0 / (1.0 + jnp.exp(-v))


class Peers:
    def __init__(self, batch=1):
        self.place = lax.axis_index("seq")
        self.group = lax.axis_index("batch")
        self.chip, self.core = self.place // 2, self.place % 2
        self.across = (self.group, (1 - self.chip) * 2 + self.core)
        self.beside = (self.group, self.chip * 2 + 1 - self.core)
        self.hops = batch.bit_length() - 1

    def bit(self, h):
        return (self.group // 2**h) % 2

    def partner(self, h):
        return (self.group + (1 - 2 * self.bit(h)) * 2**h, self.place)

    def meet(self):
        others = [self.across, self.beside] + [self.partner(h) for h in range(self.hops)]
        barrier = pltpu.get_barrier_semaphore()
        for peer in others:
            pl.semaphore_signal(barrier, inc=1, device_id=peer, device_id_type=MESH)
        pl.semaphore_wait(barrier, len(others))

    def relative(self, index):
        return ((index // 2 + self.chip) % 2) * 2 + (index % 2 + self.core) % 2


def spot(j):
    return (j % 2) * 2 + j // 2


def remote(source, target, sems, index, peer):
    send, recv = sems
    return pltpu.make_async_remote_copy(
        src_ref=source,
        dst_ref=target,
        send_sem=send.at[index],
        recv_sem=recv.at[index],
        device_id=peer,
        device_id_type=MESH,
    )


class Gather:
    def __init__(self, peers, buffer, sems, own=None):
        self.peers, self.buffer, self.sems = peers, buffer, sems
        self.own = own or (lambda k: buffer.at[k, 0])

    def chip_hop(self, k):
        return remote(self.own(k), self.buffer.at[k, 2], self.sems, 3 * k, self.peers.across)

    def core_hop(self, k):
        return remote(self.own(k), self.buffer.at[k, 1], self.sems, 3 * k + 1, self.peers.beside)

    def passed_on(self, k):
        return remote(
            self.buffer.at[k, 2], self.buffer.at[k, 3], self.sems, 3 * k + 2, self.peers.beside
        )

    def start(self, k):
        self.chip_hop(k).start()
        self.core_hop(k).start()

    def forward(self, k):
        self.chip_hop(k).wait_recv()
        self.passed_on(k).start()

    def arrived(self, k):
        self.core_hop(k).wait_recv()
        self.passed_on(k).wait_recv()

    def sent(self, k):
        self.chip_hop(k).wait_send()
        self.core_hop(k).wait_send()
        self.passed_on(k).wait_send()


class Scatter:
    def __init__(self, peers, pair, middle, came, far, sems):
        self.peers, self.pair, self.middle = peers, pair, middle
        self.came, self.far, self.sems = came, far, sems

    def core_hop(self, k):
        return remote(self.pair(k), self.came.at[k], self.sems, 2 * k, self.peers.beside)

    def chip_hop(self, k):
        return remote(self.middle(k), self.far.at[k], self.sems, 2 * k + 1, self.peers.across)

    def start(self, k):
        self.core_hop(k).start()

    def middle_step(self, k):
        self.core_hop(k).wait_recv()
        middle = self.middle(k)

        def add(rows):
            middle[rows] = (middle[rows].astype(F32) + self.came[k, 1, rows].astype(F32)).astype(BF)

        by_rows(middle.shape[0], add)
        self.chip_hop(k).start()

    def arrived(self, k):
        self.chip_hop(k).wait_recv()

    def sent(self, k):
        self.core_hop(k).wait_send()
        self.chip_hop(k).wait_send()


class Reduce:
    def __init__(self, peers, bits, send, work, came, total, sems, local):
        self.peers, self.send, self.work, self.came, self.total = peers, send, work, came, total
        self.sems, self.local = sems, local
        self.bits = bits
        self.extra = [h for h in range(peers.hops) if h not in bits]
        self.b = [peers.bit(h) for h in bits]
        b0, b1, b2 = self.b
        self.kept = b1 * 2 + b2
        self.piece = b0 * 4 + self.kept
        self.stage = 0

    def hop(self, t):
        _, b1, b2 = self.b
        if t == 0:
            source, target = self.send, self.came.at[pl.ds(0, 4)]
        elif t == 1:
            source, target = self.work.at[pl.ds((1 - b1) * 2, 2)], self.came.at[pl.ds(4, 2)]
        elif t == 2:
            source, target = self.work.at[pl.ds(b1 * 2 + 1 - b2, 1)], self.came.at[pl.ds(6, 1)]
        else:
            source, target = self.work.at[pl.ds(self.kept, 1)], self.came.at[pl.ds(4 + t, 1)]
        h = (list(self.bits) + self.extra)[t]
        return remote(source, target, self.sems, t, self.peers.partner(h))

    def back(self, t):
        b0, b1, _ = self.b
        where = (pl.ds(b0 * 4, 4), pl.ds(b0 * 4 + b1 * 2, 2), pl.ds(self.piece, 1))[t]
        source = self.work.at[pl.ds(self.kept, 1)] if t == 2 else self.total.at[where]
        index = 3 + len(self.extra) + t
        return remote(
            source, self.total.at[where], self.sems, index, self.peers.partner(self.bits[t])
        )

    def own(self):
        where = pl.ds(self.piece, 1)
        return pltpu.make_async_copy(
            self.work.at[pl.ds(self.kept, 1)], self.total.at[where], self.local
        )

    def begin(self):
        self.hop(0).start()

    def step(self, stage=None):
        t, last = self.stage if stage is None else stage, 3 + len(self.extra)
        self.stage = max(self.stage, t + 1)
        if t < last:
            _, b1, _ = self.b
            self.hop(t).wait_recv()
            if t > 2:
                self.hop(t).wait_send()
            base, first, count = (
                (0, 0, 4) if t == 0 else (b1 * 2, 4, 2) if t == 1 else (self.kept, 4 + t, 1)
            )

            def add(q):
                self.work[base + q] = (
                    self.work[base + q].astype(F32) + self.came[first + q].astype(F32)
                ).astype(BF)

            loop(count, add)
            if t + 1 < last:
                self.hop(t + 1).start()
            else:
                self.own().start()
                self.back(2).start()
        else:
            level = 2 - (t - last)
            self.back(level).wait_recv()
            if level == 2:
                self.own().wait()
            if level > 0:
                self.back(level - 1).start()

    def steps(self):
        return 6 + len(self.extra)

    def sent(self):
        for t in range(3):
            self.hop(t).wait_send()
            self.back(t).wait_send()


def by_rows(rows, fn, step=64):
    def one(r, carry):
        fn(pl.ds(pl.multiple_of(r * step, step), step))
        return carry

    lax.fori_loop(0, rows // step, one, 0)


def loop(count, fn):
    def one(k, carry):
        fn(k)
        return carry

    lax.fori_loop(0, count, one, 0)


def normalize(values, gain):
    scale = lax.rsqrt(jnp.mean(values * values, axis=-1, keepdims=True) + EPS)
    normed = values * scale
    return normed, scale, (normed * gain).astype(BF)


def norm_back(grad_out, normed, scale, gain):
    grad_normed = grad_out * gain
    inner = jnp.mean(grad_normed * normed, axis=-1, keepdims=True)
    return scale * (grad_normed - normed * inner)


def forward_kernel(
    length_ref, tokens, cotangent, wq, wk, wv, wg, wo, up, pair, down, gain_one, gain_two, gain_head,
    h1_out, qkvg_out, mixed_out, gated_out, state_out, g_out, res_out, middle_out, gmid_out, sums_out,
    gain_out,
    tok, w4, wo_v, up_v, pair_v, down_v, h1, h2, part, came, far, middle, gmid, state,
    load_sem, save_sem, gload_sem, h1_send, h1_recv, h2_send, h2_recv, g_send, g_recv,
    a_send, a_recv, b_send, b_recv,
):
    slots, rows, feat = tok.shape
    width, hid, wide = wo_v.shape[0], down.shape[0], down_v.shape[0]
    heads = width // HD
    peers = Peers()

    def load(source, target, index):
        return pltpu.make_async_copy(source, target, load_sem.at[index])

    real = pl.ds(0, hid)
    loads = [
        load(tokens, tok, 0),
        *(load(w, w4.at[m], 1 + m) for m, w in enumerate((wq, wk, wv, wg))),
        load(wo, wo_v, 5),
        load(up, up_v.at[real], 6),
        load(pair, pair_v.at[real], 7),
        load(down, down_v.at[real], 8),
        load(cotangent, g_out.at[:, 0], 9),
    ]
    for one in loads:
        one.start()
    peers.meet()
    first = Gather(peers, h1, (h1_send, h1_recv))
    second = Gather(peers, h2, (h2_send, h2_recv))
    grads = Gather(peers, g_out, (g_send, g_recv), lambda k: cotangent.at[k])
    buffers = (lambda k: part.at[k, pl.ds(2, 2)], lambda k: part.at[k, 1], came, far)
    scatter_a = Scatter(peers, *buffers, (a_send, a_recv))
    scatter_b = Scatter(peers, *buffers, (b_send, b_recv))
    g1, g2, gh = gain_one[...], gain_two[...], gain_head[...]

    loads[0].wait()

    def norm_first(k):
        def some(r):
            _, _, hidden = normalize(tok[k, r].astype(F32), g1)
            h1[k, 0, r] = hidden

        by_rows(rows, some)
        first.start(k)

    loop(slots, norm_first)
    loop(slots, lambda k: grads.core_hop(k).start())
    for target in (up_v, pair_v, down_v):
        target[hid:] = jnp.zeros((wide - hid, feat), BF)
    for one in loads[1:6]:
        one.wait()

    block = same_head(width)
    ones = block.astype(BF)

    def attend_all(qkvg, mixed_s, gated_s, state_s):
        def saves(k):
            return [
                pltpu.make_async_copy(qkvg, qkvg_out.at[k], save_sem.at[0]),
                pltpu.make_async_copy(mixed_s, mixed_out.at[k], save_sem.at[1]),
                pltpu.make_async_copy(gated_s, gated_out.at[k], save_sem.at[2]),
                pltpu.make_async_copy(state_s, state_out.at[k], save_sem.at[3]),
            ]

        def attend(k):
            first.forward(k)

            @pl.when(k == 1)
            def _():
                scatter_a.middle_step(0)
                grads.chip_hop(0).start()

            @pl.when(k > 0)
            def _():
                for one in saves(k - 1):
                    one.wait()

            first.arrived(k)
            state[...] = jnp.zeros_like(state)
            length = length_ref[k]

            def chunk(i):
                j = peers.relative(i)
                hidden = h1[k, j]
                position = lax.broadcasted_iota(jnp.int32, (rows, width), 0) + i * rows
                query = softplus(nn(hidden, w4[0])).astype(BF)
                keys = jnp.where(position < length, softplus(nn(hidden, w4[1])), 0.0).astype(BF)
                values = nn(hidden, w4[2]).astype(BF)
                gate = nn(hidden, w4[3])
                qkvg[j, 0] = query
                qkvg[j, 1] = keys
                qkvg[j, 2] = values
                qkvg[j, 3] = gate.astype(BF)
                before = state[...].astype(BF)
                state_s[i] = before
                scores = masked(nt(query, by_head(keys)), causal(rows, heads, False))
                mixed = nn(query, before) + nn(scores, by_head(values))
                state[...] += jnp.where(block, tn(keys, values), 0.0)
                mixed_s[j] = mixed.astype(BF)
                scale = lax.rsqrt(head_mean(mixed * mixed, ones) + EPS)
                gated_s[j] = (mixed * scale * gh * (gate * sigmoid(gate))).astype(BF)

            loop(BLOCKS, chunk)
            for one in saves(k):
                one.start()

            def project(p):
                j = (p % 2) * 2 + p // 2
                part[k, p] = nn(gated_s[j], wo_v[...]).astype(BF)

            project(2)
            project(3)
            scatter_a.start(k)
            project(1)
            project(0)

        loop(slots, attend)
        for one in saves(slots - 1):
            one.wait()

    v = pltpu.VMEM
    pl.run_scoped(
        attend_all,
        v((BLOCKS, 4, rows, width), BF),
        v((BLOCKS, rows, width), BF),
        v((BLOCKS, rows, width), BF),
        v((BLOCKS, width, width), BF),
    )

    def finish_attend(k):
        scatter_a.arrived(k)

        def some(r):
            value = (
                tok[k, r].astype(F32)
                + part[k, 0, r].astype(F32)
                + came[k, 0, r].astype(F32)
                + far[k, r].astype(F32)
            )
            middle[k, r] = value
            _, _, hidden = normalize(value, g2)
            h2[k, 0, r] = hidden

        by_rows(rows, some)
        second.start(k)
        scatter_a.sent(k)

    def follow(k):
        scatter_a.middle_step(k)
        grads.chip_hop(k).start()

    finish_attend(0)
    follow(1)
    h1_save = pltpu.make_async_copy(h1, h1_out, save_sem.at[4])
    h1_save.start()
    for one in loads[6:]:
        one.wait()

    def unit_all(prod_s, gu_s, gp_s, gbuf, res_s, sums, staged):
        def unit_save(k):
            return pltpu.make_async_copy(res_s, res_out.at[k], save_sem.at[9])

        def clear(m):
            sums[m // 3, pl.ds(pl.multiple_of(m % 3 * (wide // 3), wide // 3), wide // 3)] = jnp.zeros(
                (wide // 3, feat), F32
            )

        loop(9, clear)

        def unit(k):
            second.forward(k)
            grads.forward(k)

            @pl.when(k > 0)
            def _():
                unit_save(k - 1).wait()

            second.arrived(k)
            grads.arrived(k)
            for j in range(BLOCKS):
                pltpu.make_async_copy(g_out.at[k, j], gbuf.at[j], gload_sem.at[j]).start()

            def one(t):
                @pl.when((t == 2) & (k + 1 < slots))
                def _():
                    finish_attend(k + 1)

                @pl.when((t == 2) & (k + 2 < slots))
                def _():
                    follow(k + 2)

                j = t + (t // 2) * (1 - 2 * (t % 2))
                pltpu.make_async_copy(g_out.at[k, j], gbuf.at[j], gload_sem.at[j]).wait()
                hidden, grad = h2[k, j], gbuf[j]
                up_part = nt(hidden, up_v[...])
                pair_part = nt(hidden, pair_v[...])
                product = (up_part * pair_part).astype(BF)
                prod_s[j] = product
                res_s[spot(j)] = nn(product, down_v[...]).astype(BF)
                grad_product = nt(grad, down_v[...]).astype(BF).astype(F32)
                grad_up = (grad_product * pair_part).astype(BF)
                grad_pair = (grad_product * up_part).astype(BF)
                gu_s[j] = grad_up
                gp_s[j] = grad_pair
                part[k, spot(j)] = (nn(grad_up, up_v[...]) + nn(grad_pair, pair_v[...])).astype(BF)

                @pl.when(t == 2)
                def _():
                    scatter_b.start(k)

            loop(BLOCKS, one)
            unit_save(k).start()

            @pl.when(k == 1)
            def _():
                scatter_b.middle_step(0)

            @pl.when(k > 0)
            def _():
                scatter_b.middle_step(k)

            hidden_all = h2[k].reshape(BLOCKS * rows, feat)
            grad_all = gbuf[...].reshape(BLOCKS * rows, feat)
            tile = wide // 3

            def weigh(m):
                cols = pl.ds(pl.multiple_of(m * tile, tile), tile)

                def of(ref):
                    return ref[:, :, cols].reshape(BLOCKS * rows, tile)

                sums[0, cols] += tn(of(prod_s), grad_all)
                sums[1, cols] += tn(of(gu_s), hidden_all)
                sums[2, cols] += tn(of(gp_s), hidden_all)

            loop(3, weigh)

        loop(slots, unit)
        eighth = hid // 8

        def sums_save(c):
            return pltpu.make_async_copy(staged, sums_out.at[c], save_sem.at[6])

        for c in range(3):
            if c:
                sums_save(c - 1).wait()

            def convert(p):
                staged[p] = sums[c, pl.ds(pl.multiple_of(p * eighth, 8), eighth)].astype(BF)

            loop(8, convert)
            sums_save(c).start()
        sums_save(2).wait()
        unit_save(slots - 1).wait()

    pl.run_scoped(
        unit_all,
        v((BLOCKS, rows, wide), BF),
        v((BLOCKS, rows, wide), BF),
        v((BLOCKS, rows, wide), BF),
        v((BLOCKS, rows, feat), BF),
        v((BLOCKS, rows, feat), BF),
        v((3, wide, feat), F32),
        v((8, hid // 8, feat), BF),
    )
    middle_save = pltpu.make_async_copy(middle, middle_out, save_sem.at[5])
    middle_save.start()
    own_grads = load(cotangent, tok, 0)
    own_grads.start()
    own_grads.wait()
    gain_out[...] = jnp.zeros_like(gain_out)

    def gmid_save(k):
        return pltpu.make_async_copy(gmid.at[k % 2], gmid_out.at[k], save_sem.at[11 + k % 2])

    def finish_unit(k):
        scatter_b.arrived(k)

        @pl.when(k > 1)
        def _():
            gmid_save(k - 2).wait()

        def some(r):
            grad = (
                part[k, 0, r].astype(F32) + came[k, 0, r].astype(F32) + far[k, r].astype(F32)
            )
            normed, scale, _ = normalize(middle[k, r], g2)
            gain_out[...] += jnp.sum(grad * normed, axis=0, keepdims=True)
            gmid[k % 2, r] = tok[k, r].astype(F32) + norm_back(grad, normed, scale, g2)

        by_rows(rows, some)
        gmid_save(k).start()

    loop(slots, finish_unit)
    for k in range(max(slots - 2, 0), slots):
        gmid_save(k).wait()
    for save in (h1_save, middle_save):
        save.wait()

    def settle(k):
        first.sent(k)
        second.sent(k)
        grads.sent(k)
        scatter_b.sent(k)

    loop(slots, settle)


def dma(n):
    return pltpu.SemaphoreType.DMA((n,))


def anywhere(n):
    return [pl.BlockSpec(memory_space=pl.ANY)] * n


def in_vmem(n):
    return [pl.BlockSpec(memory_space=pltpu.VMEM)] * n


def forward(lengths, tokens, cotangent, q4, wo, up, pair, down, gain_one, gain_two, gain_head):
    slots, rows, feat = tokens.shape
    width, hid = wo.shape[0], down.shape[0]
    n = BLOCKS
    shape = jax.ShapeDtypeStruct
    wide = -(-hid // 256) * 256
    blocks = lambda *dims: shape((slots, n) + dims, BF)
    outs = [
        blocks(rows, feat),
        blocks(4, rows, width),
        blocks(rows, width),
        blocks(rows, width),
        blocks(width, width),
        blocks(rows, feat),
        blocks(rows, feat),
        shape((slots, rows, feat), F32),
        shape((slots, rows, feat), F32),
        shape((3, 8, hid // 8, feat), BF),
        shape((1, feat), F32),
    ]
    v = pltpu.VMEM
    scratch = [
        v((slots, rows, feat), BF),
        v((4, feat, width), BF),
        v((width, feat), BF),
        v((wide, feat), BF),
        v((wide, feat), BF),
        v((wide, feat), BF),
        v((slots, n, rows, feat), BF),
        v((slots, n, rows, feat), BF),
        v((slots, n, rows, feat), BF),
        v((slots, 2, rows, feat), BF),
        v((slots, rows, feat), BF),
        v((slots, rows, feat), F32),
        v((2, rows, feat), F32),
        v((width, width), F32),
        dma(10),
        dma(13),
        dma(n),
        *[dma(3 * slots)] * 6,
        *[dma(2 * slots)] * 4,
    ]
    total = slots * n * rows
    return pl.pallas_call(
        forward_kernel,
        in_specs=[pl.BlockSpec(memory_space=pltpu.SMEM)] + anywhere(10) + in_vmem(3),
        out_specs=anywhere(10) + in_vmem(1),
        out_shape=outs,
        scratch_shapes=scratch,
        compiler_params=pltpu.CompilerParams(
            collective_id=1, has_side_effects=True, vmem_limit_bytes=VMEM_LIMIT
        ),
        cost_estimate=pl.CostEstimate(
            flops=total * (10 * feat * width + 16 * width * width + 18 * feat * hid),
            transcendentals=total * 6 * width,
            bytes_accessed=2 * total * (6 * feat + 3 * hid),
        ),
        name="forward",
    )(lengths, tokens, cotangent, *q4, wo, up, pair, down, gain_one, gain_two, gain_head)


def backward_kernel(
    batch,
    tokens, middle, gmid, res, qkvg_in, mixed_in, state_in, h1_in, gated_in, sums_in,
    wq, wk, wv, wg, wo, gain_one, gain_head, two_part,
    result, grad_tokens, unit_total, qk_total, vg_total, out_total, gains,
    w4, wo_v, gm, part, came, far, res_mid, came2, far2, state,
    unit_work, unit_came, qk_send, qk_work, qk_came, vg_send, vg_work, vg_came,
    out_send, out_work, out_came, gain_came, head_part,
    load_sem, slot_sem, save_sem, unit_sem, local_sem,
    gm_send, gm_recv, a_send, a_recv, r_send, r_recv, gain_send, gain_recv,
    d_send, d_recv, u_send, u_recv, p_send, p_recv, q_send, q_recv, v_send, v_recv, o_send, o_recv,
):
    slots, _, rows, feat = gm.shape
    width = wo_v.shape[0]
    heads = width // HD
    peers = Peers(batch)

    def load(source, target, index):
        return pltpu.make_async_copy(source, target, load_sem.at[index])

    weight_loads = [
        *(load(w, w4.at[m], 1 + m) for m, w in enumerate((wq, wk, wv, wg))),
        load(wo, wo_v, 5),
        load(res.at[:, 1], res_mid, 6),
    ]
    half = peers.bit(0)
    unit_loads = [
        pltpu.make_async_copy(sums_in.at[c, pl.ds(half * 4, 4)], unit_work.at[c], unit_sem.at[c])
        for c in range(3)
    ]
    for one in (*weight_loads, *unit_loads):
        one.start()
    gather = Gather(peers, gm, (gm_send, gm_recv))
    scatter = Scatter(
        peers, lambda k: part.at[k, pl.ds(2, 2)], lambda k: part.at[k, 1], came, far, (a_send, a_recv)
    )
    results = Scatter(
        peers, lambda k: res.at[k, pl.ds(2, 2)], lambda k: res_mid.at[k], came2, far2, (r_send, r_recv)
    )
    unit_sums = [
        Reduce(
            peers, (0, 1, 2), sums_in.at[c, pl.ds((1 - half) * 4, 4)], unit_work.at[c],
            unit_came.at[c], unit_total.at[c], sems, local_sem.at[c],
        )
        for c, sems in enumerate(((d_send, d_recv), (u_send, u_recv), (p_send, p_recv)))
    ]
    down_sum, up_sum, pair_sum = unit_sums
    qk_sum = Reduce(
        peers, (1, 2, 0), qk_send, qk_work, qk_came, qk_total, (q_send, q_recv), local_sem.at[3]
    )
    vg_sum = Reduce(
        peers, (0, 1, 2), vg_send, vg_work, vg_came, vg_total, (v_send, v_recv), local_sem.at[4]
    )
    out_sum = Reduce(
        peers, (0, 1, 2), out_send, out_work, out_came, out_total, (o_send, o_recv), local_sem.at[5]
    )
    g1, gh = gain_one[...], gain_head[...]
    head_part[...] = jnp.zeros_like(head_part)
    gains[...] = jnp.zeros_like(gains)
    gains[1:2] = two_part[...]
    peers.meet()
    for one in unit_sums:
        one.begin()
    v = pltpu.VMEM

    def begin_all(gmv):
        whole = load(gmid, gmv, 0)
        whole.start()
        whole.wait()

        def begin(k):
            def some(r):
                gm[k, 0, r] = gmv[k, r].astype(BF)

            by_rows(rows, some)
            gather.start(k)

        loop(slots, begin)

    pl.run_scoped(begin_all, v((slots, rows, feat), F32))
    loop(slots, results.start)
    for one in weight_loads:
        one.wait()
    for one in unit_loads:
        one.wait()
    block = same_head(width)
    ones = block.astype(BF)

    def attend_all(qkvg, mixed_v, state_v, h1, gated, pre, sums, out_acc):
        def slot_loads(k):
            b = k % 2
            pairs = (
                (qkvg_in, qkvg), (mixed_in, mixed_v), (state_in, state_v), (h1_in, h1), (gated_in, gated)
            )
            return [
                pltpu.make_async_copy(source.at[k], target.at[b], slot_sem.at[5 * b + m])
                for m, (source, target) in enumerate(pairs)
            ]

        for one in slot_loads(0):
            one.start()

        def attend_back(k):
            b = k % 2
            gather.forward(k)

            @pl.when(k > 0)
            def _():
                scatter.middle_step(k - 1)

            @pl.when(k + 1 < slots)
            def _():
                for one in slot_loads(k + 1):
                    one.start()

            for one in slot_loads(k):
                one.wait()
            gather.arrived(k)
            state[...] = jnp.zeros_like(state)

            def chunk(step):
                @pl.when((k == 0) & (step == 2))
                def _():
                    down_sum.step(0)

                @pl.when((k == 1) & (step == 1))
                def _():
                    down_sum.step(2)
                    up_sum.step(1)

                @pl.when((k == 2) & (step == 1))
                def _():
                    down_sum.step(4)
                    up_sum.step(3)
                    pair_sum.step(1)

                i = BLOCKS - 1 - step
                j = peers.relative(i)
                grad_gated = nt(gm[k, j], wo_v[...]).astype(BF).astype(F32)
                query, keys, values = qkvg[b, j, 0], qkvg[b, j, 1], qkvg[b, j, 2]
                gate = qkvg[b, j, 3].astype(F32)
                mixed = mixed_v[b, j].astype(F32)
                scale = lax.rsqrt(head_mean(mixed * mixed, ones) + EPS)
                normed = mixed * scale
                opened = sigmoid(gate)
                grad_gate = grad_gated * (normed * gh) * opened * (1.0 + gate * (1.0 - opened))
                grad_head = grad_gated * (gate * opened)
                head_part[...] += jnp.sum(grad_head * normed, axis=0, keepdims=True)
                scaled = grad_head * gh
                inner = head_mean(scaled * normed, ones)
                grad_mixed = (scale * (scaled - normed * inner)).astype(BF)
                after = state[...].astype(BF)
                before = state_v[b, i]
                lower = causal(rows, heads, False)
                upper = causal(rows, heads, True)
                query_heads = by_head(query)
                mixed_heads = by_head(grad_mixed)
                grad_scores = masked(nt(grad_mixed, by_head(values)), lower)
                grad_query = nt(grad_mixed, before) + nn(grad_scores, by_head(keys))
                grad_scores_t = masked(nt(values, mixed_heads), upper)
                grad_keys = nt(values, after) + nn(grad_scores_t, query_heads)
                scores_t = masked(nt(keys, query_heads), upper)
                grad_values = nn(keys, after) + nn(scores_t, mixed_heads)
                state[...] += jnp.where(block, tn(query, grad_mixed), 0.0)

                rounded = lambda v: v.astype(BF).astype(F32)
                pre_q = (rounded(grad_query) * sigmoid_of_softplus(query.astype(F32))).astype(BF)
                pre_k = (rounded(grad_keys) * sigmoid_of_softplus(keys.astype(F32))).astype(BF)
                pre_v = grad_values.astype(BF)
                pre_g = grad_gate.astype(BF)
                for m, one in enumerate((pre_q, pre_k, pre_v, pre_g)):
                    pre[j, :, m * width : (m + 1) * width] = one
                grad_h = nt(pre_q, w4[0]) + nt(pre_k, w4[1]) + nt(pre_v, w4[2]) + nt(pre_g, w4[3])
                part[k, spot(j)] = grad_h.astype(BF)

            loop(BLOCKS, chunk)
            scatter.start(k)
            results.middle_step(k)

            @pl.when(k == 0)
            def _():
                down_sum.step(1)
                up_sum.step(0)

            @pl.when(k == 1)
            def _():
                down_sum.step(3)
                up_sum.step(2)
                pair_sum.step(0)

            pre_all = pre[...].reshape(BLOCKS * rows, 4 * width)

            def weigh(m):
                cols = pl.ds(pl.multiple_of(m * 256, 256), 256)
                term = tn(h1[b, :, :, cols].reshape(BLOCKS * rows, 256), pre_all)
                sums[cols] = jnp.where(k > 0, sums[cols], 0.0) + term

            loop(feat // 256, weigh)
            term = tn(gated[b].reshape(BLOCKS * rows, width), gm[k].reshape(BLOCKS * rows, feat))
            out_acc[...] = jnp.where(k > 0, out_acc[...], 0.0) + term

        loop(slots, attend_back)
        scatter.middle_step(slots - 1)
        eighth, part_rows = feat // 8, width // 8

        first = peers.bit(1)

        def fill_all(q):
            at = lambda top: pl.ds(pl.multiple_of((top * 4 + q) * eighth, eighth), eighth)
            qk_work[q] = sums[at(first), : 2 * width].astype(BF)
            qk_send[q] = sums[at(1 - first), : 2 * width].astype(BF)
            vg_work[q] = sums[at(half), 2 * width :].astype(BF)
            vg_send[q] = sums[at(1 - half), 2 * width :].astype(BF)
            small = lambda top: pl.ds(
                pl.multiple_of((top * 4 + q) * part_rows, part_rows), part_rows
            )
            out_work[q] = out_acc[small(half)].astype(BF)
            out_send[q] = out_acc[small(1 - half)].astype(BF)

        loop(4, fill_all)
        for one in (vg_sum, out_sum, qk_sum):
            one.begin()

    pl.run_scoped(
        attend_all,
        v((2, BLOCKS, 4, rows, width), BF),
        v((2, BLOCKS, rows, width), BF),
        v((2, BLOCKS, width, width), BF),
        v((2, BLOCKS, rows, feat), BF),
        v((2, BLOCKS, rows, width), BF),
        v((BLOCKS, rows, 4 * width), BF),
        v((feat, 4 * width), F32),
        v((width, feat), F32),
    )

    def finish_all(tok, mid, gmv, kept):
        finals = [
            load(tokens, tok, 1),
            load(middle, mid, 2),
            load(gmid, gmv, 3),
            load(res.at[:, 0], kept, 4),
        ]
        for one in finals:
            one.start()

        def grad_save(k):
            return pltpu.make_async_copy(gmv.at[k], grad_tokens.at[k], save_sem.at[k])

        def result_save(k):
            return pltpu.make_async_copy(tok.at[k], result.at[k], save_sem.at[slots + k])

        def finish(k):
            scatter.arrived(k)

            def some(r):
                grad = (
                    part[k, 0, r].astype(F32) + came[k, 0, r].astype(F32) + far[k, r].astype(F32)
                )
                normed, scale, _ = normalize(tok[k, r].astype(F32), g1)
                gains[0:1] += jnp.sum(grad * normed, axis=0, keepdims=True)
                gmv[k, r] = gmv[k, r] + norm_back(grad, normed, scale, g1)

            by_rows(rows, some)
            grad_save(k).start()

        def finish_result(k):
            results.arrived(k)

            def some(r):
                total = (
                    mid[k, r]
                    + kept[k, r].astype(F32)
                    + came2[k, 0, r].astype(F32)
                    + far2[k, r].astype(F32)
                )
                tok[k, r] = total.astype(BF)

            by_rows(rows, some)
            result_save(k).start()

        up_sum.step()
        pair_sum.step()
        for one in finals:
            one.wait()
        finish(0)
        finish_result(0)
        qk_sum.step()
        pair_sum.step()
        vg_sum.step()
        out_sum.step()
        finish(1)
        finish_result(1)
        qk_sum.step()
        pair_sum.step()
        vg_sum.step()
        out_sum.step()
        up_sum.step()
        qk_sum.step()
        for k in range(2, slots):
            finish(k)
            finish_result(k)
        lane = lax.broadcasted_iota(jnp.int32, (1, BLOCKS * width), 1) // width
        spread = jnp.concatenate([head_part[...]] * BLOCKS, axis=1)
        gains[2:3] = jnp.where(lane == peers.place, spread, 0.0)
        others = [peers.beside, peers.across] + [peers.partner(h) for h in range(peers.hops)]

        def gain_hop(t):
            return remote(gains, gain_came.at[t], (gain_send, gain_recv), t, others[t])

        def gain_step(t):
            gain_hop(t).wait_recv()
            gain_hop(t).wait_send()
            gains[...] += gain_came[t]
            if t + 1 < len(others):
                gain_hop(t + 1).start()

        gain_hop(0).start()
        waiting = [vg_sum, out_sum, pair_sum, qk_sum, up_sum]
        order = [one for _ in range(8) for one in waiting]
        hop = 0
        for one in order:
            if one.stage < one.steps():
                one.step()
                if hop < len(others):
                    gain_step(hop)
                    hop += 1
        while hop < len(others):
            gain_step(hop)
            hop += 1
        for one in (*unit_sums, qk_sum, vg_sum, out_sum):
            while one.stage < one.steps():
                one.step()
        for one in (*unit_sums, qk_sum, vg_sum, out_sum):
            one.sent()

        def settle(k):
            grad_save(k).wait()
            result_save(k).wait()
            gather.sent(k)
            scatter.sent(k)
            results.sent(k)

        loop(slots, settle)

    pl.run_scoped(
        finish_all,
        v((slots, rows, feat), BF),
        v((slots, rows, feat), F32),
        v((slots, rows, feat), F32),
        v((slots, rows, feat), BF),
    )


def backward(batch, tokens, middle, gmid, res, saved, sums, q4, wo, gain_one, gain_head, two_part):
    slots, rows, feat = tokens.shape
    width = wo.shape[0]
    eighth = sums.shape[2]
    n = BLOCKS
    shape = jax.ShapeDtypeStruct
    v = pltpu.VMEM
    outs = [
        shape((slots, rows, feat), BF),
        shape((slots, rows, feat), F32),
        shape(sums.shape, BF),
        shape((8, feat // 8, 2 * width), BF),
        shape((8, feat // 8, 2 * width), BF),
        shape((8, width // 8, feat), BF),
        shape((3, feat), F32),
    ]
    hops = batch.bit_length() - 1
    extra = hops - 3

    def pieces(*dims):
        return [v((4,) + dims, BF), v((4,) + dims, BF), v((7 + extra,) + dims, BF)]

    scratch = [
        v((4, feat, width), BF),
        v((width, feat), BF),
        v((slots, n, rows, feat), BF),
        v((slots, n, rows, feat), BF),
        v((slots, 2, rows, feat), BF),
        v((slots, rows, feat), BF),
        v((slots, rows, feat), BF),
        v((slots, 2, rows, feat), BF),
        v((slots, rows, feat), BF),
        v((width, width), F32),
        v((3, 4, eighth, feat), BF),
        v((3, 7 + extra, eighth, feat), BF),
        *pieces(feat // 8, 2 * width),
        *pieces(feat // 8, 2 * width),
        *pieces(width // 8, feat),
        v((hops + 2, 3, feat), F32),
        v((1, width), F32),
        dma(7),
        dma(10),
        dma(2 * slots),
        dma(3),
        dma(6),
        *[dma(3 * slots)] * 2,
        *[dma(2 * slots)] * 4,
        *[dma(hops + 2)] * 2,
        *[dma(6 + extra)] * 12,
    ]
    total = slots * n * rows
    return pl.pallas_call(
        functools.partial(backward_kernel, batch),
        in_specs=anywhere(15) + in_vmem(3),
        out_specs=anywhere(6) + in_vmem(1),
        out_shape=outs,
        scratch_shapes=scratch,
        compiler_params=pltpu.CompilerParams(
            collective_id=2, has_side_effects=True, vmem_limit_bytes=VMEM_LIMIT
        ),
        cost_estimate=pl.CostEstimate(
            flops=total * (20 * feat * width + 40 * width * width),
            transcendentals=total * 6 * width,
            bytes_accessed=2 * total * (6 * feat),
        ),
        name="backward",
    )(tokens, middle, gmid, res, *saved, sums, *q4, wo, gain_one, gain_head, two_part)


def widen_kernel(unit, qk, vg, out, *targets):
    width = qk.shape[2] // 2
    for c, at in enumerate((2, 0, 1)):
        targets[5 + at][...] = unit[c, 0].astype(F32)
    targets[0][...] = qk[0, :, :width].astype(F32)
    targets[1][...] = qk[0, :, width:].astype(F32)
    targets[2][...] = vg[0, :, :width].astype(F32)
    targets[3][...] = vg[0, :, width:].astype(F32)
    targets[4][...] = out[0].astype(F32)


def widen(unit, qk, vg, out):
    eighth, feat = unit.shape[2:]
    width = qk.shape[2] // 2
    block = lambda dims: pl.BlockSpec((1,) + dims, lambda i: (i, 0, 0))
    flat = lambda dims: pl.BlockSpec(dims, lambda i: (i, 0))
    whole = lambda rows, cols: jax.ShapeDtypeStruct((8 * rows, cols), F32)
    return pl.pallas_call(
        widen_kernel,
        grid=(8,),
        in_specs=[
            pl.BlockSpec((3, 1, eighth, feat), lambda i: (0, i, 0, 0)),
            block(qk.shape[1:]),
            block(vg.shape[1:]),
            block(out.shape[1:]),
        ],
        out_specs=[flat((feat // 8, width))] * 4
        + [flat((width // 8, feat))]
        + [flat((eighth, feat))] * 3,
        out_shape=[whole(feat // 8, width)] * 4 + [whole(width // 8, feat)] + [whole(eighth, feat)] * 3,
        compiler_params=pltpu.CompilerParams(vmem_limit_bytes=VMEM_LIMIT),
        name="widen",
    )(unit, qk, vg, out)


def on_device(
    batch,
    tokens,
    lengths,
    assignment,
    query_weight,
    key_weight,
    value_weight,
    gate_weight,
    out_weight,
    up_weight,
    pair_weight,
    down_weight,
    attention_norm_gain,
    mlp_gain,
    head_gain,
    cotangent,
):
    slots = tokens.shape[0]
    width = query_weight.shape[1]
    place = lax.axis_index("seq").astype(jnp.int32)
    seq_ids = lax.broadcasted_iota(jnp.int32, (slots, lengths.shape[0]), 1)
    slot_length = jnp.sum(jnp.where(assignment[:, None] == seq_ids, lengths[None, :], 0), axis=1)
    q4 = (query_weight, key_weight, value_weight, gate_weight)
    gain_one, gain_two, gain_head = attention_norm_gain[None], mlp_gain[None], head_gain[None]
    h_one, qkvg, mixed, gated, states, _, res, middle, gmid, sums, two_part = forward(
        slot_length, tokens, cotangent, q4, out_weight, up_weight.T, pair_weight.T, down_weight,
        gain_one, gain_two, gain_head,
    )
    result, grad_inputs, unit_total, qk_total, vg_total, out_total, gains = backward(
        batch, tokens, middle, gmid, res, (qkvg, mixed, states, h_one, gated), sums, q4, out_weight,
        gain_one, gain_head, two_part,
    )
    grad_qw, grad_kw, grad_vw, grad_gw, grad_outw, grad_upw, grad_pairw, grad_down = widen(
        unit_total, qk_total, vg_total, out_total
    )
    head_total = lax.dynamic_slice(gains[2], (place * width,), (width,))
    return (
        result,
        grad_inputs,
        grad_qw,
        grad_kw,
        grad_vw,
        grad_gw,
        grad_outw,
        grad_upw.T,
        grad_pairw.T,
        grad_down,
        gains[0],
        gains[1],
        head_total,
    )


def solution(mesh):
    return jax.shard_map(
        functools.partial(on_device, mesh.shape["batch"]),
        mesh=mesh,
        in_specs=(
            P("batch", "seq", None),
            P(),
            P("batch"),
            P(None, "seq"),
            P(None, "seq"),
            P(None, "seq"),
            P(None, "seq"),
            P("seq", None),
            P(None, "seq"),
            P(None, "seq"),
            P("seq", None),
            P(),
            P(),
            P("seq"),
            P("batch", "seq", None),
        ),
        out_specs=(
            P("batch", "seq", None),
            P("batch", "seq", None),
            P(None, "seq"),
            P(None, "seq"),
            P(None, "seq"),
            P(None, "seq"),
            P("seq", None),
            P(None, "seq"),
            P(None, "seq"),
            P("seq", None),
            P(),
            P(),
            P("seq"),
        ),
        check_vma=False,
    )
```

```python
import functools

import jax
import jax.numpy as jnp
from jax import lax
from jax.experimental import pallas as pl
from jax.experimental.pallas import tpu as pltpu
from jax.sharding import PartitionSpec as P

HD = 64
EPS = 1e-05
BF = jnp.bfloat16
F32 = jnp.float32
VMEM_LIMIT = 62 * 1024 * 1024
MESH = pl.DeviceIdType.MESH
BLOCKS = 4


def nn(a, b):
    return lax.dot_general(a, b, (((1,), (0,)), ((), ())), preferred_element_type=F32)


def nt(a, b):
    return lax.dot_general(a, b, (((1,), (1,)), ((), ())), preferred_element_type=F32)


def tn(a, b):
    return lax.dot_general(a, b, (((0,), (0,)), ((), ())), preferred_element_type=F32)


def same_head(width):
    rows = lax.broadcasted_iota(jnp.int32, (width, width), 0) // HD
    cols = lax.broadcasted_iota(jnp.int32, (width, width), 1) // HD
    return rows == cols


def by_head(array):
    rows, width = array.shape
    lane = lax.broadcasted_iota(jnp.int32, (rows, width), 1) // HD
    zero = jnp.zeros_like(array)
    return jnp.concatenate([jnp.where(lane == h, array, zero) for h in range(width // HD)], axis=0)


def causal(rows, heads, transposed):
    one = lax.broadcasted_iota(jnp.int32, (rows, rows), 0)
    two = lax.broadcasted_iota(jnp.int32, (rows, rows), 1)
    keep = (two >= one) if transposed else (one >= two)
    return jnp.concatenate([keep] * heads, axis=1)


def masked(scores, keep):
    return jnp.where(keep, scores, 0.0).astype(BF)


def head_mean(array, ones):
    return nn(array.astype(BF), ones) * (1.0 / HD)


def softplus(v):
    return jnp.maximum(v, 0.0) + jnp.log1p(jnp.exp(-jnp.abs(v)))


def sigmoid_of_softplus(q):
    series = q * (1.0 - q * (0.5 - q * (1.0 / 6.0)))
    return jnp.where(q < 0.03, series, 1.0 - jnp.exp(-q))


def sigmoid(v):
    return 1.0 / (1.0 + jnp.exp(-v))


class Peers:
    def __init__(self, batch=1):
        self.place = lax.axis_index("seq")
        self.group = lax.axis_index("batch")
        self.chip, self.core = self.place // 2, self.place % 2
        self.across = (self.group, (1 - self.chip) * 2 + self.core)
        self.beside = (self.group, self.chip * 2 + 1 - self.core)
        self.hops = batch.bit_length() - 1

    def bit(self, h):
        return (self.group // 2**h) % 2

    def partner(self, h):
        return (self.group + (1 - 2 * self.bit(h)) * 2**h, self.place)

    def meet(self):
        others = [self.across, self.beside] + [self.partner(h) for h in range(self.hops)]
        barrier = pltpu.get_barrier_semaphore()
        for peer in others:
            pl.semaphore_signal(barrier, inc=1, device_id=peer, device_id_type=MESH)
        pl.semaphore_wait(barrier, len(others))

    def relative(self, index):
        return ((index // 2 + self.chip) % 2) * 2 + (index % 2 + self.core) % 2


def spot(j):
    return (j % 2) * 2 + j // 2


def remote(source, target, sems, index, peer):
    send, recv = sems
    return pltpu.make_async_remote_copy(
        src_ref=source,
        dst_ref=target,
        send_sem=send.at[index],
        recv_sem=recv.at[index],
        device_id=peer,
        device_id_type=MESH,
    )


class Gather:
    def __init__(self, peers, buffer, sems, own=None):
        self.peers, self.buffer, self.sems = peers, buffer, sems
        self.own = own or (lambda k: buffer.at[k, 0])

    def chip_hop(self, k):
        return remote(self.own(k), self.buffer.at[k, 2], self.sems, 3 * k, self.peers.across)

    def core_hop(self, k):
        return remote(self.own(k), self.buffer.at[k, 1], self.sems, 3 * k + 1, self.peers.beside)

    def passed_on(self, k):
        return remote(
            self.buffer.at[k, 2], self.buffer.at[k, 3], self.sems, 3 * k + 2, self.peers.beside
        )

    def start(self, k):
        self.chip_hop(k).start()
        self.core_hop(k).start()

    def forward(self, k):
        self.chip_hop(k).wait_recv()
        self.passed_on(k).start()

    def arrived(self, k):
        self.core_hop(k).wait_recv()
        self.passed_on(k).wait_recv()

    def sent(self, k):
        self.chip_hop(k).wait_send()
        self.core_hop(k).wait_send()
        self.passed_on(k).wait_send()


class Scatter:
    def __init__(self, peers, pair, middle, came, far, sems):
        self.peers, self.pair, self.middle = peers, pair, middle
        self.came, self.far, self.sems = came, far, sems

    def core_hop(self, k):
        return remote(self.pair(k), self.came.at[k], self.sems, 2 * k, self.peers.beside)

    def chip_hop(self, k):
        return remote(self.middle(k), self.far.at[k], self.sems, 2 * k + 1, self.peers.across)

    def start(self, k):
        self.core_hop(k).start()

    def middle_step(self, k):
        self.core_hop(k).wait_recv()
        middle = self.middle(k)

        def add(rows):
            middle[rows] = (middle[rows].astype(F32) + self.came[k, 1, rows].astype(F32)).astype(BF)

        by_rows(middle.shape[0], add)
        self.chip_hop(k).start()

    def arrived(self, k):
        self.chip_hop(k).wait_recv()

    def sent(self, k):
        self.core_hop(k).wait_send()
        self.chip_hop(k).wait_send()


class Reduce:
    def __init__(self, peers, bits, send, work, came, total, sems, local, early=None):
        self.early = early
        self.peers, self.send, self.work, self.came, self.total = peers, send, work, came, total
        self.sems, self.local = sems, local
        self.bits = bits
        self.extra = [h for h in range(peers.hops) if h not in bits]
        self.b = [peers.bit(h) for h in bits]
        b0, b1, b2 = self.b
        self.kept = b1 * 2 + b2
        self.piece = b0 * 4 + self.kept
        self.stage = 0

    def hop(self, t):
        _, b1, b2 = self.b
        if t == 0:
            source, target = self.send, self.came.at[pl.ds(0, 4)]
        elif t == 1:
            source, target = self.work.at[pl.ds((1 - b1) * 2, 2)], self.came.at[pl.ds(4, 2)]
        elif t == 2:
            source, target = self.work.at[pl.ds(b1 * 2 + 1 - b2, 1)], self.came.at[pl.ds(6, 1)]
        else:
            source, target = self.work.at[pl.ds(self.kept, 1)], self.came.at[pl.ds(4 + t, 1)]
        h = (list(self.bits) + self.extra)[t]
        return remote(source, target, self.sems, t, self.peers.partner(h))

    def back(self, t):
        b0, b1, _ = self.b
        where = (pl.ds(b0 * 4, 4), pl.ds(b0 * 4 + b1 * 2, 2), pl.ds(self.piece, 1))[t]
        source = self.work.at[pl.ds(self.kept, 1)] if t == 2 else self.total.at[where]
        index = 3 + len(self.extra) + t
        return remote(
            source, self.total.at[where], self.sems, index, self.peers.partner(self.bits[t])
        )

    def own(self):
        where = pl.ds(self.piece, 1)
        return pltpu.make_async_copy(
            self.work.at[pl.ds(self.kept, 1)], self.total.at[where], self.local
        )

    def begin(self):
        self.hop(0).start()

    def step(self, stage=None):
        t, last = self.stage if stage is None else stage, 3 + len(self.extra)
        self.stage = max(self.stage, t + 1)
        if t < last:
            _, b1, _ = self.b
            if t == 0 and self.early is not None:
                self.early.wait()
            else:
                self.hop(t).wait_recv()
            if t > 2:
                self.hop(t).wait_send()
            base, first, count = (
                (0, 0, 4) if t == 0 else (b1 * 2, 4, 2) if t == 1 else (self.kept, 4 + t, 1)
            )

            def add(q):
                self.work[base + q] = (
                    self.work[base + q].astype(F32) + self.came[first + q].astype(F32)
                ).astype(BF)

            loop(count, add)
            if t + 1 < last:
                self.hop(t + 1).start()
            else:
                self.own().start()
                self.back(2).start()
        else:
            level = 2 - (t - last)
            self.back(level).wait_recv()
            if level == 2:
                self.own().wait()
            if level > 0:
                self.back(level - 1).start()

    def steps(self):
        return 6 + len(self.extra)

    def sent(self):
        for t in range(3):
            if t or self.early is None:
                self.hop(t).wait_send()
            self.back(t).wait_send()


def by_rows(rows, fn, step=64):
    def one(r, carry):
        fn(pl.ds(pl.multiple_of(r * step, step), step))
        return carry

    lax.fori_loop(0, rows // step, one, 0)


def loop(count, fn):
    def one(k, carry):
        fn(k)
        return carry

    lax.fori_loop(0, count, one, 0)


def normalize(values, gain):
    scale = lax.rsqrt(jnp.mean(values * values, axis=-1, keepdims=True) + EPS)
    normed = values * scale
    return normed, scale, (normed * gain).astype(BF)


def norm_back(grad_out, normed, scale, gain):
    grad_normed = grad_out * gain
    inner = jnp.mean(grad_normed * normed, axis=-1, keepdims=True)
    return scale * (grad_normed - normed * inner)


def forward_kernel(
    batch,
    length_ref, tokens, cotangent, wq, wk, wv, wg, wo, up, pair, down, gain_one, gain_two, gain_head,
    h1_out, qkvg_out, mixed_out, gated_out, state_out, g_out, res_out, middle_out, gmid_out, sums_out,
    down_came, gain_out,
    tok, w4, wo_v, up_v, pair_v, down_v, h1, h2, part, came, far, middle, state,
    load_sem, save_sem, gload_sem, h1_send, h1_recv, h2_send, h2_recv, g_send, g_recv,
    a_send, a_recv, b_send, b_recv, y_send, y_recv,
):
    slots, rows, feat = tok.shape
    width, hid, wide = wo_v.shape[0], down.shape[0], down_v.shape[0]
    heads = width // HD
    peers = Peers(batch)
    peers.hops = 1

    def load(source, target, index):
        return pltpu.make_async_copy(source, target, load_sem.at[index])

    real = pl.ds(0, hid)
    loads = [
        load(tokens, tok, 0),
        *(load(w, w4.at[m], 1 + m) for m, w in enumerate((wq, wk, wv, wg))),
        load(wo, wo_v, 5),
        load(up, up_v.at[real], 6),
        load(pair, pair_v.at[real], 7),
        load(down, down_v.at[real], 8),
        load(cotangent, g_out.at[:, 0], 9),
    ]
    for one in loads:
        one.start()
    peers.meet()
    down_hop = remote(
        sums_out.at[0, pl.ds((1 - peers.bit(0)) * 4, 4)], down_came, (y_send, y_recv), 0,
        peers.partner(0),
    )
    first = Gather(peers, h1, (h1_send, h1_recv))
    second = Gather(peers, h2, (h2_send, h2_recv))
    grads = Gather(peers, g_out, (g_send, g_recv), lambda k: cotangent.at[k])
    buffers = (lambda k: part.at[k, pl.ds(2, 2)], lambda k: part.at[k, 1], came, far)
    scatter_a = Scatter(peers, *buffers, (a_send, a_recv))
    scatter_b = Scatter(peers, *buffers, (b_send, b_recv))
    g1, g2, gh = gain_one[...], gain_two[...], gain_head[...]
    grads.chip_hop(0).start()
    loads[0].wait()

    def norm_first(k):
        def some(r):
            _, _, hidden = normalize(tok[k, r].astype(F32), g1)
            h1[k, 0, r] = hidden

        by_rows(rows, some)
        first.start(k)

    loop(slots, norm_first)
    loop(slots, lambda k: grads.core_hop(k).start())
    for target in (up_v, pair_v, down_v):
        target[hid:] = jnp.zeros((wide - hid, feat), BF)
    for one in loads[1:6]:
        one.wait()

    block = same_head(width)
    ones = block.astype(BF)

    def attend_all(qkvg, mixed_s, gated_s, state_s):
        def saves(k):
            return [
                pltpu.make_async_copy(qkvg, qkvg_out.at[k], save_sem.at[0]),
                pltpu.make_async_copy(mixed_s, mixed_out.at[k], save_sem.at[1]),
                pltpu.make_async_copy(gated_s, gated_out.at[k], save_sem.at[2]),
                pltpu.make_async_copy(state_s, state_out.at[k], save_sem.at[3]),
            ]

        def attend(k):
            first.forward(k)

            @pl.when(k == 1)
            def _():
                scatter_a.middle_step(0)
                grads.chip_hop(1).start()

            @pl.when(k > 0)
            def _():
                for one in saves(k - 1):
                    one.wait()

            first.arrived(k)
            state[...] = jnp.zeros_like(state)
            length = length_ref[k]

            def chunk(i):
                j = peers.relative(i)
                hidden = h1[k, j]
                position = lax.broadcasted_iota(jnp.int32, (rows, width), 0) + i * rows
                query = softplus(nn(hidden, w4[0])).astype(BF)
                keys = jnp.where(position < length, softplus(nn(hidden, w4[1])), 0.0).astype(BF)
                values = nn(hidden, w4[2]).astype(BF)
                gate = nn(hidden, w4[3])
                qkvg[j, 0] = query
                qkvg[j, 1] = keys
                qkvg[j, 2] = values
                qkvg[j, 3] = gate.astype(BF)
                before = state[...].astype(BF)
                state_s[i] = before
                scores = masked(nt(query, by_head(keys)), causal(rows, heads, False))
                mixed = nn(query, before) + nn(scores, by_head(values))
                state[...] += jnp.where(block, tn(keys, values), 0.0)
                mixed_s[j] = mixed.astype(BF)
                scale = lax.rsqrt(head_mean(mixed * mixed, ones) + EPS)
                gated_s[j] = (mixed * scale * gh * (gate * sigmoid(gate))).astype(BF)

            loop(BLOCKS, chunk)
            for one in saves(k):
                one.start()

            def project(p):
                j = (p % 2) * 2 + p // 2
                part[k, p] = nn(gated_s[j], wo_v[...]).astype(BF)

            project(2)
            project(3)
            scatter_a.start(k)
            project(1)
            project(0)

        loop(slots, attend)
        for one in saves(slots - 1):
            one.wait()

    v = pltpu.VMEM
    pl.run_scoped(
        attend_all,
        v((BLOCKS, 4, rows, width), BF),
        v((BLOCKS, rows, width), BF),
        v((BLOCKS, rows, width), BF),
        v((BLOCKS, width, width), BF),
    )

    def finish_attend(k):
        scatter_a.arrived(k)

        def some(r):
            value = (
                tok[k, r].astype(F32)
                + part[k, 0, r].astype(F32)
                + came[k, 0, r].astype(F32)
                + far[k, r].astype(F32)
            )
            middle[k, r] = value
            _, _, hidden = normalize(value, g2)
            h2[k, 0, r] = hidden

        by_rows(rows, some)
        second.start(k)
        scatter_a.sent(k)

    finish_attend(0)
    for k in range(1, slots):
        scatter_a.middle_step(k)
    h1_save = pltpu.make_async_copy(h1, h1_out, save_sem.at[4])
    h1_save.start()
    for one in loads[6:]:
        one.wait()

    def unit_all(prod_s, gu_s, gp_s, gbuf, res_s, sums, staged):
        def unit_save(k):
            return pltpu.make_async_copy(res_s, res_out.at[k], save_sem.at[9])

        def clear(m):
            sums[m // 3, pl.ds(pl.multiple_of(m % 3 * (wide // 3), wide // 3), wide // 3)] = jnp.zeros(
                (wide // 3, feat), F32
            )

        loop(9, clear)

        def gload(k, j):
            return pltpu.make_async_copy(g_out.at[k, j], gbuf.at[j], gload_sem.at[j])

        tile = wide // 3
        eighth = hid // 8

        def weigh(c, left, right):
            def one(m):
                cols = pl.ds(pl.multiple_of(m * tile, tile), tile)
                sums[c, cols] += tn(left[:, :, cols].reshape(BLOCKS * rows, tile), right())

            loop(3, one)

        def sums_save(c):
            return pltpu.make_async_copy(staged, sums_out.at[c], save_sem.at[6])

        def settle_sums(c):
            def convert(p):
                staged[p] = sums[c, pl.ds(pl.multiple_of(p * eighth, 8), eighth)].astype(BF)

            loop(8, convert)
            sums_save(c).start()

        def unit(k):
            second.core_hop(k).wait_recv()
            grads.core_hop(k).wait_recv()
            gload(k, 0).start()
            gload(k, 1).start()

            @pl.when(k > 0)
            def _():
                unit_save(k - 1).wait()

            def one(j):
                gload(k, j).wait()
                hidden, grad = h2[k, j], gbuf[j]
                up_part = nt(hidden, up_v[...])
                pair_part = nt(hidden, pair_v[...])
                product = (up_part * pair_part).astype(BF)
                prod_s[j] = product
                res_s[spot(j)] = nn(product, down_v[...]).astype(BF)
                grad_product = nt(grad, down_v[...]).astype(BF).astype(F32)
                grad_up = (grad_product * pair_part).astype(BF)
                grad_pair = (grad_product * up_part).astype(BF)
                gu_s[j] = grad_up
                gp_s[j] = grad_pair
                part[k, spot(j)] = (nn(grad_up, up_v[...]) + nn(grad_pair, pair_v[...])).astype(BF)

            def block(j):
                @pl.when((j == 2) & (k == 1))
                def _():
                    finish_attend(2)
                    grads.chip_hop(2).start()

                @pl.when(j == 2)
                def _():
                    second.forward(k)
                    grads.forward(k)
                    gload(k, 2).start()

                @pl.when(j == 3)
                def _():
                    second.passed_on(k).wait_recv()
                    grads.passed_on(k).wait_recv()
                    gload(k, 3).start()

                one(j)

            loop(BLOCKS, block)
            unit_save(k).start()
            scatter_b.start(k)
            hidden_all = lambda: h2[k].reshape(BLOCKS * rows, feat)
            weigh(0, prod_s, lambda: gbuf[...].reshape(BLOCKS * rows, feat))

            @pl.when(k == 0)
            def _():
                finish_attend(1)

            @pl.when(k == 1)
            def _():
                scatter_b.middle_step(0)

            @pl.when(k > 0)
            def _():
                scatter_b.middle_step(k)

            @pl.when(k == slots - 1)
            def _():
                settle_sums(0)

            weigh(1, gu_s, hidden_all)

            @pl.when(k == slots - 1)
            def _():
                sums_save(0).wait()
                down_hop.start()
                settle_sums(1)

            weigh(2, gp_s, hidden_all)

        loop(slots, unit)
        sums_save(1).wait()
        settle_sums(2)
        sums_save(2).wait()
        unit_save(slots - 1).wait()

    pl.run_scoped(
        unit_all,
        v((BLOCKS, rows, wide), BF),
        v((BLOCKS, rows, wide), BF),
        v((BLOCKS, rows, wide), BF),
        v((BLOCKS, rows, feat), BF),
        v((BLOCKS, rows, feat), BF),
        v((3, wide, feat), F32),
        v((8, hid // 8, feat), BF),
    )
    middle_save = pltpu.make_async_copy(middle, middle_out, save_sem.at[5])
    middle_save.start()
    own_grads = load(cotangent, tok, 0)
    own_grads.start()
    own_grads.wait()
    gain_out[...] = jnp.zeros_like(gain_out)

    def finish_all(gmid):
        def gmid_save(k):
            return pltpu.make_async_copy(gmid.at[k], gmid_out.at[k], save_sem.at[10 + k])

        def finish_unit(k):
            scatter_b.arrived(k)

            def some(r):
                grad = (
                    part[k, 0, r].astype(F32) + came[k, 0, r].astype(F32) + far[k, r].astype(F32)
                )
                normed, scale, _ = normalize(middle[k, r], g2)
                gain_out[...] += jnp.sum(grad * normed, axis=0, keepdims=True)
                gmid[k, r] = tok[k, r].astype(F32) + norm_back(grad, normed, scale, g2)

            by_rows(rows, some)
            gmid_save(k).start()

        loop(slots, finish_unit)
        for k in range(slots):
            gmid_save(k).wait()

    pl.run_scoped(finish_all, v((slots, rows, feat), F32))
    for save in (h1_save, middle_save):
        save.wait()

    def settle(k):
        first.sent(k)
        second.sent(k)
        grads.sent(k)
        scatter_b.sent(k)

    loop(slots, settle)
    down_hop.wait()


def dma(n):
    return pltpu.SemaphoreType.DMA((n,))


def anywhere(n):
    return [pl.BlockSpec(memory_space=pl.ANY)] * n


def in_vmem(n):
    return [pl.BlockSpec(memory_space=pltpu.VMEM)] * n


def forward(batch, lengths, tokens, cotangent, q4, wo, up, pair, down, gain_one, gain_two, gain_head):
    slots, rows, feat = tokens.shape
    width, hid = wo.shape[0], down.shape[0]
    n = BLOCKS
    shape = jax.ShapeDtypeStruct
    wide = -(-hid // 256) * 256
    blocks = lambda *dims: shape((slots, n) + dims, BF)
    outs = [
        blocks(rows, feat),
        blocks(4, rows, width),
        blocks(rows, width),
        blocks(rows, width),
        blocks(width, width),
        blocks(rows, feat),
        blocks(rows, feat),
        shape((slots, rows, feat), F32),
        shape((slots, rows, feat), F32),
        shape((3, 8, hid // 8, feat), BF),
        shape((4, hid // 8, feat), BF),
        shape((1, feat), F32),
    ]
    v = pltpu.VMEM
    scratch = [
        v((slots, rows, feat), BF),
        v((4, feat, width), BF),
        v((width, feat), BF),
        v((wide, feat), BF),
        v((wide, feat), BF),
        v((wide, feat), BF),
        v((slots, n, rows, feat), BF),
        v((slots, n, rows, feat), BF),
        v((slots, n, rows, feat), BF),
        v((slots, 2, rows, feat), BF),
        v((slots, rows, feat), BF),
        v((slots, rows, feat), F32),
        v((width, width), F32),
        dma(10),
        dma(13),
        dma(n),
        *[dma(3 * slots)] * 6,
        *[dma(2 * slots)] * 4,
        *[dma(1)] * 2,
    ]
    total = slots * n * rows
    return pl.pallas_call(
        functools.partial(forward_kernel, batch),
        in_specs=[pl.BlockSpec(memory_space=pltpu.SMEM)] + anywhere(10) + in_vmem(3),
        out_specs=anywhere(11) + in_vmem(1),
        out_shape=outs,
        scratch_shapes=scratch,
        compiler_params=pltpu.CompilerParams(
            collective_id=1, has_side_effects=True, vmem_limit_bytes=VMEM_LIMIT
        ),
        cost_estimate=pl.CostEstimate(
            flops=total * (10 * feat * width + 16 * width * width + 18 * feat * hid),
            transcendentals=total * 6 * width,
            bytes_accessed=2 * total * (6 * feat + 3 * hid),
        ),
        name="forward",
    )(lengths, tokens, cotangent, *q4, wo, up, pair, down, gain_one, gain_two, gain_head)


def backward_kernel(
    batch,
    tokens, middle, gmid, res, qkvg_in, mixed_in, state_in, h1_in, gated_in, sums_in, down_came,
    wq, wk, wv, wg, wo, gain_one, gain_head, two_part,
    result, grad_tokens, unit_total, qk_total, vg_total, out_total, gains,
    w4, wo_v, gm, part, came, far, res_mid, came2, far2, state,
    unit_work, unit_came, qk_send, qk_work, qk_came, vg_send, vg_work, vg_came,
    out_send, out_work, out_came, gain_came, head_part,
    load_sem, slot_sem, save_sem, unit_sem, local_sem,
    gm_send, gm_recv, a_send, a_recv, r_send, r_recv, gain_send, gain_recv,
    d_send, d_recv, u_send, u_recv, p_send, p_recv, q_send, q_recv, v_send, v_recv, o_send, o_recv,
):
    slots, _, rows, feat = gm.shape
    width = wo_v.shape[0]
    heads = width // HD
    peers = Peers(batch)

    def load(source, target, index):
        return pltpu.make_async_copy(source, target, load_sem.at[index])

    weight_loads = [
        *(load(w, w4.at[m], 1 + m) for m, w in enumerate((wq, wk, wv, wg))),
        load(wo, wo_v, 5),
        load(res.at[:, 1], res_mid, 6),
    ]
    half = peers.bit(0)
    unit_loads = [
        pltpu.make_async_copy(sums_in.at[c, pl.ds(half * 4, 4)], unit_work.at[c], unit_sem.at[c])
        for c in range(3)
    ]
    early = pltpu.make_async_copy(down_came, unit_came.at[0, pl.ds(0, 4)], unit_sem.at[3])
    for one in (*weight_loads, *unit_loads, early):
        one.start()
    gather = Gather(peers, gm, (gm_send, gm_recv))
    scatter = Scatter(
        peers, lambda k: part.at[k, pl.ds(2, 2)], lambda k: part.at[k, 1], came, far, (a_send, a_recv)
    )
    results = Scatter(
        peers, lambda k: res.at[k, pl.ds(2, 2)], lambda k: res_mid.at[k], came2, far2, (r_send, r_recv)
    )
    unit_sums = [
        Reduce(
            peers, (0, 1, 2), sums_in.at[c, pl.ds((1 - half) * 4, 4)], unit_work.at[c],
            unit_came.at[c], unit_total.at[c], sems, local_sem.at[c], None if c else early,
        )
        for c, sems in enumerate(((d_send, d_recv), (u_send, u_recv), (p_send, p_recv)))
    ]
    down_sum, up_sum, pair_sum = unit_sums
    qk_sum = Reduce(
        peers, (1, 2, 0), qk_send, qk_work, qk_came, qk_total, (q_send, q_recv), local_sem.at[3]
    )
    vg_sum = Reduce(
        peers, (0, 1, 2), vg_send, vg_work, vg_came, vg_total, (v_send, v_recv), local_sem.at[4]
    )
    out_sum = Reduce(
        peers, (0, 1, 2), out_send, out_work, out_came, out_total, (o_send, o_recv), local_sem.at[5]
    )
    g1, gh = gain_one[...], gain_head[...]
    head_part[...] = jnp.zeros_like(head_part)
    gains[...] = jnp.zeros_like(gains)
    gains[1:2] = two_part[...]
    peers.meet()
    pair_sum.begin()
    up_sum.begin()
    v = pltpu.VMEM

    def begin_all(gmv):
        whole = load(gmid, gmv, 0)
        whole.start()
        whole.wait()

        def begin(k):
            def some(r):
                gm[k, 0, r] = gmv[k, r].astype(BF)

            by_rows(rows, some)
            gather.start(k)

        loop(slots, begin)

    pl.run_scoped(begin_all, v((slots, rows, feat), F32))
    loop(slots, results.start)
    for one in weight_loads:
        one.wait()
    for one in unit_loads:
        one.wait()
    down_sum.step(0)
    block = same_head(width)
    ones = block.astype(BF)

    def attend_all(qkvg, mixed_v, state_v, h1, gated, pre, sums, out_acc):
        def slot_loads(k):
            b = k % 2
            pairs = (
                (qkvg_in, qkvg), (mixed_in, mixed_v), (state_in, state_v), (h1_in, h1), (gated_in, gated)
            )
            return [
                pltpu.make_async_copy(source.at[k], target.at[b], slot_sem.at[5 * b + m])
                for m, (source, target) in enumerate(pairs)
            ]

        for one in slot_loads(0):
            one.start()

        plan = {
            (0, -1): ((down_sum, 1),),
            (0, 1): ((pair_sum, 0),),
            (0, 3): ((down_sum, 2),),
            (0, 4): ((pair_sum, 1),),
            (1, -1): ((up_sum, 0), (down_sum, 3)),
            (1, 2): ((pair_sum, 2),),
            (1, 3): ((up_sum, 1),),
            (1, 7): ((down_sum, 4),),
            (2, -1): ((pair_sum, 3),),
            (2, 2): ((up_sum, 2),),
        }

        def hooks(k, point):
            for (slot, where), actions in plan.items():
                if isinstance(point, int) and point != where:
                    continue

                @pl.when((k == slot) & (point == where))
                def _():
                    for one, stage in actions:
                        one.step(stage)

        def attend_back(k):
            b = k % 2
            hooks(k, -1)
            gather.forward(k)

            @pl.when(k > 0)
            def _():
                scatter.middle_step(k - 1)

            @pl.when(k + 1 < slots)
            def _():
                for one in slot_loads(k + 1):
                    one.start()

            for one in slot_loads(k):
                one.wait()
            gather.arrived(k)
            state[...] = jnp.zeros_like(state)

            def chunk(step):
                hooks(k, step)
                i = BLOCKS - 1 - step
                j = peers.relative(i)
                grad_gated = nt(gm[k, j], wo_v[...]).astype(BF).astype(F32)
                query, keys, values = qkvg[b, j, 0], qkvg[b, j, 1], qkvg[b, j, 2]
                gate = qkvg[b, j, 3].astype(F32)
                mixed = mixed_v[b, j].astype(F32)
                scale = lax.rsqrt(head_mean(mixed * mixed, ones) + EPS)
                normed = mixed * scale
                opened = sigmoid(gate)
                grad_gate = grad_gated * (normed * gh) * opened * (1.0 + gate * (1.0 - opened))
                grad_head = grad_gated * (gate * opened)
                head_part[...] += jnp.sum(grad_head * normed, axis=0, keepdims=True)
                scaled = grad_head * gh
                inner = head_mean(scaled * normed, ones)
                grad_mixed = (scale * (scaled - normed * inner)).astype(BF)
                after = state[...].astype(BF)
                before = state_v[b, i]
                lower = causal(rows, heads, False)
                upper = causal(rows, heads, True)
                query_heads = by_head(query)
                mixed_heads = by_head(grad_mixed)
                grad_scores = masked(nt(grad_mixed, by_head(values)), lower)
                grad_query = nt(grad_mixed, before) + nn(grad_scores, by_head(keys))
                grad_scores_t = masked(nt(values, mixed_heads), upper)
                grad_keys = nt(values, after) + nn(grad_scores_t, query_heads)
                scores_t = masked(nt(keys, query_heads), upper)
                grad_values = nn(keys, after) + nn(scores_t, mixed_heads)
                state[...] += jnp.where(block, tn(query, grad_mixed), 0.0)

                rounded = lambda v: v.astype(BF).astype(F32)
                pre_q = (rounded(grad_query) * sigmoid_of_softplus(query.astype(F32))).astype(BF)
                pre_k = (rounded(grad_keys) * sigmoid_of_softplus(keys.astype(F32))).astype(BF)
                pre_v = grad_values.astype(BF)
                pre_g = grad_gate.astype(BF)
                for m, one in enumerate((pre_q, pre_k, pre_v, pre_g)):
                    pre[j, :, m * width : (m + 1) * width] = one
                grad_h = nt(pre_q, w4[0]) + nt(pre_k, w4[1]) + nt(pre_v, w4[2]) + nt(pre_g, w4[3])
                part[k, spot(j)] = grad_h.astype(BF)

            loop(BLOCKS, chunk)
            scatter.start(k)
            results.middle_step(k)

            pre_all = pre[...].reshape(BLOCKS * rows, 4 * width)

            def weigh(m):
                hooks(k, BLOCKS + m)
                cols = pl.ds(pl.multiple_of(m * 256, 256), 256)
                term = tn(h1[b, :, :, cols].reshape(BLOCKS * rows, 256), pre_all)
                sums[cols] = jnp.where(k > 0, sums[cols], 0.0) + term

            loop(feat // 256, weigh)
            term = tn(gated[b].reshape(BLOCKS * rows, width), gm[k].reshape(BLOCKS * rows, feat))
            out_acc[...] = jnp.where(k > 0, out_acc[...], 0.0) + term

        loop(slots, attend_back)
        scatter.middle_step(slots - 1)
        eighth, part_rows = feat // 8, width // 8

        first = peers.bit(1)

        def fill_all(q):
            at = lambda top: pl.ds(pl.multiple_of((top * 4 + q) * eighth, eighth), eighth)
            qk_work[q] = sums[at(first), : 2 * width].astype(BF)
            qk_send[q] = sums[at(1 - first), : 2 * width].astype(BF)
            vg_work[q] = sums[at(half), 2 * width :].astype(BF)
            vg_send[q] = sums[at(1 - half), 2 * width :].astype(BF)
            small = lambda top: pl.ds(
                pl.multiple_of((top * 4 + q) * part_rows, part_rows), part_rows
            )
            out_work[q] = out_acc[small(half)].astype(BF)
            out_send[q] = out_acc[small(1 - half)].astype(BF)

        loop(4, fill_all)
        for one in (out_sum, vg_sum, qk_sum):
            one.begin()

    pl.run_scoped(
        attend_all,
        v((2, BLOCKS, 4, rows, width), BF),
        v((2, BLOCKS, rows, width), BF),
        v((2, BLOCKS, width, width), BF),
        v((2, BLOCKS, rows, feat), BF),
        v((2, BLOCKS, rows, width), BF),
        v((BLOCKS, rows, 4 * width), BF),
        v((feat, 4 * width), F32),
        v((width, feat), F32),
    )

    def finish_all(tok, mid, gmv, kept):
        finals = [
            load(tokens, tok, 1),
            load(middle, mid, 2),
            load(gmid, gmv, 3),
            load(res.at[:, 0], kept, 4),
        ]
        for one in finals:
            one.start()

        def grad_save(k):
            return pltpu.make_async_copy(gmv.at[k], grad_tokens.at[k], save_sem.at[k])

        def result_save(k):
            return pltpu.make_async_copy(kept.at[k], result.at[k], save_sem.at[slots + k])

        def finish(k):
            scatter.arrived(k)

            def some(r):
                grad = (
                    part[k, 0, r].astype(F32) + came[k, 0, r].astype(F32) + far[k, r].astype(F32)
                )
                normed, scale, _ = normalize(tok[k, r].astype(F32), g1)
                gains[0:1] += jnp.sum(grad * normed, axis=0, keepdims=True)
                gmv[k, r] = gmv[k, r] + norm_back(grad, normed, scale, g1)

            by_rows(rows, some)
            grad_save(k).start()

        def finish_result(k):
            results.arrived(k)

            def some(r):
                total = (
                    mid[k, r]
                    + kept[k, r].astype(F32)
                    + came2[k, 0, r].astype(F32)
                    + far2[k, r].astype(F32)
                )
                kept[k, r] = total.astype(BF)

            by_rows(rows, some)
            result_save(k).start()

        for one in finals:
            one.wait()
        others = [peers.beside, peers.across] + [peers.partner(h) for h in range(peers.hops)]

        def gain_hop(t):
            return remote(gains, gain_came.at[t], (gain_send, gain_recv), t, others[t])

        def gain_begin():
            lane = lax.broadcasted_iota(jnp.int32, (1, BLOCKS * width), 1) // width
            spread = jnp.concatenate([head_part[...]] * BLOCKS, axis=1)
            gains[2:3] = jnp.where(lane == peers.place, spread, 0.0)
            gain_hop(0).start()

        hop = iter(range(len(others)))

        def gain_step():
            t = next(hop, None)
            if t is None:
                return
            gain_hop(t).wait_recv()
            gain_hop(t).wait_send()
            gains[...] += gain_came[t]
            if t + 1 < len(others):
                gain_hop(t + 1).start()

        o, v, q = out_sum.step, vg_sum.step, qk_sum.step
        u, p = up_sum.step, pair_sum.step
        for one in (
            (finish, 0), (finish_result, 0), (finish_result, 1), (o,), (finish, 1), (q,), (p,), (o,),
            (v,), (finish_result, 2), (q,), (u,), (v,), (o,), (finish, 2), (gain_begin,), (q,),
            (gain_step,), (u,), (v,), (gain_step,), (o,), (q,), (gain_step,), (v,), (o,),
            (gain_step,), (v,), (gain_step,), (q,),
        ):
            one[0](*one[1:])
        for _ in others:
            gain_step()
        for one in (*unit_sums, qk_sum, vg_sum, out_sum):
            while one.stage < one.steps():
                one.step()
        for one in (*unit_sums, qk_sum, vg_sum, out_sum):
            one.sent()

        def settle(k):
            grad_save(k).wait()
            result_save(k).wait()
            gather.sent(k)
            scatter.sent(k)
            results.sent(k)

        loop(slots, settle)

    pl.run_scoped(
        finish_all,
        v((slots, rows, feat), BF),
        v((slots, rows, feat), F32),
        v((slots, rows, feat), F32),
        v((slots, rows, feat), BF),
    )


def backward(batch, tokens, middle, gmid, res, saved, sums, down_came, q4, wo, gain_one, gain_head, two_part):
    slots, rows, feat = tokens.shape
    width = wo.shape[0]
    eighth = sums.shape[2]
    n = BLOCKS
    shape = jax.ShapeDtypeStruct
    v = pltpu.VMEM
    outs = [
        shape((slots, rows, feat), BF),
        shape((slots, rows, feat), F32),
        shape(sums.shape, BF),
        shape((8, feat // 8, 2 * width), BF),
        shape((8, feat // 8, 2 * width), BF),
        shape((8, width // 8, feat), BF),
        shape((3, feat), F32),
    ]
    hops = batch.bit_length() - 1
    extra = hops - 3

    def pieces(*dims):
        return [v((4,) + dims, BF), v((4,) + dims, BF), v((7 + extra,) + dims, BF)]

    scratch = [
        v((4, feat, width), BF),
        v((width, feat), BF),
        v((slots, n, rows, feat), BF),
        v((slots, n, rows, feat), BF),
        v((slots, 2, rows, feat), BF),
        v((slots, rows, feat), BF),
        v((slots, rows, feat), BF),
        v((slots, 2, rows, feat), BF),
        v((slots, rows, feat), BF),
        v((width, width), F32),
        v((3, 4, eighth, feat), BF),
        v((3, 7 + extra, eighth, feat), BF),
        *pieces(feat // 8, 2 * width),
        *pieces(feat // 8, 2 * width),
        *pieces(width // 8, feat),
        v((hops + 2, 3, feat), F32),
        v((1, width), F32),
        dma(7),
        dma(10),
        dma(2 * slots),
        dma(4),
        dma(6),
        *[dma(3 * slots)] * 2,
        *[dma(2 * slots)] * 4,
        *[dma(hops + 2)] * 2,
        *[dma(6 + extra)] * 12,
    ]
    total = slots * n * rows
    return pl.pallas_call(
        functools.partial(backward_kernel, batch),
        in_specs=anywhere(16) + in_vmem(3),
        out_specs=anywhere(6) + in_vmem(1),
        out_shape=outs,
        scratch_shapes=scratch,
        compiler_params=pltpu.CompilerParams(
            collective_id=2, has_side_effects=True, vmem_limit_bytes=VMEM_LIMIT
        ),
        cost_estimate=pl.CostEstimate(
            flops=total * (20 * feat * width + 40 * width * width),
            transcendentals=total * 6 * width,
            bytes_accessed=2 * total * (6 * feat),
        ),
        name="backward",
    )(tokens, middle, gmid, res, *saved, sums, down_came, *q4, wo, gain_one, gain_head, two_part)


def widen_kernel(unit, qk, vg, out, *targets):
    width = qk.shape[2] // 2
    for c, at in enumerate((2, 0, 1)):
        targets[5 + at][...] = unit[c, 0].astype(F32)
    targets[0][...] = qk[0, :, :width].astype(F32)
    targets[1][...] = qk[0, :, width:].astype(F32)
    targets[2][...] = vg[0, :, :width].astype(F32)
    targets[3][...] = vg[0, :, width:].astype(F32)
    targets[4][...] = out[0].astype(F32)


def widen(unit, qk, vg, out):
    eighth, feat = unit.shape[2:]
    width = qk.shape[2] // 2
    block = lambda dims: pl.BlockSpec((1,) + dims, lambda i: (i, 0, 0))
    flat = lambda dims: pl.BlockSpec(dims, lambda i: (i, 0))
    whole = lambda rows, cols: jax.ShapeDtypeStruct((8 * rows, cols), F32)
    return pl.pallas_call(
        widen_kernel,
        grid=(8,),
        in_specs=[
            pl.BlockSpec((3, 1, eighth, feat), lambda i: (0, i, 0, 0)),
            block(qk.shape[1:]),
            block(vg.shape[1:]),
            block(out.shape[1:]),
        ],
        out_specs=[flat((feat // 8, width))] * 4
        + [flat((width // 8, feat))]
        + [flat((eighth, feat))] * 3,
        out_shape=[whole(feat // 8, width)] * 4 + [whole(width // 8, feat)] + [whole(eighth, feat)] * 3,
        compiler_params=pltpu.CompilerParams(vmem_limit_bytes=VMEM_LIMIT),
        name="widen",
    )(unit, qk, vg, out)


def on_device(
    batch,
    tokens,
    lengths,
    assignment,
    query_weight,
    key_weight,
    value_weight,
    gate_weight,
    out_weight,
    up_weight,
    pair_weight,
    down_weight,
    attention_norm_gain,
    mlp_gain,
    head_gain,
    cotangent,
):
    slots = tokens.shape[0]
    width = query_weight.shape[1]
    place = lax.axis_index("seq").astype(jnp.int32)
    seq_ids = lax.broadcasted_iota(jnp.int32, (slots, lengths.shape[0]), 1)
    slot_length = jnp.sum(jnp.where(assignment[:, None] == seq_ids, lengths[None, :], 0), axis=1)
    q4 = (query_weight, key_weight, value_weight, gate_weight)
    gain_one, gain_two, gain_head = attention_norm_gain[None], mlp_gain[None], head_gain[None]
    h_one, qkvg, mixed, gated, states, _, res, middle, gmid, sums, down_came, two_part = forward(
        batch, slot_length, tokens, cotangent, q4, out_weight, up_weight.T, pair_weight.T, down_weight,
        gain_one, gain_two, gain_head,
    )
    result, grad_inputs, unit_total, qk_total, vg_total, out_total, gains = backward(
        batch, tokens, middle, gmid, res, (qkvg, mixed, states, h_one, gated), sums, down_came, q4,
        out_weight,
        gain_one, gain_head, two_part,
    )
    grad_qw, grad_kw, grad_vw, grad_gw, grad_outw, grad_upw, grad_pairw, grad_down = widen(
        unit_total, qk_total, vg_total, out_total
    )
    head_total = lax.dynamic_slice(gains[2], (place * width,), (width,))
    return (
        result,
        grad_inputs,
        grad_qw,
        grad_kw,
        grad_vw,
        grad_gw,
        grad_outw,
        grad_upw.T,
        grad_pairw.T,
        grad_down,
        gains[0],
        gains[1],
        head_total,
    )


def solution(mesh):
    return jax.shard_map(
        functools.partial(on_device, mesh.shape["batch"]),
        mesh=mesh,
        in_specs=(
            P("batch", "seq", None),
            P(),
            P("batch"),
            P(None, "seq"),
            P(None, "seq"),
            P(None, "seq"),
            P(None, "seq"),
            P("seq", None),
            P(None, "seq"),
            P(None, "seq"),
            P("seq", None),
            P(),
            P(),
            P("seq"),
            P("batch", "seq", None),
        ),
        out_specs=(
            P("batch", "seq", None),
            P("batch", "seq", None),
            P(None, "seq"),
            P(None, "seq"),
            P(None, "seq"),
            P(None, "seq"),
            P("seq", None),
            P(None, "seq"),
            P(None, "seq"),
            P("seq", None),
            P(),
            P(),
            P("seq"),
        ),
        check_vma=False,
    )
```

```python
import functools

import jax
import jax.numpy as jnp
from jax import lax
from jax.experimental import pallas as pl
from jax.experimental.pallas import tpu as pltpu
from jax.sharding import PartitionSpec as P

HD = 64
EPS = 1e-05
BF = jnp.bfloat16
F32 = jnp.float32
VMEM_LIMIT = 62 * 1024 * 1024
MESH = pl.DeviceIdType.MESH
BLOCKS = 4


def nn(a, b):
    return lax.dot_general(a, b, (((1,), (0,)), ((), ())), preferred_element_type=F32)


def nt(a, b):
    return lax.dot_general(a, b, (((1,), (1,)), ((), ())), preferred_element_type=F32)


def tn(a, b):
    return lax.dot_general(a, b, (((0,), (0,)), ((), ())), preferred_element_type=F32)


def same_head(width):
    rows = lax.broadcasted_iota(jnp.int32, (width, width), 0) // HD
    cols = lax.broadcasted_iota(jnp.int32, (width, width), 1) // HD
    return rows == cols


def by_head(array):
    rows, width = array.shape
    lane = lax.broadcasted_iota(jnp.int32, (rows, width), 1) // HD
    zero = jnp.zeros_like(array)
    return jnp.concatenate([jnp.where(lane == h, array, zero) for h in range(width // HD)], axis=0)


def causal(rows, heads, transposed):
    one = lax.broadcasted_iota(jnp.int32, (rows, rows), 0)
    two = lax.broadcasted_iota(jnp.int32, (rows, rows), 1)
    keep = (two >= one) if transposed else (one >= two)
    return jnp.concatenate([keep] * heads, axis=1)


def masked(scores, keep):
    return jnp.where(keep, scores, 0.0).astype(BF)


def head_mean(array, ones):
    return nn(array.astype(BF), ones) * (1.0 / HD)


def softplus(v):
    return jnp.maximum(v, 0.0) + jnp.log1p(jnp.exp(-jnp.abs(v)))


def sigmoid_of_softplus(q):
    series = q * (1.0 - q * (0.5 - q * (1.0 / 6.0)))
    return jnp.where(q < 0.03, series, 1.0 - jnp.exp(-q))


def sigmoid(v):
    return 1.0 / (1.0 + jnp.exp(-v))


class Peers:
    def __init__(self, batch=1):
        self.place = lax.axis_index("seq")
        self.group = lax.axis_index("batch")
        self.chip, self.core = self.place // 2, self.place % 2
        self.across = (self.group, (1 - self.chip) * 2 + self.core)
        self.beside = (self.group, self.chip * 2 + 1 - self.core)
        self.hops = batch.bit_length() - 1

    def bit(self, h):
        return (self.group // 2**h) % 2

    def partner(self, h):
        return (self.group + (1 - 2 * self.bit(h)) * 2**h, self.place)

    def meet(self):
        others = [self.across, self.beside] + [self.partner(h) for h in range(self.hops)]
        barrier = pltpu.get_barrier_semaphore()
        for peer in others:
            pl.semaphore_signal(barrier, inc=1, device_id=peer, device_id_type=MESH)
        pl.semaphore_wait(barrier, len(others))

    def relative(self, index):
        return ((index // 2 + self.chip) % 2) * 2 + (index % 2 + self.core) % 2


def spot(j):
    return (j % 2) * 2 + j // 2


def remote(source, target, sems, index, peer):
    send, recv = sems
    return pltpu.make_async_remote_copy(
        src_ref=source,
        dst_ref=target,
        send_sem=send.at[index],
        recv_sem=recv.at[index],
        device_id=peer,
        device_id_type=MESH,
    )


class Gather:
    def __init__(self, peers, buffer, sems, own=None):
        self.peers, self.buffer, self.sems = peers, buffer, sems
        self.own = own or (lambda k: buffer.at[k, 0])

    def chip_hop(self, k):
        return remote(self.own(k), self.buffer.at[k, 2], self.sems, 3 * k, self.peers.across)

    def core_hop(self, k):
        return remote(self.own(k), self.buffer.at[k, 1], self.sems, 3 * k + 1, self.peers.beside)

    def passed_on(self, k):
        return remote(
            self.buffer.at[k, 2], self.buffer.at[k, 3], self.sems, 3 * k + 2, self.peers.beside
        )

    def start(self, k):
        self.chip_hop(k).start()
        self.core_hop(k).start()

    def forward(self, k):
        self.chip_hop(k).wait_recv()
        self.passed_on(k).start()

    def arrived(self, k):
        self.core_hop(k).wait_recv()
        self.passed_on(k).wait_recv()

    def sent(self, k):
        self.chip_hop(k).wait_send()
        self.core_hop(k).wait_send()
        self.passed_on(k).wait_send()


class Scatter:
    def __init__(self, peers, pair, middle, came, far, sems):
        self.peers, self.pair, self.middle = peers, pair, middle
        self.came, self.far, self.sems = came, far, sems

    def core_hop(self, k):
        return remote(self.pair(k), self.came.at[k], self.sems, 2 * k, self.peers.beside)

    def chip_hop(self, k):
        return remote(self.middle(k), self.far.at[k], self.sems, 2 * k + 1, self.peers.across)

    def start(self, k):
        self.core_hop(k).start()

    def middle_step(self, k):
        self.core_hop(k).wait_recv()
        middle = self.middle(k)

        def add(rows):
            middle[rows] = (middle[rows].astype(F32) + self.came[k, 1, rows].astype(F32)).astype(BF)

        by_rows(middle.shape[0], add)
        self.chip_hop(k).start()

    def arrived(self, k):
        self.chip_hop(k).wait_recv()

    def sent(self, k):
        self.core_hop(k).wait_send()
        self.chip_hop(k).wait_send()


class Chain:
    def __init__(self, peers, bits, work, came, room, total, sems, load, source=None, far=None, across=None):
        self.peers, self.sems, self.stages, self.waited = peers, sems, [], set()
        b0, b1, b2 = (peers.bit(h) for h in bits)
        pair = 2 if across == "last" else 1
        start = 0 if pair == 2 else b0 * 4
        kept = (start + b1 * 2 + b2) * pair
        self.kept = kept
        piece = b0 * 4 + b1 * 2 + b2

        def fetch(ref):
            copy = pltpu.make_async_copy(ref, room.at[pl.ds(0, ref.shape[0])], load)
            copy.start()
            copy.wait()

        def add(at, base, count):
            def finish():
                fetch(came.at[pl.ds(at, count)])

                def one(q):
                    work[base + q] = (work[base + q].astype(F32) + room[q].astype(F32)).astype(BF)

                loop(count, one)

            return finish

        def spread():
            fetch(far)

            def one(q):
                work[q] = (work[q].astype(F32) + room[q].astype(F32)).astype(BF)

            loop(8, one)

        def meet():
            fetch(far.at[pl.ds(0, 1)])
            work[kept] = (work[kept].astype(F32) + room[0].astype(F32)).astype(BF)

        def other(base, bit, count):
            return work.at[pl.ds((base + (1 - bit) * count) * pair, count * pair)]

        if across == "first":
            self.stages.append((source.at[pl.ds(8, 8)], far, peers.across, spread))
        first = source.at[pl.ds((1 - b0) * 8, 8)] if pair == 2 else other(0, b0, 4)
        at = 0
        for bit, base, count, h in (
            (b0, start, 4, bits[0]), (b1, start, 2, bits[1]), (b2, start + b1 * 2, 1, bits[2])
        ):
            here = base + (bit * count if count < 4 else 0)
            ref = first if count == 4 else other(base, bit, count)
            self.stages.append(
                (ref, came.at[pl.ds(at, count * pair)], peers.partner(h), add(at, here * pair, count * pair))
            )
            at += count * pair
        for h in range(peers.hops):
            if h not in bits:
                ref = work.at[pl.ds(kept, pair)]
                self.stages.append((ref, came.at[pl.ds(at, pair)], peers.partner(h), add(at, kept, pair)))
                self.waited.add(len(self.stages) - 1)
                at += pair
        if across == "last":
            self.stages.append((work.at[pl.ds(kept + 1, 1)], far.at[pl.ds(0, 1)], peers.across, meet))
        self.local = lambda: pltpu.make_async_copy(
            work.at[pl.ds(kept, 1)], total.at[pl.ds(piece, 1)], load
        )
        for where, h in (
            (pl.ds(piece, 1), bits[2]),
            (pl.ds(b0 * 4 + b1 * 2, 2), bits[1]),
            (pl.ds(b0 * 4, 4), bits[0]),
        ):
            ref = work.at[pl.ds(kept, 1)] if h == bits[2] else total.at[where]
            self.stages.append((ref, total.at[where], peers.partner(h), lambda: None))
        self.count = len(self.stages)

    def hop(self, t):
        source, target, peer, _ = self.stages[t]
        return remote(source, target, self.sems, t, peer)

    def begin(self):
        self.hop(0).start()

    def step(self, t):
        self.hop(t).wait_recv()
        if t in self.waited:
            self.hop(t).wait_send()
        self.stages[t][3]()
        if t == self.count - 4:
            own = self.local()
            own.start()
            own.wait()
        if t + 1 < self.count:
            self.hop(t + 1).start()

    def sent(self):
        for t in range(self.count):
            if t not in self.waited:
                self.hop(t).wait_send()


def by_rows(rows, fn, step=64):
    def one(r, carry):
        fn(pl.ds(pl.multiple_of(r * step, step), step))
        return carry

    lax.fori_loop(0, rows // step, one, 0)


def loop(count, fn):
    def one(k, carry):
        fn(k)
        return carry

    lax.fori_loop(0, count, one, 0)


def normalize(values, gain):
    scale = lax.rsqrt(jnp.mean(values * values, axis=-1, keepdims=True) + EPS)
    normed = values * scale
    return normed, scale, (normed * gain).astype(BF)


def norm_back(grad_out, normed, scale, gain):
    grad_normed = grad_out * gain
    inner = jnp.mean(grad_normed * normed, axis=-1, keepdims=True)
    return scale * (grad_normed - normed * inner)


def block_kernel(
    batch,
    length_ref, tokens, cotangent, wq, wk, wv, wg, wo, up, pair, down, gain_one, gain_two, gain_head,
    result, grad_tokens, unit_total, qk_total, vg_total, out_total, gains,
    qkvg_hbm, mixed_hbm, gated_hbm, state_hbm, gm, other, sums, unit_came, unit_far, qk_came, vg_came,
    out_came,
    tok, w4, wo_v, h1, h2, g, part, came, far, middle, state, gain_came, head_part,
    load_sem, save_sem, slot_sem, mat_sem, chain_sem,
    h1_send, h1_recv, gm_send, gm_recv, h2_send, h2_recv, g_send, g_recv, w_send, w_recv,
    a_send, a_recv, b_send, b_recv, c_send, c_recv, gain_send, gain_recv,
    d_send, d_recv, u_send, u_recv, p_send, p_recv,
    d2_send, d2_recv, u2_send, u2_recv, p2_send, p2_recv, q_send, q_recv, v_send, v_recv, o_send, o_recv,
):
    slots, rows, feat = tok.shape
    width, hid = wo_v.shape[0], down.shape[0]
    heads, eighth = width // HD, feat // 8
    both = 2 * hid
    peers = Peers(batch)
    v = pltpu.VMEM

    def load(source, target, index):
        return pltpu.make_async_copy(source, target, load_sem.at[index])

    loads = [
        load(tokens, tok, 0),
        *(load(w, w4.at[m], 1 + m) for m, w in enumerate((wq, wk, wv, wg))),
        load(wo, wo_v, 5),
        load(cotangent, g.at[:, 0], 6),
    ]
    for one in loads:
        one.start()
    peers.meet()

    mats = (up, pair, down)
    b0, b1, b2 = (peers.bit(h) for h in range(3))

    def columns(first, count):
        return pl.ds(pl.multiple_of(first * eighth, eighth), count * eighth)

    def weight_hop(t, c):
        mine = other.at[c]
        cols = (
            columns(b0 * 4 + b1 * 2 + b2, 1), columns(b0 * 4 + b1 * 2 + b2, 1),
            columns(b0 * 4 + b1 * 2, 2), columns(b0 * 4, 4),
        )[t]
        source = (mats[c] if t == 0 else mine).at[:, cols]
        peer = peers.across if t == 0 else peers.partner(3 - t)
        return remote(source, mine.at[:, cols], (w_send, w_recv), 4 * c + t, peer)

    def weight_step(t, c):
        weight_hop(t - 1, c).wait_recv()
        if t < 4:
            weight_hop(t, c).start()

    for c in range(3):
        weight_hop(0, c).start()
    first = Gather(peers, h1, (h1_send, h1_recv))
    third = Gather(peers, gm, (gm_send, gm_recv), lambda k: tok.at[k])

    def pass_h2(k):
        return remote(h2.at[k, 0], h2.at[k, 1], (h2_send, h2_recv), k, peers.beside)

    def pass_g(k):
        return remote(cotangent.at[k], g.at[k, 1], (g_send, g_recv), k, peers.beside)

    buffers = (lambda k: part.at[k, pl.ds(2, 2)], lambda k: part.at[k, 1], came, far)
    scatter_a = Scatter(peers, *buffers, (a_send, a_recv))
    scatter_c = Scatter(peers, *buffers, (c_send, c_recv))

    def pass_grad(k):
        return remote(part.at[k, 1], came.at[k, 0], (b_send, b_recv), 2 * k, peers.beside)

    def pass_result(k):
        return remote(part.at[k, 3], came.at[k, 1], (b_send, b_recv), 2 * k + 1, peers.beside)

    g1, g2, gh = gain_one[...], gain_two[...], gain_head[...]
    gains[...] = jnp.zeros_like(gains)
    head_part[...] = jnp.zeros_like(head_part)
    loads[0].wait()

    def norm_first(k):
        def some(r):
            _, _, hidden = normalize(tok[k, r].astype(F32), g1)
            h1[k, 0, r] = hidden

        by_rows(rows, some)
        first.start(k)

    loop(slots, norm_first)
    loop(slots, lambda k: pass_g(k).start())
    for t, c in ((1, 0), (1, 1), (1, 2), (2, 0), (2, 1), (3, 0)):
        weight_step(t, c)
    for one in loads[1:6]:
        one.wait()

    same = same_head(width)
    ones = same.astype(BF)

    def attend_all(qkvg, mixed_s, gated_s, state_s):
        def saves(k):
            return [
                pltpu.make_async_copy(qkvg, qkvg_hbm.at[k], save_sem.at[0]),
                pltpu.make_async_copy(mixed_s, mixed_hbm.at[k], save_sem.at[1]),
                pltpu.make_async_copy(gated_s, gated_hbm.at[k], save_sem.at[2]),
                pltpu.make_async_copy(state_s, state_hbm.at[k], save_sem.at[3]),
            ]

        def attend(k):
            first.forward(k)

            @pl.when(k > 0)
            def _():
                scatter_a.middle_step(k - 1)
                for one in saves(k - 1):
                    one.wait()

            @pl.when(k == 1)
            def _():
                weight_step(2, 2)
                weight_step(3, 1)

            @pl.when(k == 2)
            def _():
                weight_step(3, 2)

            first.arrived(k)
            state[...] = jnp.zeros_like(state)
            length = length_ref[k]

            def chunk(i):
                j = peers.relative(i)
                hidden = h1[k, j]
                position = lax.broadcasted_iota(jnp.int32, (rows, width), 0) + i * rows
                query = softplus(nn(hidden, w4[0])).astype(BF)
                keys = jnp.where(position < length, softplus(nn(hidden, w4[1])), 0.0).astype(BF)
                values = nn(hidden, w4[2]).astype(BF)
                gate = nn(hidden, w4[3])
                qkvg[j, 0] = query
                qkvg[j, 1] = keys
                qkvg[j, 2] = values
                qkvg[j, 3] = gate.astype(BF)
                before = state[...].astype(BF)
                state_s[i] = before
                scores = masked(nt(query, by_head(keys)), causal(rows, heads, False))
                mixed = nn(query, before) + nn(scores, by_head(values))
                state[...] += jnp.where(same, tn(keys, values), 0.0)
                mixed_s[j] = mixed.astype(BF)
                scale = lax.rsqrt(head_mean(mixed * mixed, ones) + EPS)
                gated_s[j] = (mixed * scale * gh * (gate * sigmoid(gate))).astype(BF)

            loop(BLOCKS, chunk)
            for one in saves(k):
                one.start()

            def project(p):
                j = (p % 2) * 2 + p // 2
                part[k, p] = nn(gated_s[j], wo_v[...]).astype(BF)

            project(2)
            project(3)
            scatter_a.start(k)
            project(1)
            project(0)

        loop(slots, attend)
        for one in saves(slots - 1):
            one.wait()

    pl.run_scoped(
        attend_all,
        v((BLOCKS, 4, rows, width), BF),
        v((BLOCKS, rows, width), BF),
        v((BLOCKS, rows, width), BF),
        v((BLOCKS, width, width), BF),
    )
    scatter_a.middle_step(slots - 1)

    def finish_attend(k):
        scatter_a.arrived(k)

        def some(r):
            value = (
                tok[k, r].astype(F32)
                + part[k, 0, r].astype(F32)
                + came[k, 0, r].astype(F32)
                + far[k, r].astype(F32)
            )
            middle[k, r] = value
            _, _, hidden = normalize(value, g2)
            h2[k, 0, r] = hidden

        by_rows(rows, some)
        pass_h2(k).start()
        scatter_a.sent(k)

    finish_attend(0)
    finish_attend(1)
    loads[6].wait()

    def result_save(k):
        return pltpu.make_async_copy(part.at[k, 2], result.at[k], save_sem.at[4 + k])

    def unit_all(mat, prod_s, gu_s, gp_s, staged):
        def mat_load(c, which):
            source = mats[c] if which == 0 else other.at[c]
            return pltpu.make_async_copy(
                source, mat.at[c, pl.ds(which * hid, hid)], mat_sem.at[2 * c + which]
            )

        for c in range(3):
            mat_load(c, 0).start()
        for c in range(3):
            weight_step(4, c)
            mat_load(c, 1).start()
        for c in range(3):
            mat_load(c, 0).wait()
            mat_load(c, 1).wait()

        def unit(k):
            pass_h2(k).wait_recv()
            pass_g(k).wait_recv()

            def one(t):
                j = 1 - t
                hidden, grad = h2[k, j], g[k, j]
                up_part = nt(hidden, mat[0])
                pair_part = nt(hidden, mat[1])
                product = (up_part * pair_part).astype(BF)
                prod_s[k, j] = product
                part[k, 2 + j] = nn(product, mat[2]).astype(BF)
                grad_product = nt(grad, mat[2]).astype(BF).astype(F32)
                grad_up = (grad_product * pair_part).astype(BF)
                grad_pair = (grad_product * up_part).astype(BF)
                gu_s[k, j] = grad_up
                gp_s[k, j] = grad_pair
                part[k, j] = (nn(grad_up, mat[0]) + nn(grad_pair, mat[1])).astype(BF)

                @pl.when(t == 0)
                def _():
                    pass_grad(k).start()
                    pass_result(k).start()

            loop(2, one)

            @pl.when(k == 0)
            def _():
                for m in range(2, slots):
                    finish_attend(m)

            pass_grad(k).wait_recv()
            pass_result(k).wait_recv()

            def some(r):
                value = middle[k, r]
                total = value + part[k, 2, r].astype(F32) + came[k, 1, r].astype(F32)
                part[k, 2, r] = total.astype(BF)
                grad = part[k, 0, r].astype(F32) + came[k, 0, r].astype(F32)
                normed, scale, _ = normalize(value, g2)
                gains[1:2] += jnp.sum(grad * normed, axis=0, keepdims=True)
                back = g[k, 0, r].astype(F32) + norm_back(grad, normed, scale, g2)
                middle[k, r] = back
                tok[k, r] = back.astype(BF)

            by_rows(rows, some)
            third.start(k)
            pltpu.make_async_copy(tok.at[k], gm.at[k, 0], save_sem.at[4 + slots + k]).start()
            result_save(k).start()

        loop(slots, unit)
        tile = 256
        everything = slots * 2 * rows

        def weigh(c, left, right):
            for start in range(0, both, tile):
                span = min(tile, both - start)
                term = tn(
                    left[:, :, :, start : start + span].reshape(everything, span),
                    right[...].reshape(everything, feat),
                ).astype(BF)
                for q in range(2):
                    for m in range(2):
                        base = q * hid + m * (hid // 2)
                        low, high = max(start, base), min(start + span, base + hid // 2)
                        if low >= high:
                            continue
                        for p in range(8):
                            index = q * 8 + p if KINDS["UPD"[c] if m == 0 else "upd"[c]][0] == "first" else p * 2 + q
                            staged[index, low - q * hid : high - q * hid] = term[
                                low - start : high - start, p * eighth : (p + 1) * eighth
                            ]
            save = pltpu.make_async_copy(staged, sums.at[c], save_sem.at[3])
            save.start()
            save.wait()
            for m in range(2):
                begin_unit(c, m)

        turn = iter(range(slots))
        for c in UNIT_ORDER:
            weigh(c, (gu_s, gp_s, prod_s)[c], (h2, h2, g)[c])
            third.forward(next(turn))
        for k in turn:
            third.forward(k)

    half = pl.ds(0, hid // 2), pl.ds(hid // 2, hid // 2)
    unit_sems = (
        ((u_send, u_recv), (p_send, p_recv), (d_send, d_recv)),
        ((u2_send, u2_recv), (p2_send, p2_recv), (d2_send, d2_recv)),
    )

    def unit_chain(c, m, work, room):
        across, bits = KINDS[("UPD", "upd")[m][c]]
        return Chain(
            peers, bits, work, unit_came.at[c, :, half[m]], room, unit_total.at[c, :, half[m]],
            unit_sems[m][c], chain_sem.at[0], sums.at[c, :, half[m]], unit_far.at[c, :, half[m]], across,
        )

    def begin_unit(c, m):
        unit_chain(c, m, h2.at[0], None).begin()

    pl.run_scoped(
        unit_all,
        v((3, both, feat), BF),
        v((slots, 2, rows, both), BF),
        v((slots, 2, rows, both), BF),
        v((slots, 2, rows, both), BF),
        v((16, hid, eighth), BF),
    )

    def rest(works, room, qk_work, vg_work, out_work, pair_room, small_room):
        chains = {}
        work_loads = []
        for m in range(2):
            for c in range(3):
                name = ("UPD", "upd")[m][c]
                work = works.at[c, :, half[m]]
                chains[name] = unit_chain(c, m, work, room)
                first_half = 0 if KINDS[name][0] == "first" else peers.bit(KINDS[name][1][0]) * 8
                work_loads.append(
                    pltpu.make_async_copy(
                        sums.at[c, pl.ds(first_half, 8), half[m]], work, mat_sem.at[3 * m + c]
                    )
                )
        for name, work, come, space, total, pair_sems in (
            ("Q", qk_work, qk_came, pair_room, qk_total, (q_send, q_recv)),
            ("V", vg_work, vg_came, pair_room, vg_total, (v_send, v_recv)),
            ("O", out_work, out_came, small_room, out_total, (o_send, o_recv)),
        ):
            chains[name] = Chain(
                peers, KINDS[name][1], work, come, space, total, pair_sems, chain_sem.at[0]
            )
        for one in work_loads:
            one.start()
        for one in work_loads:
            one.wait()
        done = {name: 0 for name in chains}
        plan, tail, where = {}, [], (0, -1)
        for name, at in SCHEDULE:
            if name == "c":
                where = (at // 10, at % 10 + 1)
            elif name == "g":
                where = (at, 0)
            elif name == "T":
                where = None
            elif name in chains and where is None or name in ("F", "B", "A"):
                tail.append((name, at))
            elif name in chains:
                slot, point = where
                if point == 8 and slot + 1 < slots:
                    slot, point = slot + 1, -1
                plan.setdefault((slot, point), []).append((name, at))

        def play(actions):
            for name, stage in actions:
                chains[name].step(stage)
                done[name] = max(done[name], stage + 1)

        def attend_all_back(qkvg, mixed_v, state_v, gated, gm_v, pre, acc, out_acc):
            def slot_loads(k):
                b = k % 2
                pairs = (
                    (qkvg_hbm, qkvg), (mixed_hbm, mixed_v), (state_hbm, state_v), (gated_hbm, gated)
                )
                return [
                    pltpu.make_async_copy(source.at[k], target.at[b], slot_sem.at[4 * b + m])
                    for m, (source, target) in enumerate(pairs)
                ]

            for one in slot_loads(0):
                one.start()

            def hooks(k, point, low, high):
                for (slot, at), actions in plan.items():
                    if not low <= at < high:
                        continue

                    @pl.when((k == slot) & (point == at))
                    def _():
                        play(actions)

            def attend_back(k):
                b = k % 2
                hooks(k, -1, -1, 0)
                hooks(k, 0, 0, 1)
                third.arrived(k)
                pltpu.make_async_copy(tok.at[k], gm.at[k, 0], save_sem.at[4 + slots + k]).wait()
                fetch = pltpu.make_async_copy(gm.at[k], gm_v, slot_sem.at[8])
                fetch.start()

                @pl.when(k > 0)
                def _():
                    scatter_c.middle_step(k - 1)

                @pl.when(k + 1 < slots)
                def _():
                    for one in slot_loads(k + 1):
                        one.start()

                for one in slot_loads(k):
                    one.wait()
                result_save(k).wait()
                pass_grad(k).wait_send()
                pass_result(k).wait_send()
                state[...] = jnp.zeros_like(state)
                fetch.wait()

                def chunk(step):
                    hooks(k, step, 1, BLOCKS)
                    i = BLOCKS - 1 - step
                    j = peers.relative(i)
                    grad_gated = nt(gm_v[j], wo_v[...]).astype(BF).astype(F32)
                    query, keys, values = qkvg[b, j, 0], qkvg[b, j, 1], qkvg[b, j, 2]
                    gate = qkvg[b, j, 3].astype(F32)
                    mixed = mixed_v[b, j].astype(F32)
                    scale = lax.rsqrt(head_mean(mixed * mixed, ones) + EPS)
                    normed = mixed * scale
                    opened = sigmoid(gate)
                    grad_gate = grad_gated * (normed * gh) * opened * (1.0 + gate * (1.0 - opened))
                    grad_head = grad_gated * (gate * opened)
                    head_part[...] += jnp.sum(grad_head * normed, axis=0, keepdims=True)
                    scaled = grad_head * gh
                    inner = head_mean(scaled * normed, ones)
                    grad_mixed = (scale * (scaled - normed * inner)).astype(BF)
                    after = state[...].astype(BF)
                    before = state_v[b, i]
                    lower = causal(rows, heads, False)
                    upper = causal(rows, heads, True)
                    query_heads = by_head(query)
                    mixed_heads = by_head(grad_mixed)
                    grad_scores = masked(nt(grad_mixed, by_head(values)), lower)
                    grad_query = nt(grad_mixed, before) + nn(grad_scores, by_head(keys))
                    grad_scores_t = masked(nt(values, mixed_heads), upper)
                    grad_keys = nt(values, after) + nn(grad_scores_t, query_heads)
                    scores_t = masked(nt(keys, query_heads), upper)
                    grad_values = nn(keys, after) + nn(scores_t, mixed_heads)
                    state[...] += jnp.where(same, tn(query, grad_mixed), 0.0)

                    rounded = lambda x: x.astype(BF).astype(F32)
                    pre_q = (rounded(grad_query) * sigmoid_of_softplus(query.astype(F32))).astype(BF)
                    pre_k = (rounded(grad_keys) * sigmoid_of_softplus(keys.astype(F32))).astype(BF)
                    pre_v = grad_values.astype(BF)
                    pre_g = grad_gate.astype(BF)
                    for m, one in enumerate((pre_q, pre_k, pre_v, pre_g)):
                        pre[j, :, m * width : (m + 1) * width] = one
                    grad_h = (
                        nt(pre_q, w4[0]) + nt(pre_k, w4[1]) + nt(pre_v, w4[2]) + nt(pre_g, w4[3])
                    )
                    part[k, spot(j)] = grad_h.astype(BF)

                loop(BLOCKS, chunk)
                scatter_c.start(k)
                pre_all = pre[...].reshape(BLOCKS * rows, 4 * width)

                def weigh(m):
                    hooks(k, BLOCKS + m, BLOCKS, 8)
                    cols = pl.ds(pl.multiple_of(m * 256, 256), 256)
                    term = tn(h1[k, :, :, cols].reshape(BLOCKS * rows, 256), pre_all)
                    acc[cols] = jnp.where(k > 0, acc[cols], 0.0) + term

                loop(feat // 256, weigh)
                term = tn(gated[b].reshape(BLOCKS * rows, width), gm_v[...].reshape(BLOCKS * rows, feat))
                out_acc[...] = jnp.where(k > 0, out_acc[...], 0.0) + term

            loop(slots, attend_back)
            play(plan.get((slots - 1, 8), ()))
            scatter_c.middle_step(slots - 1)
            part_rows = width // 8

            def fill(p):
                at = pl.ds(pl.multiple_of(p * eighth, eighth), eighth)
                small = pl.ds(pl.multiple_of(p * part_rows, part_rows), part_rows)
                qk_work[p] = acc[at, : 2 * width].astype(BF)
                vg_work[p] = acc[at, 2 * width :].astype(BF)
                out_work[p] = out_acc[small].astype(BF)

            loop(8, fill)
            for name in ATTENTION_ORDER:
                chains[name].begin()

        pl.run_scoped(
            attend_all_back,
            v((2, BLOCKS, 4, rows, width), BF),
            v((2, BLOCKS, rows, width), BF),
            v((2, BLOCKS, width, width), BF),
            v((2, BLOCKS, rows, width), BF),
            v((BLOCKS, rows, feat), BF),
            v((BLOCKS, rows, 4 * width), BF),
            v((feat, 4 * width), F32),
            v((width, feat), F32),
        )
        loop(slots, lambda k: third.sent(k))
        again = load(tokens, tok, 0)
        again.start()

        def grad_save(k):
            return pltpu.make_async_copy(middle.at[k], grad_tokens.at[k], save_sem.at[4 + k])

        def finish(k):
            scatter_c.arrived(k)

            def some(r):
                grad = (
                    part[k, 0, r].astype(F32) + came[k, 0, r].astype(F32) + far[k, r].astype(F32)
                )
                normed, scale, _ = normalize(tok[k, r].astype(F32), g1)
                gains[0:1] += jnp.sum(grad * normed, axis=0, keepdims=True)
                middle[k, r] = middle[k, r] + norm_back(grad, normed, scale, g1)

            by_rows(rows, some)
            grad_save(k).start()

        others = [peers.beside, peers.across] + [peers.partner(h) for h in range(peers.hops)]

        def gain_hop(t):
            return remote(gains, gain_came.at[t], (gain_send, gain_recv), t, others[t])

        def gain_begin():
            lane = lax.broadcasted_iota(jnp.int32, (1, BLOCKS * width), 1) // width
            spread = jnp.concatenate([head_part[...]] * BLOCKS, axis=1)
            gains[2:3] = jnp.where(lane == peers.place, spread, 0.0)
            gain_hop(0).start()

        hop = iter(range(len(others)))

        def gain_step():
            t = next(hop, None)
            if t is None:
                return
            gain_hop(t).wait_recv()
            gain_hop(t).wait_send()
            gains[...] += gain_came[t]
            if t + 1 < len(others):
                gain_hop(t + 1).start()

        again.wait()
        turn = iter(range(slots))
        for name, stage in tail:
            if name == "F":
                finish(next(turn))
            elif name == "B":
                for k in turn:
                    finish(k)
                gain_begin()
            elif name == "A":
                gain_step()
            else:
                play([(name, stage)])
        for _ in others:
            gain_step()
        most = max(one.count for one in chains.values())
        for t in range(most):
            for name in chains:
                if done[name] <= t < chains[name].count:
                    play([(name, t)])
        for one in chains.values():
            one.sent()

        def settle(k):
            grad_save(k).wait()
            first.sent(k)
            scatter_c.sent(k)
            pass_h2(k).wait_send()
            pass_g(k).wait_send()

        loop(slots, settle)

        def settle_weights(c):
            for t in range(4):
                weight_hop(t, c).wait_send()

        for c in range(3):
            settle_weights(c)

    pl.run_scoped(
        rest,
        v((3, 8, hid, eighth), BF),
        v((8, hid // 2, eighth), BF),
        v((8, eighth, 2 * width), BF),
        v((8, eighth, 2 * width), BF),
        v((8, width // 8, feat), BF),
        v((4, eighth, 2 * width), BF),
        v((4, width // 8, feat), BF),
    )


def dma(n):
    return pltpu.SemaphoreType.DMA((n,))


def anywhere(n):
    return [pl.BlockSpec(memory_space=pl.ANY)] * n


def in_vmem(n):
    return [pl.BlockSpec(memory_space=pltpu.VMEM)] * n


KINDS = {
    "U": ("first", (0, 1, 2)),
    "P": ("last", (0, 1, 2)),
    "D": ("first", (0, 1, 2)),
    "u": ("last", (1, 0, 2)),
    "p": ("last", (0, 1, 2)),
    "d": ("first", (0, 1, 2)),
    "Q": (None, (0, 1, 2)),
    "V": (None, (1, 0, 2)),
    "O": (None, (0, 1, 2)),
}
UNIT_ORDER = (1, 0, 2)
ATTENTION_ORDER = ('O', 'V', 'Q')
SCHEDULE = (
    ("P", 0), ("g", 0), ("c", 0), ("U", 0), ("u", 0), ("c", 1), ("p", 0), ("P", 1), ("c", 2), ("c", 3),
    ("c", 4), ("U", 1), ("D", 0), ("p", 1), ("c", 5), ("c", 6), ("P", 2), ("c", 7), ("u", 1), ("g", 1),
    ("U", 2), ("c", 10), ("p", 2), ("D", 1), ("c", 11), ("d", 0), ("P", 3), ("u", 2), ("c", 12), ("U", 3),
    ("D", 2), ("c", 13), ("P", 4), ("c", 14), ("d", 1), ("c", 15), ("p", 3), ("U", 4), ("c", 16), ("P", 5),
    ("u", 3), ("c", 17), ("D", 3), ("g", 2), ("p", 4), ("d", 2), ("c", 20), ("c", 21), ("U", 5), ("c", 22),
    ("D", 4), ("c", 23), ("c", 24), ("p", 5), ("c", 25), ("d", 3), ("c", 26), ("c", 27), ("T", 0), ("F", 0),
    ("F", 1), ("O", 0), ("d", 4), ("F", 2), ("B", 0), ("V", 0), ("u", 4), ("D", 5), ("A", 0), ("O", 1),
    ("A", 0), ("A", 0), ("Q", 0), ("A", 0), ("O", 2), ("A", 0), ("V", 1), ("Q", 1), ("d", 5), ("O", 3),
    ("V", 2), ("O", 4), ("Q", 2), ("u", 5), ("V", 3), ("Q", 3), ("V", 4), ("Q", 4),
)


def block(batch, lengths, tokens, cotangent, q4, wo, up, pair, down, gain_one, gain_two, gain_head):
    slots, rows, feat = tokens.shape
    width, hid = wo.shape[0], down.shape[0]
    eighth = feat // 8
    n = BLOCKS
    hops = batch.bit_length() - 1
    extra = hops - 3
    shape = jax.ShapeDtypeStruct
    blocks = lambda *dims: shape((slots, n) + dims, BF)
    outs = [
        shape((slots, rows, feat), BF),
        shape((slots, rows, feat), F32),
        shape((3, 8, hid, eighth), BF),
        shape((8, eighth, 2 * width), BF),
        shape((8, eighth, 2 * width), BF),
        shape((8, width // 8, feat), BF),
        shape((3, feat), F32),
        blocks(4, rows, width),
        blocks(rows, width),
        blocks(rows, width),
        blocks(width, width),
        blocks(rows, feat),
        shape((3, hid, feat), BF),
        shape((3, 16, hid, eighth), BF),
        shape((3, 14 + 2 * extra, hid, eighth), BF),
        shape((3, 8, hid, eighth), BF),
        shape((7 + extra, eighth, 2 * width), BF),
        shape((7 + extra, eighth, 2 * width), BF),
        shape((7 + extra, width // 8, feat), BF),
    ]
    v = pltpu.VMEM
    scratch = [
        v((slots, rows, feat), BF),
        v((4, feat, width), BF),
        v((width, feat), BF),
        v((slots, n, rows, feat), BF),
        v((slots, 2, rows, feat), BF),
        v((slots, 2, rows, feat), BF),
        v((slots, n, rows, feat), BF),
        v((slots, 2, rows, feat), BF),
        v((slots, rows, feat), BF),
        v((slots, rows, feat), F32),
        v((width, width), F32),
        v((hops + 2, 3, feat), F32),
        v((1, width), F32),
        dma(7),
        dma(4 + 2 * slots),
        dma(9),
        dma(6),
        dma(1),
        *[dma(3 * slots)] * 4,
        *[dma(slots)] * 4,
        *[dma(12)] * 2,
        *[dma(2 * slots)] * 6,
        *[dma(hops + 2)] * 2,
        *[dma(7 + extra)] * 18,
    ]
    total = slots * n * rows
    return pl.pallas_call(
        functools.partial(block_kernel, batch),
        in_specs=[pl.BlockSpec(memory_space=pltpu.SMEM)] + anywhere(10) + in_vmem(3),
        out_specs=anywhere(6) + in_vmem(1) + anywhere(12),
        out_shape=outs,
        scratch_shapes=scratch,
        compiler_params=pltpu.CompilerParams(
            collective_id=1, has_side_effects=True, vmem_limit_bytes=VMEM_LIMIT
        ),
        cost_estimate=pl.CostEstimate(
            flops=total * (30 * feat * width + 56 * width * width + 18 * feat * hid),
            transcendentals=total * 12 * width,
            bytes_accessed=2 * total * (12 * feat + 3 * hid),
        ),
        name="block",
    )(lengths, tokens, cotangent, *q4, wo, up, pair, down, gain_one, gain_two, gain_head)


def widen_kernel(unit, qk, vg, out, *targets):
    width = qk.shape[2] // 2
    for c in range(3):
        targets[5 + c][...] = unit[c, 0].astype(F32)
    targets[0][...] = qk[0, :, :width].astype(F32)
    targets[1][...] = qk[0, :, width:].astype(F32)
    targets[2][...] = vg[0, :, :width].astype(F32)
    targets[3][...] = vg[0, :, width:].astype(F32)
    targets[4][...] = out[0].astype(F32)


def widen(unit, qk, vg, out):
    hid, eighth = unit.shape[2:]
    width, feat = qk.shape[2] // 2, 8 * eighth
    piece = lambda dims: pl.BlockSpec((1,) + dims, lambda i: (i, 0, 0))
    flat = lambda dims: pl.BlockSpec(dims, lambda i: (i, 0))
    whole = lambda rows, cols: jax.ShapeDtypeStruct((rows, cols), F32)
    return pl.pallas_call(
        widen_kernel,
        grid=(8,),
        in_specs=[
            pl.BlockSpec((3, 1, hid, eighth), lambda i: (0, i, 0, 0)),
            piece(qk.shape[1:]),
            piece(vg.shape[1:]),
            piece(out.shape[1:]),
        ],
        out_specs=[flat((eighth, width))] * 4
        + [flat((width // 8, feat))]
        + [pl.BlockSpec((hid, eighth), lambda i: (0, i))] * 3,
        out_shape=[whole(feat, width)] * 4 + [whole(width, feat)] + [whole(hid, feat)] * 3,
        compiler_params=pltpu.CompilerParams(vmem_limit_bytes=VMEM_LIMIT),
        name="widen",
    )(unit, qk, vg, out)


def on_device(
    batch,
    tokens,
    lengths,
    assignment,
    query_weight,
    key_weight,
    value_weight,
    gate_weight,
    out_weight,
    up_weight,
    pair_weight,
    down_weight,
    attention_norm_gain,
    mlp_gain,
    head_gain,
    cotangent,
):
    slots = tokens.shape[0]
    width = query_weight.shape[1]
    place = lax.axis_index("seq").astype(jnp.int32)
    seq_ids = lax.broadcasted_iota(jnp.int32, (slots, lengths.shape[0]), 1)
    slot_length = jnp.sum(jnp.where(assignment[:, None] == seq_ids, lengths[None, :], 0), axis=1)
    q4 = (query_weight, key_weight, value_weight, gate_weight)
    gain_one, gain_two, gain_head = attention_norm_gain[None], mlp_gain[None], head_gain[None]
    result, grad_inputs, unit_total, qk_total, vg_total, out_total, gains = block(
        batch, slot_length, tokens, cotangent, q4, out_weight, up_weight.T, pair_weight.T, down_weight,
        gain_one, gain_two, gain_head,
    )[:7]
    grad_qw, grad_kw, grad_vw, grad_gw, grad_outw, grad_upw, grad_pairw, grad_down = widen(
        unit_total, qk_total, vg_total, out_total
    )
    head_total = lax.dynamic_slice(gains[2], (place * width,), (width,))
    return (
        result,
        grad_inputs,
        grad_qw,
        grad_kw,
        grad_vw,
        grad_gw,
        grad_outw,
        grad_upw.T,
        grad_pairw.T,
        grad_down,
        gains[0],
        gains[1],
        head_total,
    )


def solution(mesh):
    return jax.shard_map(
        functools.partial(on_device, mesh.shape["batch"]),
        mesh=mesh,
        in_specs=(
            P("batch", "seq", None),
            P(),
            P("batch"),
            P(None, "seq"),
            P(None, "seq"),
            P(None, "seq"),
            P(None, "seq"),
            P("seq", None),
            P(None, "seq"),
            P(None, "seq"),
            P("seq", None),
            P(),
            P(),
            P("seq"),
            P("batch", "seq", None),
        ),
        out_specs=(
            P("batch", "seq", None),
            P("batch", "seq", None),
            P(None, "seq"),
            P(None, "seq"),
            P(None, "seq"),
            P(None, "seq"),
            P("seq", None),
            P(None, "seq"),
            P(None, "seq"),
            P("seq", None),
            P(),
            P(),
            P("seq"),
        ),
        check_vma=False,
    )
```

```python
import functools

import jax
import jax.numpy as jnp
from jax import lax
from jax.experimental import pallas as pl
from jax.experimental.pallas import tpu as pltpu
from jax.sharding import PartitionSpec as P

HD = 64
EPS = 1e-05
BF = jnp.bfloat16
F32 = jnp.float32
VMEM_LIMIT = 62 * 1024 * 1024
MESH = pl.DeviceIdType.MESH
BLOCKS = 4


def nn(a, b):
    return lax.dot_general(a, b, (((1,), (0,)), ((), ())), preferred_element_type=F32)


def nt(a, b):
    return lax.dot_general(a, b, (((1,), (1,)), ((), ())), preferred_element_type=F32)


def tn(a, b):
    return lax.dot_general(a, b, (((0,), (0,)), ((), ())), preferred_element_type=F32)


def same_head(width):
    rows = lax.broadcasted_iota(jnp.int32, (width, width), 0) // HD
    cols = lax.broadcasted_iota(jnp.int32, (width, width), 1) // HD
    return rows == cols


def by_head(array):
    rows, width = array.shape
    lane = lax.broadcasted_iota(jnp.int32, (rows, width), 1) // HD
    zero = jnp.zeros_like(array)
    return jnp.concatenate([jnp.where(lane == h, array, zero) for h in range(width // HD)], axis=0)


def causal(rows, heads, transposed):
    one = lax.broadcasted_iota(jnp.int32, (rows, rows), 0)
    two = lax.broadcasted_iota(jnp.int32, (rows, rows), 1)
    keep = (two >= one) if transposed else (one >= two)
    return jnp.concatenate([keep] * heads, axis=1)


def masked(scores, keep):
    return jnp.where(keep, scores, 0.0).astype(BF)


def head_mean(array, ones):
    return nn(array.astype(BF), ones) * (1.0 / HD)


def softplus(v):
    return jnp.maximum(v, 0.0) + jnp.log1p(jnp.exp(-jnp.abs(v)))


def sigmoid_of_softplus(q):
    series = q * (1.0 - q * (0.5 - q * (1.0 / 6.0)))
    return jnp.where(q < 0.03, series, 1.0 - jnp.exp(-q))


def sigmoid(v):
    return 1.0 / (1.0 + jnp.exp(-v))


class Peers:
    def __init__(self, batch=1):
        self.place = lax.axis_index("seq")
        self.group = lax.axis_index("batch")
        self.chip, self.core = self.place // 2, self.place % 2
        self.across = (self.group, (1 - self.chip) * 2 + self.core)
        self.beside = (self.group, self.chip * 2 + 1 - self.core)
        self.hops = batch.bit_length() - 1

    def bit(self, h):
        return (self.group // 2**h) % 2

    def partner(self, h):
        return (self.group + (1 - 2 * self.bit(h)) * 2**h, self.place)

    def meet(self):
        others = [self.across, self.beside] + [self.partner(h) for h in range(self.hops)]
        barrier = pltpu.get_barrier_semaphore()
        for peer in others:
            pl.semaphore_signal(barrier, inc=1, device_id=peer, device_id_type=MESH)
        pl.semaphore_wait(barrier, len(others))

    def relative(self, index):
        return ((index // 2 + self.chip) % 2) * 2 + (index % 2 + self.core) % 2


def spot(j):
    return (j % 2) * 2 + j // 2


def remote(source, target, sems, index, peer):
    send, recv = sems
    return pltpu.make_async_remote_copy(
        src_ref=source,
        dst_ref=target,
        send_sem=send.at[index],
        recv_sem=recv.at[index],
        device_id=peer,
        device_id_type=MESH,
    )


class Gather:
    def __init__(self, peers, buffer, sems, own=None):
        self.peers, self.buffer, self.sems = peers, buffer, sems
        self.own = own or (lambda k: buffer.at[k, 0])

    def chip_hop(self, k):
        return remote(self.own(k), self.buffer.at[k, 2], self.sems, 3 * k, self.peers.across)

    def core_hop(self, k):
        return remote(self.own(k), self.buffer.at[k, 1], self.sems, 3 * k + 1, self.peers.beside)

    def passed_on(self, k):
        return remote(
            self.buffer.at[k, 2], self.buffer.at[k, 3], self.sems, 3 * k + 2, self.peers.beside
        )

    def start(self, k):
        self.chip_hop(k).start()
        self.core_hop(k).start()

    def forward(self, k):
        self.chip_hop(k).wait_recv()
        self.passed_on(k).start()

    def arrived(self, k):
        self.core_hop(k).wait_recv()
        self.passed_on(k).wait_recv()

    def sent(self, k):
        self.chip_hop(k).wait_send()
        self.core_hop(k).wait_send()
        self.passed_on(k).wait_send()


class Scatter:
    def __init__(self, peers, pair, middle, came, far, sems):
        self.peers, self.pair, self.middle = peers, pair, middle
        self.came, self.far, self.sems = came, far, sems

    def core_hop(self, k):
        return remote(self.pair(k), self.came.at[k], self.sems, 2 * k, self.peers.beside)

    def chip_hop(self, k):
        return remote(self.middle(k), self.far.at[k], self.sems, 2 * k + 1, self.peers.across)

    def start(self, k):
        self.core_hop(k).start()

    def middle_step(self, k):
        self.core_hop(k).wait_recv()
        middle = self.middle(k)

        def add(rows):
            middle[rows] = (middle[rows].astype(F32) + self.came[k, 1, rows].astype(F32)).astype(BF)

        by_rows(middle.shape[0], add)
        self.chip_hop(k).start()

    def arrived(self, k):
        self.chip_hop(k).wait_recv()

    def sent(self, k):
        self.core_hop(k).wait_send()
        self.chip_hop(k).wait_send()


class Chain:
    def __init__(self, peers, bits, work, came, room, total, sems, load, source=None, far=None, across=None):
        self.peers, self.sems, self.stages, self.waited = peers, sems, [], set()
        b0, b1, b2 = (peers.bit(h) for h in bits)
        pair = 2 if across == "last" else 1
        start = 0 if pair == 2 else b0 * 4
        kept = (start + b1 * 2 + b2) * pair
        self.kept = kept
        piece = b0 * 4 + b1 * 2 + b2

        def fetch(ref):
            copy = pltpu.make_async_copy(ref, room.at[pl.ds(0, ref.shape[0])], load)
            copy.start()
            copy.wait()

        def add(at, base, count):
            def finish():
                fetch(came.at[pl.ds(at, count)])

                def one(q):
                    work[base + q] = (work[base + q].astype(F32) + room[q].astype(F32)).astype(BF)

                loop(count, one)

            return finish

        def spread():
            fetch(far)

            def one(q):
                work[q] = (work[q].astype(F32) + room[q].astype(F32)).astype(BF)

            loop(8, one)

        def meet():
            fetch(far.at[pl.ds(0, 1)])
            work[kept] = (work[kept].astype(F32) + room[0].astype(F32)).astype(BF)

        def other(base, bit, count):
            return work.at[pl.ds((base + (1 - bit) * count) * pair, count * pair)]

        if across == "first":
            self.stages.append((source.at[pl.ds(8, 8)], far, peers.across, spread))
        first = source.at[pl.ds((1 - b0) * 8, 8)] if pair == 2 else other(0, b0, 4)
        at = 0
        for bit, base, count, h in (
            (b0, start, 4, bits[0]), (b1, start, 2, bits[1]), (b2, start + b1 * 2, 1, bits[2])
        ):
            here = base + (bit * count if count < 4 else 0)
            ref = first if count == 4 else other(base, bit, count)
            self.stages.append(
                (ref, came.at[pl.ds(at, count * pair)], peers.partner(h), add(at, here * pair, count * pair))
            )
            at += count * pair
        for h in range(peers.hops):
            if h not in bits:
                ref = work.at[pl.ds(kept, pair)]
                self.stages.append((ref, came.at[pl.ds(at, pair)], peers.partner(h), add(at, kept, pair)))
                self.waited.add(len(self.stages) - 1)
                at += pair
        if across == "last":
            self.stages.append((work.at[pl.ds(kept + 1, 1)], far.at[pl.ds(0, 1)], peers.across, meet))
        self.local = lambda: pltpu.make_async_copy(
            work.at[pl.ds(kept, 1)], total.at[pl.ds(piece, 1)], load
        )
        for where, h in (
            (pl.ds(piece, 1), bits[2]),
            (pl.ds(b0 * 4 + b1 * 2, 2), bits[1]),
            (pl.ds(b0 * 4, 4), bits[0]),
        ):
            ref = work.at[pl.ds(kept, 1)] if h == bits[2] else total.at[where]
            self.stages.append((ref, total.at[where], peers.partner(h), lambda: None))
        self.count = len(self.stages)

    def hop(self, t):
        source, target, peer, _ = self.stages[t]
        return remote(source, target, self.sems, t, peer)

    def begin(self):
        self.hop(0).start()

    def step(self, t):
        self.hop(t).wait_recv()
        if t in self.waited:
            self.hop(t).wait_send()
        self.stages[t][3]()
        if t == self.count - 4:
            own = self.local()
            own.start()
            own.wait()
        if t + 1 < self.count:
            self.hop(t + 1).start()

    def sent(self):
        for t in range(self.count):
            if t not in self.waited:
                self.hop(t).wait_send()


def by_rows(rows, fn, step=64):
    def one(r, carry):
        fn(pl.ds(pl.multiple_of(r * step, step), step))
        return carry

    lax.fori_loop(0, rows // step, one, 0)


def loop(count, fn):
    def one(k, carry):
        fn(k)
        return carry

    lax.fori_loop(0, count, one, 0)


def normalize(values, gain):
    scale = lax.rsqrt(jnp.mean(values * values, axis=-1, keepdims=True) + EPS)
    normed = values * scale
    return normed, scale, (normed * gain).astype(BF)


def norm_back(grad_out, normed, scale, gain):
    grad_normed = grad_out * gain
    inner = jnp.mean(grad_normed * normed, axis=-1, keepdims=True)
    return scale * (grad_normed - normed * inner)


def block_kernel(
    batch,
    length_ref, tokens, cotangent, wq, wk, wv, wg, wo, up, pair, down, gain_one, gain_two, gain_head,
    result, grad_tokens, unit_total, qk_total, vg_total, out_total, gains,
    qkvg_hbm, mixed_hbm, gated_hbm, state_hbm, gm, other, sums, unit_came, unit_far, qk_came, vg_came,
    out_came,
    tok, w4, wo_v, h1, h2, g, part, came, far, middle, state, gain_came, head_part,
    load_sem, save_sem, slot_sem, mat_sem, chain_sem,
    h1_send, h1_recv, gm_send, gm_recv, h2_send, h2_recv, g_send, g_recv, w_send, w_recv,
    a_send, a_recv, b_send, b_recv, c_send, c_recv, gain_send, gain_recv,
    d_send, d_recv, u_send, u_recv, p_send, p_recv,
    d2_send, d2_recv, u2_send, u2_recv, p2_send, p2_recv, q_send, q_recv, v_send, v_recv, o_send, o_recv,
):
    slots, rows, feat = tok.shape
    width, hid = wo_v.shape[0], down.shape[0]
    heads, eighth = width // HD, feat // 8
    both = 2 * hid
    peers = Peers(batch)
    v = pltpu.VMEM

    def load(source, target, index):
        return pltpu.make_async_copy(source, target, load_sem.at[index])

    loads = [
        load(tokens, tok, 0),
        *(load(w, w4.at[m], 1 + m) for m, w in enumerate((wq, wk, wv, wg))),
        load(wo, wo_v, 5),
        load(cotangent, g.at[:, 0], 6),
    ]
    for one in loads:
        one.start()
    peers.meet()

    mats = (up, pair, down)
    b0, b1, b2 = (peers.bit(h) for h in range(3))

    def columns(first, count):
        return pl.ds(pl.multiple_of(first * eighth, eighth), count * eighth)

    def weight_hop(t, c):
        mine = other.at[c]
        cols = (
            columns(b0 * 4 + b1 * 2 + b2, 1), columns(b0 * 4 + b1 * 2 + b2, 1),
            columns(b0 * 4 + b1 * 2, 2), columns(b0 * 4, 4),
        )[t]
        source = (mats[c] if t == 0 else mine).at[:, cols]
        peer = peers.across if t == 0 else peers.partner(3 - t)
        return remote(source, mine.at[:, cols], (w_send, w_recv), 4 * c + t, peer)

    def weight_step(t, c):
        weight_hop(t - 1, c).wait_recv()
        if t < 4:
            weight_hop(t, c).start()

    for c in range(3):
        weight_hop(0, c).start()
    first = Gather(peers, h1, (h1_send, h1_recv))
    third = Gather(peers, gm, (gm_send, gm_recv), lambda k: tok.at[k])

    def pass_h2(k):
        return remote(h2.at[k, 0], h2.at[k, 1], (h2_send, h2_recv), k, peers.beside)

    def pass_g(k):
        return remote(cotangent.at[k], g.at[k, 1], (g_send, g_recv), k, peers.beside)

    buffers = (lambda k: part.at[k, pl.ds(2, 2)], lambda k: part.at[k, 1], came, far)
    scatter_a = Scatter(peers, *buffers, (a_send, a_recv))
    scatter_c = Scatter(peers, *buffers, (c_send, c_recv))

    def pass_grad(k):
        return remote(part.at[k, 1], came.at[k, 0], (b_send, b_recv), 2 * k, peers.beside)

    def pass_result(k):
        return remote(part.at[k, 3], came.at[k, 1], (b_send, b_recv), 2 * k + 1, peers.beside)

    g1, g2, gh = gain_one[...], gain_two[...], gain_head[...]
    gains[...] = jnp.zeros_like(gains)
    head_part[...] = jnp.zeros_like(head_part)
    loads[0].wait()

    def norm_first(k):
        def some(r):
            _, _, hidden = normalize(tok[k, r].astype(F32), g1)
            h1[k, 0, r] = hidden

        by_rows(rows, some)
        first.start(k)

    loop(slots, norm_first)
    loop(slots, lambda k: pass_g(k).start())
    for t, c in ((1, 0), (1, 1), (1, 2), (2, 0), (2, 1), (3, 0)):
        weight_step(t, c)
    for one in loads[1:6]:
        one.wait()

    same = same_head(width)
    ones = same.astype(BF)

    def attend_all(qkvg, mixed_s, gated_s, state_s):
        def saves(k):
            return [
                pltpu.make_async_copy(qkvg, qkvg_hbm.at[k], save_sem.at[0]),
                pltpu.make_async_copy(mixed_s, mixed_hbm.at[k], save_sem.at[1]),
                pltpu.make_async_copy(gated_s, gated_hbm.at[k], save_sem.at[2]),
                pltpu.make_async_copy(state_s, state_hbm.at[k], save_sem.at[3]),
            ]

        def attend(k):
            first.forward(k)

            @pl.when(k > 0)
            def _():
                scatter_a.middle_step(k - 1)
                for one in saves(k - 1):
                    one.wait()

            @pl.when(k == 1)
            def _():
                weight_step(2, 2)
                weight_step(3, 1)

            @pl.when(k == 2)
            def _():
                weight_step(3, 2)

            first.arrived(k)
            state[...] = jnp.zeros_like(state)
            length = length_ref[k]

            def chunk(i):
                j = peers.relative(i)
                hidden = h1[k, j]
                position = lax.broadcasted_iota(jnp.int32, (rows, width), 0) + i * rows
                query = softplus(nn(hidden, w4[0])).astype(BF)
                keys = jnp.where(position < length, softplus(nn(hidden, w4[1])), 0.0).astype(BF)
                values = nn(hidden, w4[2]).astype(BF)
                gate = nn(hidden, w4[3])
                qkvg[j, 0] = query
                qkvg[j, 1] = keys
                qkvg[j, 2] = values
                qkvg[j, 3] = gate.astype(BF)
                before = state[...].astype(BF)
                state_s[i] = before
                scores = masked(nt(query, by_head(keys)), causal(rows, heads, False))
                mixed = nn(query, before) + nn(scores, by_head(values))
                state[...] += jnp.where(same, tn(keys, values), 0.0)
                mixed_s[j] = mixed.astype(BF)
                scale = lax.rsqrt(head_mean(mixed * mixed, ones) + EPS)
                gated_s[j] = (mixed * scale * gh * (gate * sigmoid(gate))).astype(BF)

            loop(BLOCKS, chunk)
            for one in saves(k):
                one.start()

            def project(p):
                j = (p % 2) * 2 + p // 2
                part[k, p] = nn(gated_s[j], wo_v[...]).astype(BF)

            project(2)
            project(3)
            scatter_a.start(k)
            project(1)
            project(0)

        loop(slots, attend)
        for one in saves(slots - 1):
            one.wait()

    pl.run_scoped(
        attend_all,
        v((BLOCKS, 4, rows, width), BF),
        v((BLOCKS, rows, width), BF),
        v((BLOCKS, rows, width), BF),
        v((BLOCKS, width, width), BF),
    )
    scatter_a.middle_step(slots - 1)

    def finish_attend(k):
        scatter_a.arrived(k)

        def some(r):
            value = (
                tok[k, r].astype(F32)
                + part[k, 0, r].astype(F32)
                + came[k, 0, r].astype(F32)
                + far[k, r].astype(F32)
            )
            middle[k, r] = value
            _, _, hidden = normalize(value, g2)
            h2[k, 0, r] = hidden

        by_rows(rows, some)
        pass_h2(k).start()
        scatter_a.sent(k)

    finish_attend(0)
    finish_attend(1)
    loads[6].wait()

    def result_save(k):
        return pltpu.make_async_copy(part.at[k, 2], result.at[k], save_sem.at[4 + k])

    def unit_all(mat, prod_s, gu_s, gp_s, staged):
        def mat_load(c, which):
            source = mats[c] if which == 0 else other.at[c]
            return pltpu.make_async_copy(
                source, mat.at[c, pl.ds(which * hid, hid)], mat_sem.at[2 * c + which]
            )

        for c in range(3):
            mat_load(c, 0).start()
        for c in range(3):
            weight_step(4, c)
            mat_load(c, 1).start()
        for c in range(3):
            mat_load(c, 0).wait()
            mat_load(c, 1).wait()

        def unit(k):
            pass_h2(k).wait_recv()
            pass_g(k).wait_recv()

            def one(t):
                j = 1 - t
                hidden, grad = h2[k, j], g[k, j]
                up_part = nt(hidden, mat[0])
                pair_part = nt(hidden, mat[1])
                product = (up_part * pair_part).astype(BF)
                prod_s[k, j] = product
                part[k, 2 + j] = nn(product, mat[2]).astype(BF)
                grad_product = nt(grad, mat[2]).astype(BF).astype(F32)
                grad_up = (grad_product * pair_part).astype(BF)
                grad_pair = (grad_product * up_part).astype(BF)
                gu_s[k, j] = grad_up
                gp_s[k, j] = grad_pair
                part[k, j] = (nn(grad_up, mat[0]) + nn(grad_pair, mat[1])).astype(BF)

                @pl.when(t == 0)
                def _():
                    pass_grad(k).start()
                    pass_result(k).start()

            loop(2, one)

            @pl.when(k == 0)
            def _():
                for m in range(2, slots):
                    finish_attend(m)

            pass_grad(k).wait_recv()
            pass_result(k).wait_recv()

            def some(r):
                value = middle[k, r]
                total = value + part[k, 2, r].astype(F32) + came[k, 1, r].astype(F32)
                part[k, 2, r] = total.astype(BF)
                grad = part[k, 0, r].astype(F32) + came[k, 0, r].astype(F32)
                normed, scale, _ = normalize(value, g2)
                gains[1:2] += jnp.sum(grad * normed, axis=0, keepdims=True)
                back = g[k, 0, r].astype(F32) + norm_back(grad, normed, scale, g2)
                middle[k, r] = back
                tok[k, r] = back.astype(BF)

            by_rows(rows, some)
            third.start(k)
            pltpu.make_async_copy(tok.at[k], gm.at[k, 0], save_sem.at[4 + slots + k]).start()
            result_save(k).start()

        loop(slots, unit)
        tile = 256
        everything = slots * 2 * rows

        def weigh(c, left, right):
            for start in range(0, both, tile):
                span = min(tile, both - start)
                term = tn(
                    left[:, :, :, start : start + span].reshape(everything, span),
                    right[...].reshape(everything, feat),
                ).astype(BF)
                for q in range(2):
                    for m in range(2):
                        base = q * hid + m * (hid // 2)
                        low, high = max(start, base), min(start + span, base + hid // 2)
                        if low >= high:
                            continue
                        for p in range(8):
                            index = q * 8 + p if KINDS["UPD"[c] if m == 0 else "upd"[c]][0] == "first" else p * 2 + q
                            staged[index, low - q * hid : high - q * hid] = term[
                                low - start : high - start, p * eighth : (p + 1) * eighth
                            ]
            save = pltpu.make_async_copy(staged, sums.at[c], save_sem.at[3])
            save.start()
            save.wait()
            for m in range(2):
                begin_unit(c, m)

        turn = iter(range(slots))
        for c in UNIT_ORDER:
            weigh(c, (gu_s, gp_s, prod_s)[c], (h2, h2, g)[c])
            third.forward(next(turn))
        for k in turn:
            third.forward(k)

    half = pl.ds(0, hid // 2), pl.ds(hid // 2, hid // 2)
    unit_sems = (
        ((u_send, u_recv), (p_send, p_recv), (d_send, d_recv)),
        ((u2_send, u2_recv), (p2_send, p2_recv), (d2_send, d2_recv)),
    )

    def unit_chain(c, m, work, room):
        across, bits = KINDS[("UPD", "upd")[m][c]]
        return Chain(
            peers, bits, work, unit_came.at[c, :, half[m]], room, unit_total.at[c, :, half[m]],
            unit_sems[m][c], chain_sem.at[0], sums.at[c, :, half[m]], unit_far.at[c, :, half[m]], across,
        )

    def begin_unit(c, m):
        unit_chain(c, m, h2.at[0], None).begin()

    pl.run_scoped(
        unit_all,
        v((3, both, feat), BF),
        v((slots, 2, rows, both), BF),
        v((slots, 2, rows, both), BF),
        v((slots, 2, rows, both), BF),
        v((16, hid, eighth), BF),
    )

    def rest(works, room, qk_work, vg_work, out_work, pair_room, small_room):
        chains = {}
        work_loads = []
        for m in range(2):
            for c in range(3):
                name = ("UPD", "upd")[m][c]
                work = works.at[c, :, half[m]]
                chains[name] = unit_chain(c, m, work, room)
                first_half = 0 if KINDS[name][0] == "first" else peers.bit(KINDS[name][1][0]) * 8
                work_loads.append(
                    pltpu.make_async_copy(
                        sums.at[c, pl.ds(first_half, 8), half[m]], work, mat_sem.at[3 * m + c]
                    )
                )
        for name, work, come, space, total, pair_sems in (
            ("Q", qk_work, qk_came, pair_room, qk_total, (q_send, q_recv)),
            ("V", vg_work, vg_came, pair_room, vg_total, (v_send, v_recv)),
            ("O", out_work, out_came, small_room, out_total, (o_send, o_recv)),
        ):
            chains[name] = Chain(
                peers, KINDS[name][1], work, come, space, total, pair_sems, chain_sem.at[0]
            )
        for one in work_loads:
            one.start()
        for one in work_loads:
            one.wait()
        done = {name: 0 for name in chains}
        plan, tail, where = {}, [], (0, -1)
        for name, at in SCHEDULE:
            if name == "c":
                where = (at // 10, at % 10 + 1)
            elif name == "g":
                where = (at, 0)
            elif name == "T":
                where = None
            elif name in chains and where is None or name in ("F", "B", "A"):
                tail.append((name, at))
            elif name in chains:
                slot, point = where
                if point == 8 and slot + 1 < slots:
                    slot, point = slot + 1, -1
                plan.setdefault((slot, point), []).append((name, at))

        def play(actions):
            for name, stage in actions:
                chains[name].step(stage)
                done[name] = max(done[name], stage + 1)

        def attend_all_back(qkvg, mixed_v, state_v, gated, gm_v, pre, acc, out_acc):
            def slot_loads(k):
                b = k % 2
                pairs = (
                    (qkvg_hbm, qkvg), (mixed_hbm, mixed_v), (state_hbm, state_v), (gated_hbm, gated)
                )
                return [
                    pltpu.make_async_copy(source.at[k], target.at[b], slot_sem.at[4 * b + m])
                    for m, (source, target) in enumerate(pairs)
                ]

            for one in slot_loads(0):
                one.start()

            def hooks(k, point, low, high):
                for (slot, at), actions in plan.items():
                    if not low <= at < high:
                        continue

                    @pl.when((k == slot) & (point == at))
                    def _():
                        play(actions)

            def attend_back(k):
                b = k % 2
                hooks(k, -1, -1, 0)
                hooks(k, 0, 0, 1)
                third.arrived(k)
                pltpu.make_async_copy(tok.at[k], gm.at[k, 0], save_sem.at[4 + slots + k]).wait()
                fetch = pltpu.make_async_copy(gm.at[k], gm_v, slot_sem.at[8])
                fetch.start()

                @pl.when(k > 0)
                def _():
                    scatter_c.middle_step(k - 1)

                @pl.when(k + 1 < slots)
                def _():
                    for one in slot_loads(k + 1):
                        one.start()

                for one in slot_loads(k):
                    one.wait()
                result_save(k).wait()
                pass_grad(k).wait_send()
                pass_result(k).wait_send()
                state[...] = jnp.zeros_like(state)
                fetch.wait()

                def chunk(step):
                    hooks(k, step, 1, BLOCKS)
                    i = BLOCKS - 1 - step
                    j = peers.relative(i)
                    grad_gated = nt(gm_v[j], wo_v[...]).astype(BF).astype(F32)
                    query, keys, values = qkvg[b, j, 0], qkvg[b, j, 1], qkvg[b, j, 2]
                    gate = qkvg[b, j, 3].astype(F32)
                    mixed = mixed_v[b, j].astype(F32)
                    scale = lax.rsqrt(head_mean(mixed * mixed, ones) + EPS)
                    normed = mixed * scale
                    opened = sigmoid(gate)
                    grad_gate = grad_gated * (normed * gh) * opened * (1.0 + gate * (1.0 - opened))
                    grad_head = grad_gated * (gate * opened)
                    head_part[...] += jnp.sum(grad_head * normed, axis=0, keepdims=True)
                    scaled = grad_head * gh
                    inner = head_mean(scaled * normed, ones)
                    grad_mixed = (scale * (scaled - normed * inner)).astype(BF)
                    after = state[...].astype(BF)
                    before = state_v[b, i]
                    lower = causal(rows, heads, False)
                    upper = causal(rows, heads, True)
                    query_heads = by_head(query)
                    mixed_heads = by_head(grad_mixed)
                    grad_scores = masked(nt(grad_mixed, by_head(values)), lower)
                    grad_query = nt(grad_mixed, before) + nn(grad_scores, by_head(keys))
                    grad_scores_t = masked(nt(values, mixed_heads), upper)
                    grad_keys = nt(values, after) + nn(grad_scores_t, query_heads)
                    scores_t = masked(nt(keys, query_heads), upper)
                    grad_values = nn(keys, after) + nn(scores_t, mixed_heads)
                    state[...] += jnp.where(same, tn(query, grad_mixed), 0.0)

                    rounded = lambda x: x.astype(BF).astype(F32)
                    pre_q = (rounded(grad_query) * sigmoid_of_softplus(query.astype(F32))).astype(BF)
                    pre_k = (rounded(grad_keys) * sigmoid_of_softplus(keys.astype(F32))).astype(BF)
                    pre_v = grad_values.astype(BF)
                    pre_g = grad_gate.astype(BF)
                    for m, one in enumerate((pre_q, pre_k, pre_v, pre_g)):
                        pre[j, :, m * width : (m + 1) * width] = one
                    grad_h = (
                        nt(pre_q, w4[0]) + nt(pre_k, w4[1]) + nt(pre_v, w4[2]) + nt(pre_g, w4[3])
                    )
                    part[k, spot(j)] = grad_h.astype(BF)

                loop(BLOCKS, chunk)
                scatter_c.start(k)
                pre_all = pre[...].reshape(BLOCKS * rows, 4 * width)

                def weigh(m):
                    hooks(k, BLOCKS + m, BLOCKS, 8)
                    cols = pl.ds(pl.multiple_of(m * 256, 256), 256)
                    term = tn(h1[k, :, :, cols].reshape(BLOCKS * rows, 256), pre_all)
                    acc[cols] = jnp.where(k > 0, acc[cols], 0.0) + term

                loop(feat // 256, weigh)
                term = tn(gated[b].reshape(BLOCKS * rows, width), gm_v[...].reshape(BLOCKS * rows, feat))
                out_acc[...] = jnp.where(k > 0, out_acc[...], 0.0) + term

            loop(slots, attend_back)
            play(plan.get((slots - 1, 8), ()))
            scatter_c.middle_step(slots - 1)
            part_rows = width // 8

            def fill(p):
                at = pl.ds(pl.multiple_of(p * eighth, eighth), eighth)
                small = pl.ds(pl.multiple_of(p * part_rows, part_rows), part_rows)
                qk_work[p] = acc[at, : 2 * width].astype(BF)
                vg_work[p] = acc[at, 2 * width :].astype(BF)
                out_work[p] = out_acc[small].astype(BF)

            loop(8, fill)
            for name in ATTENTION_ORDER:
                chains[name].begin()

        pl.run_scoped(
            attend_all_back,
            v((2, BLOCKS, 4, rows, width), BF),
            v((2, BLOCKS, rows, width), BF),
            v((2, BLOCKS, width, width), BF),
            v((2, BLOCKS, rows, width), BF),
            v((BLOCKS, rows, feat), BF),
            v((BLOCKS, rows, 4 * width), BF),
            v((feat, 4 * width), F32),
            v((width, feat), F32),
        )
        loop(slots, lambda k: third.sent(k))
        again = load(tokens, tok, 0)
        again.start()

        def grad_save(k):
            return pltpu.make_async_copy(middle.at[k], grad_tokens.at[k], save_sem.at[4 + k])

        def finish(k):
            scatter_c.arrived(k)

            def some(r):
                grad = (
                    part[k, 0, r].astype(F32) + came[k, 0, r].astype(F32) + far[k, r].astype(F32)
                )
                normed, scale, _ = normalize(tok[k, r].astype(F32), g1)
                gains[0:1] += jnp.sum(grad * normed, axis=0, keepdims=True)
                middle[k, r] = middle[k, r] + norm_back(grad, normed, scale, g1)

            by_rows(rows, some)
            grad_save(k).start()

        others = [peers.beside, peers.across] + [peers.partner(h) for h in range(peers.hops)]

        def gain_hop(t):
            return remote(gains, gain_came.at[t], (gain_send, gain_recv), t, others[t])

        def gain_begin():
            lane = lax.broadcasted_iota(jnp.int32, (1, BLOCKS * width), 1) // width
            spread = jnp.concatenate([head_part[...]] * BLOCKS, axis=1)
            gains[2:3] = jnp.where(lane == peers.place, spread, 0.0)
            gain_hop(0).start()

        hop = iter(range(len(others)))

        def gain_step():
            t = next(hop, None)
            if t is None:
                return
            gain_hop(t).wait_recv()
            gain_hop(t).wait_send()
            gains[...] += gain_came[t]
            if t + 1 < len(others):
                gain_hop(t + 1).start()

        again.wait()
        turn = iter(range(slots))
        for name, stage in tail:
            if name == "F":
                finish(next(turn))
            elif name == "B":
                for k in turn:
                    finish(k)
                gain_begin()
            elif name == "A":
                gain_step()
            else:
                play([(name, stage)])
        for _ in others:
            gain_step()
        most = max(one.count for one in chains.values())
        for t in range(most):
            for name in chains:
                if done[name] <= t < chains[name].count:
                    play([(name, t)])
        for one in chains.values():
            one.sent()

        def settle(k):
            grad_save(k).wait()
            first.sent(k)
            scatter_c.sent(k)
            pass_h2(k).wait_send()
            pass_g(k).wait_send()

        loop(slots, settle)

        def settle_weights(c):
            for t in range(4):
                weight_hop(t, c).wait_send()

        for c in range(3):
            settle_weights(c)

    pl.run_scoped(
        rest,
        v((3, 8, hid, eighth), BF),
        v((8, hid // 2, eighth), BF),
        v((8, eighth, 2 * width), BF),
        v((8, eighth, 2 * width), BF),
        v((8, width // 8, feat), BF),
        v((4, eighth, 2 * width), BF),
        v((4, width // 8, feat), BF),
    )


def dma(n):
    return pltpu.SemaphoreType.DMA((n,))


def anywhere(n):
    return [pl.BlockSpec(memory_space=pl.ANY)] * n


def in_vmem(n):
    return [pl.BlockSpec(memory_space=pltpu.VMEM)] * n


KINDS = {
    "U": ("last", (0, 1, 2)),
    "P": ("first", (0, 1, 2)),
    "D": ("first", (0, 1, 2)),
    "u": ("last", (1, 0, 2)),
    "p": ("first", (0, 1, 2)),
    "d": ("last", (1, 0, 2)),
    "Q": (None, (1, 0, 2)),
    "V": (None, (0, 1, 2)),
    "O": (None, (0, 1, 2)),
}
UNIT_ORDER = (0, 1, 2)
ATTENTION_ORDER = ('O', 'Q', 'V')
SCHEDULE = (
    ("u", 0), ("U", 0), ("g", 0), ("P", 0), ("c", 0), ("c", 1), ("u", 1), ("c", 2), ("c", 3), ("P", 1),
    ("p", 0), ("U", 1), ("c", 4), ("u", 2), ("c", 5), ("c", 6), ("P", 2), ("c", 7), ("p", 1), ("g", 1),
    ("D", 0), ("u", 3), ("p", 2), ("c", 10), ("c", 11), ("u", 4), ("c", 12), ("D", 1), ("p", 3), ("c", 13),
    ("c", 14), ("D", 2), ("c", 15), ("p", 4), ("c", 16), ("c", 17), ("g", 2), ("P", 3), ("u", 5), ("p", 5),
    ("d", 0), ("D", 3), ("c", 20), ("P", 4), ("c", 21), ("c", 22), ("c", 23), ("D", 4), ("c", 24), ("c", 25),
    ("P", 5), ("d", 1), ("c", 26), ("c", 27), ("T", 0), ("U", 2), ("F", 0), ("d", 2), ("F", 1), ("O", 0),
    ("F", 2), ("B", 0), ("U", 3), ("Q", 0), ("O", 1), ("d", 3), ("V", 0), ("U", 4), ("D", 5), ("A", 0),
    ("O", 2), ("A", 0), ("Q", 1), ("A", 0), ("V", 1), ("A", 0), ("A", 0), ("U", 5), ("O", 3), ("Q", 2),
    ("d", 4), ("V", 2), ("O", 4), ("d", 5), ("Q", 3), ("V", 3), ("Q", 4), ("V", 4),
)


def block(batch, lengths, tokens, cotangent, q4, wo, up, pair, down, gain_one, gain_two, gain_head):
    slots, rows, feat = tokens.shape
    width, hid = wo.shape[0], down.shape[0]
    eighth = feat // 8
    n = BLOCKS
    hops = batch.bit_length() - 1
    extra = hops - 3
    shape = jax.ShapeDtypeStruct
    blocks = lambda *dims: shape((slots, n) + dims, BF)
    outs = [
        shape((slots, rows, feat), BF),
        shape((slots, rows, feat), F32),
        shape((3, 8, hid, eighth), BF),
        shape((8, eighth, 2 * width), BF),
        shape((8, eighth, 2 * width), BF),
        shape((8, width // 8, feat), BF),
        shape((3, feat), F32),
        blocks(4, rows, width),
        blocks(rows, width),
        blocks(rows, width),
        blocks(width, width),
        blocks(rows, feat),
        shape((3, hid, feat), BF),
        shape((3, 16, hid, eighth), BF),
        shape((3, 14 + 2 * extra, hid, eighth), BF),
        shape((3, 8, hid, eighth), BF),
        shape((7 + extra, eighth, 2 * width), BF),
        shape((7 + extra, eighth, 2 * width), BF),
        shape((7 + extra, width // 8, feat), BF),
    ]
    v = pltpu.VMEM
    scratch = [
        v((slots, rows, feat), BF),
        v((4, feat, width), BF),
        v((width, feat), BF),
        v((slots, n, rows, feat), BF),
        v((slots, 2, rows, feat), BF),
        v((slots, 2, rows, feat), BF),
        v((slots, n, rows, feat), BF),
        v((slots, 2, rows, feat), BF),
        v((slots, rows, feat), BF),
        v((slots, rows, feat), F32),
        v((width, width), F32),
        v((hops + 2, 3, feat), F32),
        v((1, width), F32),
        dma(7),
        dma(4 + 2 * slots),
        dma(9),
        dma(6),
        dma(1),
        *[dma(3 * slots)] * 4,
        *[dma(slots)] * 4,
        *[dma(12)] * 2,
        *[dma(2 * slots)] * 6,
        *[dma(hops + 2)] * 2,
        *[dma(7 + extra)] * 18,
    ]
    total = slots * n * rows
    return pl.pallas_call(
        functools.partial(block_kernel, batch),
        in_specs=[pl.BlockSpec(memory_space=pltpu.SMEM)] + anywhere(10) + in_vmem(3),
        out_specs=anywhere(6) + in_vmem(1) + anywhere(12),
        out_shape=outs,
        scratch_shapes=scratch,
        compiler_params=pltpu.CompilerParams(
            collective_id=1, has_side_effects=True, vmem_limit_bytes=VMEM_LIMIT
        ),
        cost_estimate=pl.CostEstimate(
            flops=total * (30 * feat * width + 56 * width * width + 18 * feat * hid),
            transcendentals=total * 12 * width,
            bytes_accessed=2 * total * (12 * feat + 3 * hid),
        ),
        name="block",
    )(lengths, tokens, cotangent, *q4, wo, up, pair, down, gain_one, gain_two, gain_head)


def widen_kernel(unit, qk, vg, out, first_in, second_in, *targets):
    targets[8][...] = first_in[...]
    targets[9][...] = second_in[...]
    width = qk.shape[2] // 2
    eighth = unit.shape[3]
    for c in range(3):
        for p in range(8):
            targets[5 + c][:, p * eighth : (p + 1) * eighth] = unit[c, p].astype(F32)
    targets[0][...] = qk[0, :, :width].astype(F32)
    targets[1][...] = qk[0, :, width:].astype(F32)
    targets[2][...] = vg[0, :, :width].astype(F32)
    targets[3][...] = vg[0, :, width:].astype(F32)
    targets[4][...] = out[0].astype(F32)


def widen(unit, qk, vg, out, first, second):
    hid, eighth = unit.shape[2:]
    width, feat = qk.shape[2] // 2, 8 * eighth
    piece = lambda dims: pl.BlockSpec((1,) + dims, lambda i: (i, 0, 0))
    flat = lambda dims: pl.BlockSpec(dims, lambda i: (i, 0))
    whole = lambda rows, cols: jax.ShapeDtypeStruct((rows, cols), F32)
    slots, rows, _ = first.shape
    through = [pl.BlockSpec((slots, rows // 8, feat), lambda i: (0, i, 0))] * 2
    like = lambda x: jax.ShapeDtypeStruct(x.shape, x.dtype)
    return pl.pallas_call(
        widen_kernel,
        grid=(8,),
        in_specs=[
            pl.BlockSpec((3, 8, hid // 8, eighth), lambda i: (0, 0, i, 0)),
            piece(qk.shape[1:]),
            piece(vg.shape[1:]),
            piece(out.shape[1:]),
        ]
        + through,
        out_specs=[flat((eighth, width))] * 4
        + [flat((width // 8, feat))]
        + [flat((hid // 8, feat))] * 3
        + through,
        out_shape=[whole(feat, width)] * 4
        + [whole(width, feat)]
        + [whole(hid, feat)] * 3
        + [like(first), like(second)],
        compiler_params=pltpu.CompilerParams(vmem_limit_bytes=VMEM_LIMIT),
        name="widen",
    )(unit, qk, vg, out, first, second)


def on_device(
    batch,
    tokens,
    lengths,
    assignment,
    query_weight,
    key_weight,
    value_weight,
    gate_weight,
    out_weight,
    up_weight,
    pair_weight,
    down_weight,
    attention_norm_gain,
    mlp_gain,
    head_gain,
    cotangent,
):
    slots = tokens.shape[0]
    width = query_weight.shape[1]
    place = lax.axis_index("seq").astype(jnp.int32)
    seq_ids = lax.broadcasted_iota(jnp.int32, (slots, lengths.shape[0]), 1)
    slot_length = jnp.sum(jnp.where(assignment[:, None] == seq_ids, lengths[None, :], 0), axis=1)
    q4 = (query_weight, key_weight, value_weight, gate_weight)
    gain_one, gain_two, gain_head = attention_norm_gain[None], mlp_gain[None], head_gain[None]
    result, grad_inputs, unit_total, qk_total, vg_total, out_total, gains = block(
        batch, slot_length, tokens, cotangent, q4, out_weight, up_weight.T, pair_weight.T, down_weight,
        gain_one, gain_two, gain_head,
    )[:7]
    (
        grad_qw, grad_kw, grad_vw, grad_gw, grad_outw, grad_upw, grad_pairw, grad_down, result, grad_inputs,
    ) = widen(unit_total, qk_total, vg_total, out_total, result, grad_inputs)
    head_total = lax.dynamic_slice(gains[2], (place * width,), (width,))
    return (
        result,
        grad_inputs,
        grad_qw,
        grad_kw,
        grad_vw,
        grad_gw,
        grad_outw,
        grad_upw.T,
        grad_pairw.T,
        grad_down,
        gains[0],
        gains[1],
        head_total,
    )


def solution(mesh):
    return jax.shard_map(
        functools.partial(on_device, mesh.shape["batch"]),
        mesh=mesh,
        in_specs=(
            P("batch", "seq", None),
            P(),
            P("batch"),
            P(None, "seq"),
            P(None, "seq"),
            P(None, "seq"),
            P(None, "seq"),
            P("seq", None),
            P(None, "seq"),
            P(None, "seq"),
            P("seq", None),
            P(),
            P(),
            P("seq"),
            P("batch", "seq", None),
        ),
        out_specs=(
            P("batch", "seq", None),
            P("batch", "seq", None),
            P(None, "seq"),
            P(None, "seq"),
            P(None, "seq"),
            P(None, "seq"),
            P("seq", None),
            P(None, "seq"),
            P(None, "seq"),
            P("seq", None),
            P(),
            P(),
            P("seq"),
        ),
        check_vma=False,
    )
```

```python
import functools

import jax
import jax.numpy as jnp
from jax import lax
from jax.experimental import pallas as pl
from jax.experimental.pallas import tpu as pltpu
from jax.sharding import PartitionSpec as P

HD = 64
EPS = 1e-05
BF = jnp.bfloat16
F32 = jnp.float32
VMEM_LIMIT = 62 * 1024 * 1024
MESH = pl.DeviceIdType.MESH
BLOCKS = 4


def nn(a, b):
    return lax.dot_general(a, b, (((1,), (0,)), ((), ())), preferred_element_type=F32)


def nt(a, b):
    return lax.dot_general(a, b, (((1,), (1,)), ((), ())), preferred_element_type=F32)


def tn(a, b):
    return lax.dot_general(a, b, (((0,), (0,)), ((), ())), preferred_element_type=F32)


def same_head(width):
    rows = lax.broadcasted_iota(jnp.int32, (width, width), 0) // HD
    cols = lax.broadcasted_iota(jnp.int32, (width, width), 1) // HD
    return rows == cols


def by_head(array):
    rows, width = array.shape
    lane = lax.broadcasted_iota(jnp.int32, (rows, width), 1) // HD
    zero = jnp.zeros_like(array)
    return jnp.concatenate([jnp.where(lane == h, array, zero) for h in range(width // HD)], axis=0)


def causal(rows, heads, transposed):
    one = lax.broadcasted_iota(jnp.int32, (rows, rows), 0)
    two = lax.broadcasted_iota(jnp.int32, (rows, rows), 1)
    keep = (two >= one) if transposed else (one >= two)
    return jnp.concatenate([keep] * heads, axis=1)


def masked(scores, keep):
    return jnp.where(keep, scores, 0.0).astype(BF)


def head_mean(array, ones):
    return nn(array.astype(BF), ones) * (1.0 / HD)


def softplus(v):
    return jnp.maximum(v, 0.0) + jnp.log1p(jnp.exp(-jnp.abs(v)))


def sigmoid_of_softplus(q):
    series = q * (1.0 - q * (0.5 - q * (1.0 / 6.0)))
    return jnp.where(q < 0.03, series, 1.0 - jnp.exp(-q))


def sigmoid(v):
    return 1.0 / (1.0 + jnp.exp(-v))


class Peers:
    def __init__(self, batch=1):
        self.place = lax.axis_index("seq")
        self.group = lax.axis_index("batch")
        self.chip, self.core = self.place // 2, self.place % 2
        self.across = (self.group, (1 - self.chip) * 2 + self.core)
        self.beside = (self.group, self.chip * 2 + 1 - self.core)
        self.hops = batch.bit_length() - 1

    def bit(self, h):
        return (self.group // 2**h) % 2

    def partner(self, h):
        return (self.group + (1 - 2 * self.bit(h)) * 2**h, self.place)

    def meet(self):
        others = [self.across, self.beside] + [self.partner(h) for h in range(self.hops)]
        barrier = pltpu.get_barrier_semaphore()
        for peer in others:
            pl.semaphore_signal(barrier, inc=1, device_id=peer, device_id_type=MESH)
        pl.semaphore_wait(barrier, len(others))

    def relative(self, index):
        return ((index // 2 + self.chip) % 2) * 2 + (index % 2 + self.core) % 2


def spot(j):
    return (j % 2) * 2 + j // 2


def remote(source, target, sems, index, peer):
    send, recv = sems
    return pltpu.make_async_remote_copy(
        src_ref=source,
        dst_ref=target,
        send_sem=send.at[index],
        recv_sem=recv.at[index],
        device_id=peer,
        device_id_type=MESH,
    )


class Gather:
    def __init__(self, peers, buffer, sems, own=None):
        self.peers, self.buffer, self.sems = peers, buffer, sems
        self.own = own or (lambda k: buffer.at[k, 0])

    def chip_hop(self, k):
        return remote(self.own(k), self.buffer.at[k, 2], self.sems, 3 * k, self.peers.across)

    def core_hop(self, k):
        return remote(self.own(k), self.buffer.at[k, 1], self.sems, 3 * k + 1, self.peers.beside)

    def passed_on(self, k):
        return remote(
            self.buffer.at[k, 2], self.buffer.at[k, 3], self.sems, 3 * k + 2, self.peers.beside
        )

    def start(self, k):
        self.chip_hop(k).start()
        self.core_hop(k).start()

    def forward(self, k):
        self.chip_hop(k).wait_recv()
        self.passed_on(k).start()

    def arrived(self, k):
        self.core_hop(k).wait_recv()
        self.passed_on(k).wait_recv()

    def sent(self, k):
        self.chip_hop(k).wait_send()
        self.core_hop(k).wait_send()
        self.passed_on(k).wait_send()


class Scatter:
    def __init__(self, peers, pair, middle, came, far, sems):
        self.peers, self.pair, self.middle = peers, pair, middle
        self.came, self.far, self.sems = came, far, sems

    def core_hop(self, k):
        return remote(self.pair(k), self.came.at[k], self.sems, 2 * k, self.peers.beside)

    def chip_hop(self, k):
        return remote(self.middle(k), self.far.at[k], self.sems, 2 * k + 1, self.peers.across)

    def start(self, k):
        self.core_hop(k).start()

    def middle_step(self, k):
        self.core_hop(k).wait_recv()
        middle = self.middle(k)

        def add(rows):
            middle[rows] = (middle[rows].astype(F32) + self.came[k, 1, rows].astype(F32)).astype(BF)

        by_rows(middle.shape[0], add)
        self.chip_hop(k).start()

    def arrived(self, k):
        self.chip_hop(k).wait_recv()

    def sent(self, k):
        self.core_hop(k).wait_send()
        self.chip_hop(k).wait_send()


class Chain:
    def __init__(self, peers, bits, work, came, room, total, sems, load, keep, source=None, far=None, across=None):
        self.peers, self.sems, self.stages, self.waited = peers, sems, [], set()
        b0, b1, b2 = (peers.bit(h) for h in bits)
        pair = 2 if across == "last" else 1
        start = 0 if pair == 2 else b0 * 4
        kept = (start + b1 * 2 + b2) * pair
        self.kept = kept
        piece = b0 * 4 + b1 * 2 + b2

        def fetch(ref):
            copy = pltpu.make_async_copy(ref, room.at[pl.ds(0, ref.shape[0])], load)
            copy.start()
            copy.wait()

        def add(at, base, count):
            def finish():
                fetch(came.at[pl.ds(at, count)])

                def one(q):
                    work[base + q] = (work[base + q].astype(F32) + room[q].astype(F32)).astype(BF)

                loop(count, one)

            return finish

        def spread():
            fetch(far)

            def one(q):
                work[q] = (work[q].astype(F32) + room[q].astype(F32)).astype(BF)

            loop(8, one)

        def meet():
            fetch(far.at[pl.ds(0, 1)])
            work[kept] = (work[kept].astype(F32) + room[0].astype(F32)).astype(BF)

        def other(base, bit, count):
            return work.at[pl.ds((base + (1 - bit) * count) * pair, count * pair)]

        if across == "first":
            self.stages.append((source.at[pl.ds(8, 8)], far, peers.across, spread))
        first = source.at[pl.ds((1 - b0) * 8, 8)] if pair == 2 else other(0, b0, 4)
        at = 0
        for bit, base, count, h in (
            (b0, start, 4, bits[0]), (b1, start, 2, bits[1]), (b2, start + b1 * 2, 1, bits[2])
        ):
            here = base + (bit * count if count < 4 else 0)
            ref = first if count == 4 else other(base, bit, count)
            self.stages.append(
                (ref, came.at[pl.ds(at, count * pair)], peers.partner(h), add(at, here * pair, count * pair))
            )
            at += count * pair
        for h in range(peers.hops):
            if h not in bits:
                ref = work.at[pl.ds(kept, pair)]
                self.stages.append((ref, came.at[pl.ds(at, pair)], peers.partner(h), add(at, kept, pair)))
                self.waited.add(len(self.stages) - 1)
                at += pair
        if across == "last":
            self.stages.append((work.at[pl.ds(kept + 1, 1)], far.at[pl.ds(0, 1)], peers.across, meet))
        self.local = lambda: pltpu.make_async_copy(
            work.at[pl.ds(kept, 1)], total.at[pl.ds(piece, 1)], keep
        )
        for where, h in (
            (pl.ds(piece, 1), bits[2]),
            (pl.ds(b0 * 4 + b1 * 2, 2), bits[1]),
            (pl.ds(b0 * 4, 4), bits[0]),
        ):
            ref = work.at[pl.ds(kept, 1)] if h == bits[2] else total.at[where]
            self.stages.append((ref, total.at[where], peers.partner(h), lambda: None))
        self.count = len(self.stages)

    def hop(self, t):
        source, target, peer, _ = self.stages[t]
        return remote(source, target, self.sems, t, peer)

    def begin(self):
        self.hop(0).start()

    def step(self, t):
        self.hop(t).wait_recv()
        if t in self.waited:
            self.hop(t).wait_send()
        self.stages[t][3]()
        if t == self.count - 4:
            self.local().start()
        if t == self.count - 3:
            self.local().wait()
        if t + 1 < self.count:
            self.hop(t + 1).start()

    def sent(self):
        for t in range(self.count):
            if t not in self.waited:
                self.hop(t).wait_send()


def by_rows(rows, fn, step=64):
    def one(r, carry):
        fn(pl.ds(pl.multiple_of(r * step, step), step))
        return carry

    lax.fori_loop(0, rows // step, one, 0)


def loop(count, fn):
    def one(k, carry):
        fn(k)
        return carry

    lax.fori_loop(0, count, one, 0)


def normalize(values, gain):
    scale = lax.rsqrt(jnp.mean(values * values, axis=-1, keepdims=True) + EPS)
    normed = values * scale
    return normed, scale, (normed * gain).astype(BF)


def norm_back(grad_out, normed, scale, gain):
    grad_normed = grad_out * gain
    inner = jnp.mean(grad_normed * normed, axis=-1, keepdims=True)
    return scale * (grad_normed - normed * inner)


def block_kernel(
    batch,
    length_ref, tokens, cotangent, wq, wk, wv, wg, wo, up, pair, down, gain_one, gain_two, gain_head,
    result, grad_tokens, unit_total, qk_total, vg_total, out_total, gains,
    qkvg_hbm, mixed_hbm, gated_hbm, state_hbm, gm, other, sums, unit_came, unit_far, qk_came, vg_came,
    out_came,
    tok, w4, wo_v, h1, h2, g, part, came, far, middle, state, gain_came, head_part,
    load_sem, save_sem, slot_sem, mat_sem, chain_sem,
    h1_send, h1_recv, gm_send, gm_recv, h2_send, h2_recv, g_send, g_recv, w_send, w_recv,
    a_send, a_recv, b_send, b_recv, c_send, c_recv, gain_send, gain_recv,
    d_send, d_recv, u_send, u_recv, p_send, p_recv,
    d2_send, d2_recv, u2_send, u2_recv, p2_send, p2_recv, q_send, q_recv, v_send, v_recv, o_send, o_recv,
):
    slots, rows, feat = tok.shape
    width, hid = wo_v.shape[0], down.shape[0]
    heads, eighth = width // HD, feat // 8
    both = 2 * hid
    peers = Peers(batch)
    v = pltpu.VMEM

    def load(source, target, index):
        return pltpu.make_async_copy(source, target, load_sem.at[index])

    loads = [
        load(tokens, tok, 0),
        *(load(w, w4.at[m], 1 + m) for m, w in enumerate((wq, wk, wv, wg))),
        load(wo, wo_v, 5),
        load(cotangent, g.at[:, 0], 6),
    ]
    for one in loads:
        one.start()
    peers.meet()

    mats = (up, pair, down)
    b0, b1, b2 = (peers.bit(h) for h in range(3))

    def columns(first, count):
        return pl.ds(pl.multiple_of(first * eighth, eighth), count * eighth)

    def weight_hop(t, c):
        mine = other.at[c]
        cols = (
            columns(b0 * 4 + b1 * 2 + b2, 1), columns(b0 * 4 + b1 * 2 + b2, 1),
            columns(b0 * 4 + b1 * 2, 2), columns(b0 * 4, 4),
        )[t]
        source = (mats[c] if t == 0 else mine).at[:, cols]
        peer = peers.across if t == 0 else peers.partner(3 - t)
        return remote(source, mine.at[:, cols], (w_send, w_recv), 4 * c + t, peer)

    def weight_step(t, c):
        weight_hop(t - 1, c).wait_recv()
        if t < 4:
            weight_hop(t, c).start()

    for c in range(3):
        weight_hop(0, c).start()
    first = Gather(peers, h1, (h1_send, h1_recv))
    third = Gather(peers, gm, (gm_send, gm_recv), lambda k: tok.at[k])

    def pass_h2(k):
        return remote(h2.at[k, 0], h2.at[k, 1], (h2_send, h2_recv), k, peers.beside)

    def pass_g(k):
        return remote(cotangent.at[k], g.at[k, 1], (g_send, g_recv), k, peers.beside)

    buffers = (lambda k: part.at[k, pl.ds(2, 2)], lambda k: part.at[k, 1], came, far)
    scatter_a = Scatter(peers, *buffers, (a_send, a_recv))
    scatter_c = Scatter(peers, *buffers, (c_send, c_recv))

    def pass_grad(k):
        return remote(part.at[k, 1], came.at[k, 0], (b_send, b_recv), 2 * k, peers.beside)

    def pass_result(k):
        return remote(part.at[k, 3], came.at[k, 1], (b_send, b_recv), 2 * k + 1, peers.beside)

    g1, g2, gh = gain_one[...], gain_two[...], gain_head[...]
    gains[...] = jnp.zeros_like(gains)
    head_part[...] = jnp.zeros_like(head_part)
    loads[0].wait()

    def norm_first(k):
        def some(r):
            _, _, hidden = normalize(tok[k, r].astype(F32), g1)
            h1[k, 0, r] = hidden

        by_rows(rows, some)
        first.start(k)

    loop(slots, norm_first)
    loop(slots, lambda k: pass_g(k).start())
    for t, c in ((1, 0), (1, 1), (1, 2), (2, 0), (2, 1), (3, 0)):
        weight_step(t, c)
    for one in loads[1:6]:
        one.wait()

    same = same_head(width)
    ones = same.astype(BF)

    def attend_all(qkvg, mixed_s, gated_s, state_s):
        def saves(k):
            return [
                pltpu.make_async_copy(qkvg, qkvg_hbm.at[k], save_sem.at[0]),
                pltpu.make_async_copy(mixed_s, mixed_hbm.at[k], save_sem.at[1]),
                pltpu.make_async_copy(gated_s, gated_hbm.at[k], save_sem.at[2]),
                pltpu.make_async_copy(state_s, state_hbm.at[k], save_sem.at[3]),
            ]

        def attend(k):
            first.forward(k)

            @pl.when(k > 0)
            def _():
                scatter_a.middle_step(k - 1)
                for one in saves(k - 1):
                    one.wait()

            @pl.when(k == 1)
            def _():
                weight_step(2, 2)
                weight_step(3, 1)

            @pl.when(k == 2)
            def _():
                weight_step(3, 2)

            first.arrived(k)
            state[...] = jnp.zeros_like(state)
            length = length_ref[k]

            def chunk(i):
                j = peers.relative(i)
                hidden = h1[k, j]
                position = lax.broadcasted_iota(jnp.int32, (rows, width), 0) + i * rows
                query = softplus(nn(hidden, w4[0])).astype(BF)
                keys = jnp.where(position < length, softplus(nn(hidden, w4[1])), 0.0).astype(BF)
                values = nn(hidden, w4[2]).astype(BF)
                gate = nn(hidden, w4[3])
                qkvg[j, 0] = query
                qkvg[j, 1] = keys
                qkvg[j, 2] = values
                qkvg[j, 3] = gate.astype(BF)
                before = state[...].astype(BF)
                state_s[i] = before
                scores = masked(nt(query, by_head(keys)), causal(rows, heads, False))
                mixed = nn(query, before) + nn(scores, by_head(values))
                state[...] += jnp.where(same, tn(keys, values), 0.0)
                mixed_s[j] = mixed.astype(BF)
                scale = lax.rsqrt(head_mean(mixed * mixed, ones) + EPS)
                gated_s[j] = (mixed * scale * gh * (gate * sigmoid(gate))).astype(BF)

            loop(BLOCKS, chunk)
            for one in saves(k):
                one.start()

            def project(p):
                j = (p % 2) * 2 + p // 2
                part[k, p] = nn(gated_s[j], wo_v[...]).astype(BF)

            project(2)
            project(3)
            scatter_a.start(k)
            project(1)
            project(0)

        loop(slots, attend)
        for one in saves(slots - 1):
            one.wait()

    pl.run_scoped(
        attend_all,
        v((BLOCKS, 4, rows, width), BF),
        v((BLOCKS, rows, width), BF),
        v((BLOCKS, rows, width), BF),
        v((BLOCKS, width, width), BF),
    )
    scatter_a.middle_step(slots - 1)

    def finish_attend(k):
        scatter_a.arrived(k)

        def some(r):
            value = (
                tok[k, r].astype(F32)
                + part[k, 0, r].astype(F32)
                + came[k, 0, r].astype(F32)
                + far[k, r].astype(F32)
            )
            middle[k, r] = value
            _, _, hidden = normalize(value, g2)
            h2[k, 0, r] = hidden

        by_rows(rows, some)
        pass_h2(k).start()
        scatter_a.sent(k)

    finish_attend(0)
    finish_attend(1)
    loads[6].wait()

    def result_save(k):
        return pltpu.make_async_copy(part.at[k, 2], result.at[k], save_sem.at[4 + k])

    def unit_all(mat, prod_s, gu_s, gp_s, staged):
        def mat_load(c, which):
            source = mats[c] if which == 0 else other.at[c]
            return pltpu.make_async_copy(
                source, mat.at[c, pl.ds(which * hid, hid)], mat_sem.at[2 * c + which]
            )

        for c in range(3):
            mat_load(c, 0).start()
        for c in range(3):
            weight_step(4, c)
            mat_load(c, 1).start()
        for c in range(3):
            mat_load(c, 0).wait()
            mat_load(c, 1).wait()

        def unit(k):
            pass_h2(k).wait_recv()
            pass_g(k).wait_recv()

            def one(t):
                j = 1 - t
                hidden, grad = h2[k, j], g[k, j]
                up_part = nt(hidden, mat[0])
                pair_part = nt(hidden, mat[1])
                product = (up_part * pair_part).astype(BF)
                prod_s[k, j] = product
                part[k, 2 + j] = nn(product, mat[2]).astype(BF)
                grad_product = nt(grad, mat[2]).astype(BF).astype(F32)
                grad_up = (grad_product * pair_part).astype(BF)
                grad_pair = (grad_product * up_part).astype(BF)
                gu_s[k, j] = grad_up
                gp_s[k, j] = grad_pair
                part[k, j] = (nn(grad_up, mat[0]) + nn(grad_pair, mat[1])).astype(BF)

                @pl.when(t == 0)
                def _():
                    pass_grad(k).start()
                    pass_result(k).start()

            loop(2, one)

            @pl.when(k == 0)
            def _():
                for m in range(2, slots):
                    finish_attend(m)

            pass_grad(k).wait_recv()
            pass_result(k).wait_recv()

            def some(r):
                value = middle[k, r]
                total = value + part[k, 2, r].astype(F32) + came[k, 1, r].astype(F32)
                part[k, 2, r] = total.astype(BF)
                grad = part[k, 0, r].astype(F32) + came[k, 0, r].astype(F32)
                normed, scale, _ = normalize(value, g2)
                gains[1:2] += jnp.sum(grad * normed, axis=0, keepdims=True)
                back = g[k, 0, r].astype(F32) + norm_back(grad, normed, scale, g2)
                middle[k, r] = back
                tok[k, r] = back.astype(BF)

            by_rows(rows, some)
            third.start(k)
            pltpu.make_async_copy(tok.at[k], gm.at[k, 0], save_sem.at[4 + slots + k]).start()
            result_save(k).start()

        loop(slots, unit)
        tile = 256
        everything = slots * 2 * rows

        def weigh(c, left, right):
            for start in range(0, both, tile):
                span = min(tile, both - start)
                term = tn(
                    left[:, :, :, start : start + span].reshape(everything, span),
                    right[...].reshape(everything, feat),
                ).astype(BF)
                for q in range(2):
                    for m in range(2):
                        base = q * hid + m * (hid // 2)
                        low, high = max(start, base), min(start + span, base + hid // 2)
                        if low >= high:
                            continue
                        for p in range(8):
                            index = q * 8 + p if KINDS["UPD"[c] if m == 0 else "upd"[c]][0] == "first" else p * 2 + q
                            staged[index, low - q * hid : high - q * hid] = term[
                                low - start : high - start, p * eighth : (p + 1) * eighth
                            ]
            save = pltpu.make_async_copy(staged, sums.at[c], save_sem.at[3])
            save.start()
            save.wait()
            for m in range(2):
                begin_unit(c, m)

        turn = iter(range(slots))
        for c in UNIT_ORDER:
            weigh(c, (gu_s, gp_s, prod_s)[c], (h2, h2, g)[c])
            third.forward(next(turn))
        for k in turn:
            third.forward(k)

    half = pl.ds(0, hid // 2), pl.ds(hid // 2, hid // 2)
    unit_sems = (
        ((u_send, u_recv), (p_send, p_recv), (d_send, d_recv)),
        ((u2_send, u2_recv), (p2_send, p2_recv), (d2_send, d2_recv)),
    )

    def unit_chain(c, m, work, room):
        across, bits = KINDS[("UPD", "upd")[m][c]]
        return Chain(
            peers, bits, work, unit_came.at[c, :, half[m]], room, unit_total.at[c, :, half[m]],
            unit_sems[m][c], chain_sem.at[0], chain_sem.at[1 + 3 * m + c],
            sums.at[c, :, half[m]], unit_far.at[c, :, half[m]], across,
        )

    def begin_unit(c, m):
        unit_chain(c, m, h2.at[0], None).begin()

    pl.run_scoped(
        unit_all,
        v((3, both, feat), BF),
        v((slots, 2, rows, both), BF),
        v((slots, 2, rows, both), BF),
        v((slots, 2, rows, both), BF),
        v((16, hid, eighth), BF),
    )

    def rest(works, room, qk_work, vg_work, out_work, pair_room, small_room):
        chains = {}
        work_loads = []
        for m in range(2):
            for c in range(3):
                name = ("UPD", "upd")[m][c]
                work = works.at[c, :, half[m]]
                chains[name] = unit_chain(c, m, work, room)
                first_half = 0 if KINDS[name][0] == "first" else peers.bit(KINDS[name][1][0]) * 8
                work_loads.append(
                    pltpu.make_async_copy(
                        sums.at[c, pl.ds(first_half, 8), half[m]], work, mat_sem.at[3 * m + c]
                    )
                )
        for n, (name, work, come, space, total, pair_sems) in enumerate((
            ("Q", qk_work, qk_came, pair_room, qk_total, (q_send, q_recv)),
            ("V", vg_work, vg_came, pair_room, vg_total, (v_send, v_recv)),
            ("O", out_work, out_came, small_room, out_total, (o_send, o_recv)),
        )):
            chains[name] = Chain(
                peers, KINDS[name][1], work, come, space, total, pair_sems, chain_sem.at[0],
                chain_sem.at[7 + n],
            )
        for one in work_loads:
            one.start()
        for one in work_loads:
            one.wait()
        done = {name: 0 for name in chains}
        plan, tail, where = {}, [], (0, -1)
        for name, at in SCHEDULE:
            if name == "c":
                where = (at // 10, at % 10 + 1)
            elif name == "g":
                where = (at, 0)
            elif name == "T":
                where = None
            elif name in chains and where is None or name in ("F", "B", "A"):
                tail.append((name, at))
            elif name in chains:
                slot, point = where
                if point == 8 and slot + 1 < slots:
                    slot, point = slot + 1, -1
                plan.setdefault((slot, point), []).append((name, at))

        def play(actions):
            for name, stage in actions:
                chains[name].step(stage)
                done[name] = max(done[name], stage + 1)

        def attend_all_back(qkvg, mixed_v, state_v, gated, gm_v, pre, acc, out_acc):
            def slot_loads(k):
                b = k % 2
                pairs = (
                    (qkvg_hbm, qkvg), (mixed_hbm, mixed_v), (state_hbm, state_v), (gated_hbm, gated)
                )
                return [
                    pltpu.make_async_copy(source.at[k], target.at[b], slot_sem.at[4 * b + m])
                    for m, (source, target) in enumerate(pairs)
                ]

            for one in slot_loads(0):
                one.start()

            def hooks(k, point, low, high):
                for (slot, at), actions in plan.items():
                    if not low <= at < high:
                        continue

                    @pl.when((k == slot) & (point == at))
                    def _():
                        play(actions)

            def attend_back(k):
                b = k % 2
                hooks(k, -1, -1, 0)
                hooks(k, 0, 0, 1)
                third.arrived(k)
                pltpu.make_async_copy(tok.at[k], gm.at[k, 0], save_sem.at[4 + slots + k]).wait()
                fetch = pltpu.make_async_copy(gm.at[k], gm_v, slot_sem.at[8])
                fetch.start()

                @pl.when(k > 0)
                def _():
                    scatter_c.middle_step(k - 1)

                @pl.when(k + 1 < slots)
                def _():
                    for one in slot_loads(k + 1):
                        one.start()

                for one in slot_loads(k):
                    one.wait()
                result_save(k).wait()
                pass_grad(k).wait_send()
                pass_result(k).wait_send()
                state[...] = jnp.zeros_like(state)
                fetch.wait()

                def chunk(step):
                    hooks(k, step, 1, BLOCKS)
                    i = BLOCKS - 1 - step
                    j = peers.relative(i)
                    grad_gated = nt(gm_v[j], wo_v[...]).astype(BF).astype(F32)
                    query, keys, values = qkvg[b, j, 0], qkvg[b, j, 1], qkvg[b, j, 2]
                    gate = qkvg[b, j, 3].astype(F32)
                    mixed = mixed_v[b, j].astype(F32)
                    scale = lax.rsqrt(head_mean(mixed * mixed, ones) + EPS)
                    normed = mixed * scale
                    opened = sigmoid(gate)
                    grad_gate = grad_gated * (normed * gh) * opened * (1.0 + gate * (1.0 - opened))
                    grad_head = grad_gated * (gate * opened)
                    head_part[...] += jnp.sum(grad_head * normed, axis=0, keepdims=True)
                    scaled = grad_head * gh
                    inner = head_mean(scaled * normed, ones)
                    grad_mixed = (scale * (scaled - normed * inner)).astype(BF)
                    after = state[...].astype(BF)
                    before = state_v[b, i]
                    lower = causal(rows, heads, False)
                    upper = causal(rows, heads, True)
                    query_heads = by_head(query)
                    mixed_heads = by_head(grad_mixed)
                    grad_scores = masked(nt(grad_mixed, by_head(values)), lower)
                    grad_query = nt(grad_mixed, before) + nn(grad_scores, by_head(keys))
                    grad_scores_t = masked(nt(values, mixed_heads), upper)
                    grad_keys = nt(values, after) + nn(grad_scores_t, query_heads)
                    scores_t = masked(nt(keys, query_heads), upper)
                    grad_values = nn(keys, after) + nn(scores_t, mixed_heads)
                    state[...] += jnp.where(same, tn(query, grad_mixed), 0.0)

                    rounded = lambda x: x.astype(BF).astype(F32)
                    pre_q = (rounded(grad_query) * sigmoid_of_softplus(query.astype(F32))).astype(BF)
                    pre_k = (rounded(grad_keys) * sigmoid_of_softplus(keys.astype(F32))).astype(BF)
                    pre_v = grad_values.astype(BF)
                    pre_g = grad_gate.astype(BF)
                    for m, one in enumerate((pre_q, pre_k, pre_v, pre_g)):
                        pre[j, :, m * width : (m + 1) * width] = one
                    grad_h = (
                        nt(pre_q, w4[0]) + nt(pre_k, w4[1]) + nt(pre_v, w4[2]) + nt(pre_g, w4[3])
                    )
                    part[k, spot(j)] = grad_h.astype(BF)

                loop(BLOCKS, chunk)
                scatter_c.start(k)
                pre_all = pre[...].reshape(BLOCKS * rows, 4 * width)

                def weigh(m):
                    hooks(k, BLOCKS + m, BLOCKS, 8)
                    cols = pl.ds(pl.multiple_of(m * 256, 256), 256)
                    term = tn(h1[k, :, :, cols].reshape(BLOCKS * rows, 256), pre_all)
                    acc[cols] = jnp.where(k > 0, acc[cols], 0.0) + term

                loop(feat // 256, weigh)
                term = tn(gated[b].reshape(BLOCKS * rows, width), gm_v[...].reshape(BLOCKS * rows, feat))
                out_acc[...] = jnp.where(k > 0, out_acc[...], 0.0) + term

            loop(slots, attend_back)
            play(plan.get((slots - 1, 8), ()))
            scatter_c.middle_step(slots - 1)
            part_rows = width // 8

            def fill(p):
                at = pl.ds(pl.multiple_of(p * eighth, eighth), eighth)
                small = pl.ds(pl.multiple_of(p * part_rows, part_rows), part_rows)
                qk_work[p] = acc[at, : 2 * width].astype(BF)
                vg_work[p] = acc[at, 2 * width :].astype(BF)
                out_work[p] = out_acc[small].astype(BF)

            loop(8, fill)
            for name in ATTENTION_ORDER:
                chains[name].begin()

        pl.run_scoped(
            attend_all_back,
            v((2, BLOCKS, 4, rows, width), BF),
            v((2, BLOCKS, rows, width), BF),
            v((2, BLOCKS, width, width), BF),
            v((2, BLOCKS, rows, width), BF),
            v((BLOCKS, rows, feat), BF),
            v((BLOCKS, rows, 4 * width), BF),
            v((feat, 4 * width), F32),
            v((width, feat), F32),
        )
        loop(slots, lambda k: third.sent(k))
        again = load(tokens, tok, 0)
        again.start()

        def grad_save(k):
            return pltpu.make_async_copy(middle.at[k], grad_tokens.at[k], save_sem.at[4 + k])

        def finish(k):
            scatter_c.arrived(k)

            def some(r):
                grad = (
                    part[k, 0, r].astype(F32) + came[k, 0, r].astype(F32) + far[k, r].astype(F32)
                )
                normed, scale, _ = normalize(tok[k, r].astype(F32), g1)
                gains[0:1] += jnp.sum(grad * normed, axis=0, keepdims=True)
                middle[k, r] = middle[k, r] + norm_back(grad, normed, scale, g1)

            by_rows(rows, some)
            grad_save(k).start()

        others = [peers.beside, peers.across] + [peers.partner(h) for h in range(peers.hops)]

        def gain_hop(t):
            return remote(gains, gain_came.at[t], (gain_send, gain_recv), t, others[t])

        def gain_begin():
            lane = lax.broadcasted_iota(jnp.int32, (1, BLOCKS * width), 1) // width
            spread = jnp.concatenate([head_part[...]] * BLOCKS, axis=1)
            gains[2:3] = jnp.where(lane == peers.place, spread, 0.0)
            gain_hop(0).start()

        hop = iter(range(len(others)))

        def gain_step():
            t = next(hop, None)
            if t is None:
                return
            gain_hop(t).wait_recv()
            gain_hop(t).wait_send()
            gains[...] += gain_came[t]
            if t + 1 < len(others):
                gain_hop(t + 1).start()

        again.wait()
        turn = iter(range(slots))
        for name, stage in tail:
            if name == "F":
                finish(next(turn))
            elif name == "B":
                for k in turn:
                    finish(k)
                gain_begin()
            elif name == "A":
                gain_step()
            else:
                play([(name, stage)])
        for _ in others:
            gain_step()
        most = max(one.count for one in chains.values())
        for t in range(most):
            for name in chains:
                if done[name] <= t < chains[name].count:
                    play([(name, t)])
        for one in chains.values():
            one.sent()

        def settle(k):
            grad_save(k).wait()
            first.sent(k)
            scatter_c.sent(k)
            pass_h2(k).wait_send()
            pass_g(k).wait_send()

        loop(slots, settle)

        def settle_weights(c):
            for t in range(4):
                weight_hop(t, c).wait_send()

        for c in range(3):
            settle_weights(c)

    pl.run_scoped(
        rest,
        v((3, 8, hid, eighth), BF),
        v((8, hid // 2, eighth), BF),
        v((8, eighth, 2 * width), BF),
        v((8, eighth, 2 * width), BF),
        v((8, width // 8, feat), BF),
        v((4, eighth, 2 * width), BF),
        v((4, width // 8, feat), BF),
    )


def dma(n):
    return pltpu.SemaphoreType.DMA((n,))


def anywhere(n):
    return [pl.BlockSpec(memory_space=pl.ANY)] * n


def in_vmem(n):
    return [pl.BlockSpec(memory_space=pltpu.VMEM)] * n


KINDS = {
    "U": ("last", (0, 1, 2)),
    "P": ("first", (0, 1, 2)),
    "D": ("first", (0, 1, 2)),
    "u": ("last", (1, 0, 2)),
    "p": ("first", (0, 1, 2)),
    "d": ("last", (1, 0, 2)),
    "Q": (None, (1, 0, 2)),
    "V": (None, (0, 1, 2)),
    "O": (None, (0, 1, 2)),
}
UNIT_ORDER = (0, 1, 2)
ATTENTION_ORDER = ('O', 'Q', 'V')
SCHEDULE = (
    ("u", 0), ("U", 0), ("g", 0), ("P", 0), ("c", 0), ("c", 1), ("u", 1), ("c", 2), ("c", 3), ("P", 1),
    ("p", 0), ("U", 1), ("c", 4), ("u", 2), ("c", 5), ("c", 6), ("P", 2), ("c", 7), ("p", 1), ("g", 1),
    ("D", 0), ("u", 3), ("p", 2), ("c", 10), ("c", 11), ("u", 4), ("c", 12), ("D", 1), ("p", 3), ("c", 13),
    ("c", 14), ("D", 2), ("c", 15), ("p", 4), ("c", 16), ("c", 17), ("g", 2), ("P", 3), ("u", 5), ("p", 5),
    ("d", 0), ("D", 3), ("c", 20), ("P", 4), ("c", 21), ("c", 22), ("c", 23), ("D", 4), ("c", 24), ("c", 25),
    ("P", 5), ("d", 1), ("c", 26), ("c", 27), ("T", 0), ("U", 2), ("F", 0), ("d", 2), ("F", 1), ("O", 0),
    ("F", 2), ("B", 0), ("U", 3), ("Q", 0), ("O", 1), ("d", 3), ("V", 0), ("U", 4), ("D", 5), ("A", 0),
    ("O", 2), ("A", 0), ("Q", 1), ("A", 0), ("V", 1), ("A", 0), ("A", 0), ("U", 5), ("O", 3), ("Q", 2),
    ("d", 4), ("V", 2), ("O", 4), ("d", 5), ("Q", 3), ("V", 3), ("Q", 4), ("V", 4),
)


def block(batch, lengths, tokens, cotangent, q4, wo, up, pair, down, gain_one, gain_two, gain_head):
    slots, rows, feat = tokens.shape
    width, hid = wo.shape[0], down.shape[0]
    eighth = feat // 8
    n = BLOCKS
    hops = batch.bit_length() - 1
    extra = hops - 3
    shape = jax.ShapeDtypeStruct
    blocks = lambda *dims: shape((slots, n) + dims, BF)
    outs = [
        shape((slots, rows, feat), BF),
        shape((slots, rows, feat), F32),
        shape((3, 8, hid, eighth), BF),
        shape((8, eighth, 2 * width), BF),
        shape((8, eighth, 2 * width), BF),
        shape((8, width // 8, feat), BF),
        shape((3, feat), F32),
        blocks(4, rows, width),
        blocks(rows, width),
        blocks(rows, width),
        blocks(width, width),
        blocks(rows, feat),
        shape((3, hid, feat), BF),
        shape((3, 16, hid, eighth), BF),
        shape((3, 14 + 2 * extra, hid, eighth), BF),
        shape((3, 8, hid, eighth), BF),
        shape((7 + extra, eighth, 2 * width), BF),
        shape((7 + extra, eighth, 2 * width), BF),
        shape((7 + extra, width // 8, feat), BF),
    ]
    v = pltpu.VMEM
    scratch = [
        v((slots, rows, feat), BF),
        v((4, feat, width), BF),
        v((width, feat), BF),
        v((slots, n, rows, feat), BF),
        v((slots, 2, rows, feat), BF),
        v((slots, 2, rows, feat), BF),
        v((slots, n, rows, feat), BF),
        v((slots, 2, rows, feat), BF),
        v((slots, rows, feat), BF),
        v((slots, rows, feat), F32),
        v((width, width), F32),
        v((hops + 2, 3, feat), F32),
        v((1, width), F32),
        dma(7),
        dma(4 + 2 * slots),
        dma(9),
        dma(6),
        dma(10),
        *[dma(3 * slots)] * 4,
        *[dma(slots)] * 4,
        *[dma(12)] * 2,
        *[dma(2 * slots)] * 6,
        *[dma(hops + 2)] * 2,
        *[dma(7 + extra)] * 18,
    ]
    total = slots * n * rows
    return pl.pallas_call(
        functools.partial(block_kernel, batch),
        in_specs=[pl.BlockSpec(memory_space=pltpu.SMEM)] + anywhere(10) + in_vmem(3),
        out_specs=anywhere(6) + in_vmem(1) + anywhere(12),
        out_shape=outs,
        scratch_shapes=scratch,
        compiler_params=pltpu.CompilerParams(
            collective_id=1, has_side_effects=True, vmem_limit_bytes=VMEM_LIMIT
        ),
        cost_estimate=pl.CostEstimate(
            flops=total * (30 * feat * width + 56 * width * width + 18 * feat * hid),
            transcendentals=total * 12 * width,
            bytes_accessed=2 * total * (12 * feat + 3 * hid),
        ),
        name="block",
    )(lengths, tokens, cotangent, *q4, wo, up, pair, down, gain_one, gain_two, gain_head)


def widen_kernel(unit, qk, vg, out, first_in, second_in, *targets):
    targets[8][...] = first_in[...]
    targets[9][...] = second_in[...]
    width = qk.shape[2] // 2
    eighth = unit.shape[3]
    for c in range(3):
        for p in range(8):
            targets[5 + c][:, p * eighth : (p + 1) * eighth] = unit[c, p].astype(F32)
    targets[0][...] = qk[0, :, :width].astype(F32)
    targets[1][...] = qk[0, :, width:].astype(F32)
    targets[2][...] = vg[0, :, :width].astype(F32)
    targets[3][...] = vg[0, :, width:].astype(F32)
    targets[4][...] = out[0].astype(F32)


def widen(unit, qk, vg, out, first, second):
    hid, eighth = unit.shape[2:]
    width, feat = qk.shape[2] // 2, 8 * eighth
    piece = lambda dims: pl.BlockSpec((1,) + dims, lambda i: (i, 0, 0))
    flat = lambda dims: pl.BlockSpec(dims, lambda i: (i, 0))
    whole = lambda rows, cols: jax.ShapeDtypeStruct((rows, cols), F32)
    slots, rows, _ = first.shape
    through = [pl.BlockSpec((slots, rows // 8, feat), lambda i: (0, i, 0))] * 2
    like = lambda x: jax.ShapeDtypeStruct(x.shape, x.dtype)
    return pl.pallas_call(
        widen_kernel,
        grid=(8,),
        in_specs=[
            pl.BlockSpec((3, 8, hid // 8, eighth), lambda i: (0, 0, i, 0)),
            piece(qk.shape[1:]),
            piece(vg.shape[1:]),
            piece(out.shape[1:]),
        ]
        + through,
        out_specs=[flat((eighth, width))] * 4
        + [flat((width // 8, feat))]
        + [flat((hid // 8, feat))] * 3
        + through,
        out_shape=[whole(feat, width)] * 4
        + [whole(width, feat)]
        + [whole(hid, feat)] * 3
        + [like(first), like(second)],
        compiler_params=pltpu.CompilerParams(vmem_limit_bytes=VMEM_LIMIT),
        name="widen",
    )(unit, qk, vg, out, first, second)


def on_device(
    batch,
    tokens,
    lengths,
    assignment,
    query_weight,
    key_weight,
    value_weight,
    gate_weight,
    out_weight,
    up_weight,
    pair_weight,
    down_weight,
    attention_norm_gain,
    mlp_gain,
    head_gain,
    cotangent,
):
    slots = tokens.shape[0]
    width = query_weight.shape[1]
    place = lax.axis_index("seq").astype(jnp.int32)
    seq_ids = lax.broadcasted_iota(jnp.int32, (slots, lengths.shape[0]), 1)
    slot_length = jnp.sum(jnp.where(assignment[:, None] == seq_ids, lengths[None, :], 0), axis=1)
    q4 = (query_weight, key_weight, value_weight, gate_weight)
    gain_one, gain_two, gain_head = attention_norm_gain[None], mlp_gain[None], head_gain[None]
    result, grad_inputs, unit_total, qk_total, vg_total, out_total, gains = block(
        batch, slot_length, tokens, cotangent, q4, out_weight, up_weight.T, pair_weight.T, down_weight,
        gain_one, gain_two, gain_head,
    )[:7]
    (
        grad_qw, grad_kw, grad_vw, grad_gw, grad_outw, grad_upw, grad_pairw, grad_down, result, grad_inputs,
    ) = widen(unit_total, qk_total, vg_total, out_total, result, grad_inputs)
    head_total = lax.dynamic_slice(gains[2], (place * width,), (width,))
    return (
        result,
        grad_inputs,
        grad_qw,
        grad_kw,
        grad_vw,
        grad_gw,
        grad_outw,
        grad_upw.T,
        grad_pairw.T,
        grad_down,
        gains[0],
        gains[1],
        head_total,
    )


def solution(mesh):
    return jax.shard_map(
        functools.partial(on_device, mesh.shape["batch"]),
        mesh=mesh,
        in_specs=(
            P("batch", "seq", None),
            P(),
            P("batch"),
            P(None, "seq"),
            P(None, "seq"),
            P(None, "seq"),
            P(None, "seq"),
            P("seq", None),
            P(None, "seq"),
            P(None, "seq"),
            P("seq", None),
            P(),
            P(),
            P("seq"),
            P("batch", "seq", None),
        ),
        out_specs=(
            P("batch", "seq", None),
            P("batch", "seq", None),
            P(None, "seq"),
            P(None, "seq"),
            P(None, "seq"),
            P(None, "seq"),
            P("seq", None),
            P(None, "seq"),
            P(None, "seq"),
            P("seq", None),
            P(),
            P(),
            P("seq"),
        ),
        check_vma=False,
    )
```
